32 devices in a mesh: gx: 4 (over x, core), gy: 4 (over z), gz: 2 (over y).
Axes of the slice: x: 2, y: 2, z: 4, core: 2. Of those that a mesh axis runs over, the one named last changes fastest.
Arguments:
- right_side: float32 [64, 32, 256], P('gx', 'gy', 'gz'), may hold values from -6 to 6
- inv_density: float32 [64, 32, 256], P('gx', 'gy', 'gz'), may hold values from 0.25 to 4
Outputs:
- pressure: float32 [64, 32, 256], P('gx', 'gy', 'gz')
- residual: float32 [64, 32, 256], P('gx', 'gy', 'gz')
The draws below stay inside these ranges and needn't reach their ends.
All inputs are finite; a program needn't handle non-finite values.
Results may differ from the reference program's by a relative error of at most 0.0003.
Values sent between devices are 32-bit elements; how exact they have to be, the bound alone decides.
A program may use at most 64 MiB of HBM per device.

```python
import math
import jax
import jax.numpy as jnp

LEVELS = 3
DEGREE = 2
COARSE_DEGREE = 6
NX = 64
NY = 32
NZ = 256


def draw_right_side(key, part):
    second = jax.random.fold_in(key, 1)
    values = jax.random.normal(second, (NX, NY, NZ), jnp.float32)
    return jnp.clip(values, -6.0, 6.0).astype(jnp.float32)


def block_scale(stream_key, extent, cuts, smallest, top_value):
    gain = 1.0
    for dim, parts in cuts:
        draws = jax.random.uniform(jax.random.fold_in(jax.random.fold_in(stream_key, 6), dim), (parts,), jnp.float32, smallest / len(cuts), top_value / len(cuts))
        gain = gain * jnp.repeat(jnp.exp(draws), extent[dim] // parts).reshape((-1,) + (1,) * (len(extent) - 1 - dim))
    return gain


def setup_inputs(seed: int = 0) -> dict:
    splits = jax.random.split(jax.random.key(seed), 3)
    return {
        "right_side": draw_right_side(jax.random.fold_in(splits[2], 71), 0),
        "inv_density": jnp.clip(jnp.exp(math.log(4.0) - 2.7725887 * jax.random.uniform(splits[1], (NX, NY, NZ), jnp.float32) ** block_scale(splits[1], (NX, NY, NZ), ((0, 4), (1, 4), (2, 2)), -0.2, 0.2)), 0.25, 4.0),
    }


def mean_cells(field):
    n, m, k = field.shape
    return field.reshape(n // 2, 2, m // 2, 2, k // 2, 2).sum(axis=(1, 3, 5)) * 0.125


def copy_cells(field):
    return jnp.repeat(jnp.repeat(jnp.repeat(field, 2, 0), 2, 1), 2, 2)


def harmonic(first, second):
    inside = first * second > 0.0
    return jnp.where(inside, 2.0 * first * second / (first + second), first + second)


def face_coefs(padded):
    face_x = harmonic(padded[:-1, 1:-1, 1:-1], padded[1:, 1:-1, 1:-1])
    face_y = harmonic(padded[1:-1, :-1, 1:-1], padded[1:-1, 1:, 1:-1])
    face_z = harmonic(padded[1:-1, 1:-1, :-1], padded[1:-1, 1:-1, 1:])
    return face_x, face_y, face_z


def operate(padded, faces, scale):
    face_x, face_y, face_z = faces
    center = padded[1:-1, 1:-1, 1:-1]
    total = face_x[1:] * (center - padded[2:, 1:-1, 1:-1])
    total = total + face_x[:-1] * (center - padded[:-2, 1:-1, 1:-1])
    total = total + face_y[:, 1:] * (center - padded[1:-1, 2:, 1:-1])
    total = total + face_y[:, :-1] * (center - padded[1:-1, :-2, 1:-1])
    total = total + face_z[:, :, 1:] * (center - padded[1:-1, 1:-1, 2:])
    total = total + face_z[:, :, :-1] * (center - padded[1:-1, 1:-1, :-2])
    return scale * total


def inverse_diag(faces, scale):
    face_x, face_y, face_z = faces
    total = face_x[1:] + face_x[:-1] + face_y[:, 1:] + face_y[:, :-1] + face_z[:, :, 1:] + face_z[:, :, :-1]
    return 1.0 / (scale * total)


def chebyshev(start, source, steps, lower, upper, apply_op, inv_diag):
    theta = (upper + lower) / 2.0
    delta = (upper - lower) / 2.0
    sigma = theta / delta
    rho_now = 1.0 / sigma
    if start is None:
        remain = source
        solution = jnp.zeros_like(source)
    else:
        remain = source - apply_op(start)
        solution = start
    update = remain * inv_diag / theta
    solution = solution + update
    for index in range(steps - 1):
        rho_next = 1.0 / (2.0 * sigma - rho_now)
        remain = source - apply_op(solution)
        update = rho_next * rho_now * update + (2.0 * rho_next / delta) * (remain * inv_diag)
        solution = solution + update
        rho_now = rho_next
    return solution


def vcycle(depth, source, coef):
    scale = 0.25 ** depth
    faces = face_coefs(jnp.pad(coef, 1))
    inv_diag = inverse_diag(faces, scale)

    def apply_op(field):
        return operate(jnp.pad(field, 1), faces, scale)

    if depth == LEVELS:
        return chebyshev(None, source, COARSE_DEGREE, 0.05, 2.0, apply_op, inv_diag), apply_op
    solution = chebyshev(None, source, DEGREE, 0.3, 2.0, apply_op, inv_diag)
    remain = source - apply_op(solution)
    correction, unused = vcycle(depth + 1, mean_cells(remain), mean_cells(coef))
    solution = solution + copy_cells(correction)
    solution = chebyshev(solution, source, DEGREE, 0.3, 2.0, apply_op, inv_diag)
    return solution, apply_op


def reference(right_side, inv_density):
    pressure, apply_op = vcycle(0, right_side, inv_density)
    return pressure, right_side - apply_op(pressure)
```

```python
import functools

import jax
import jax.numpy as jnp
from jax import lax
from jax.experimental import pallas as pl
from jax.experimental.pallas import tpu as pltpu
from jax.sharding import PartitionSpec as P

COARSE_DEGREE = 6
AXES = ("gx", "gy", "gz")
LANES = 128
TILE = 8
MESH = pl.DeviceIdType.MESH
F32 = jnp.float32


def div(a, n):
    if n & (n - 1) == 0:
        return lax.shift_right_logical(a, jnp.int32(n.bit_length() - 1))
    return a // n


def mod(a, n):
    if n & (n - 1) == 0:
        return a & jnp.int32(n - 1)
    return a % n


def iota(shape, dim):
    return lax.broadcasted_iota(jnp.int32, shape, dim)


def parts(v):
    high = v.astype(jnp.bfloat16)
    rest = v - high.astype(F32)
    middle = rest.astype(jnp.bfloat16)
    return high, middle, (rest - middle.astype(F32)).astype(jnp.bfloat16)


def pick_rows(left, v):
    n = v.shape[1]
    out = lax.dot(left, jnp.concatenate(parts(v), 1), preferred_element_type=F32)
    return out[:, :n] + (out[:, n:2 * n] + out[:, 2 * n:])


def pick_lanes(v, right):
    n = v.shape[0]
    if n % 16:
        high, middle, low = (lax.dot(part, right, preferred_element_type=F32) for part in parts(v))
        return high + (middle + low)
    out = lax.dot(jnp.concatenate(parts(v), 0), right, preferred_element_type=F32)
    return out[:n] + (out[n:2 * n] + out[2 * n:])


def chosen(hit, value=1.0):
    return jnp.where(hit, value, 0.0).astype(jnp.bfloat16)


def up8(n):
    return -(-n // TILE) * TILE


def upl(n):
    return -(-n // LANES) * LANES


def restrict(v, dims, width_out, offset):
    x, y, z = dims
    rows, cols = (x // 2) * (y // 2), x * y
    r, s = iota((rows, cols), 0), iota((rows, cols), 1)
    hit = (div(div(s, y), 2) == div(r, y // 2)) & (div(mod(s, y), 2) == mod(r, y // 2))
    left = chosen(hit, 0.125)
    if v.shape[1] == width_out == LANES:
        w = pick_rows(left, v)
        w = w + pltpu.roll(w, LANES - 1, 1)
        l = iota(w.shape, 1) - offset
        w = jnp.take_along_axis(w, jnp.clip(2 * l, 0, LANES - 1), axis=1)
        return jnp.where((l >= 0) & (l < z // 2), w, 0.0)
    k, l = iota((v.shape[1], width_out), 0), iota((v.shape[1], width_out), 1)
    right = chosen((l == div(k, 2) + offset) & (k < z))
    return pick_lanes(pick_rows(left, v), right)


def prolong(e, dims, width_out, coarse_y, x0, y0, z0):
    x, y, z = dims
    rows, cols = x * y, e.shape[0]
    r, s = iota((rows, cols), 0), iota((rows, cols), 1)
    want = (div(div(r, y), 2) + x0) * coarse_y + div(mod(r, y), 2) + y0
    left = chosen(s == want)
    k, l = iota((e.shape[1], width_out), 0), iota((e.shape[1], width_out), 1)
    right = chosen((k == div(l, 2) + z0) & (l < z))
    return pick_lanes(pick_rows(left, e), right)


def prolong_near(dims, rows_in, width_in, coarse_y, x0, y0, z0):
    x, y, z = dims
    shape = (x * y, rows_in)
    i, j, s = div(iota(shape, 0), y), mod(iota(shape, 0), y), iota(shape, 1)
    lefts = []
    for sx, sy in ((0, 0), (-1, 0), (1, 0), (0, -1), (0, 1)):
        want = (div(i + (sx + 2), 2) + (x0 - 1)) * coarse_y + div(j + (sy + 2), 2) + (y0 - 1)
        lefts.append(chosen(s == want))
    k, l = iota((width_in, LANES), 0), iota((width_in, LANES), 1)
    rights = [
        chosen((k == div(l + (sz + 2), 2) + (z0 - 1)) & (l < z)) for sz in (0, -1, 1)
    ]
    return jnp.concatenate(lefts, 0), rights


def harmonic(a, b):
    return 2.0 * a * b / (a + b)


def make_coefs(c, around, edges, scale):
    links, total = [], None
    for near, edge in zip(around, edges):
        face = harmonic(c, jnp.where(edge, c, near))
        total = face if total is None else total + face
        links.append(jnp.where(edge, 0.0, face) * scale)
    total = total * scale
    return links, total, 1.0 / total


def apply_op(v, around, coefs):
    links, total, unused = coefs
    out = total * v
    for near, link in zip(around, links):
        out = out - link * near
    return out


def chebyshev(start, source, steps, lower, upper, inv, op_of):
    theta = (upper + lower) / 2.0
    delta = (upper - lower) / 2.0
    sigma = theta / delta
    rho_now = 1.0 / sigma
    if start is None:
        update = source * inv * (1.0 / theta)
        field = update
    else:
        remain = source - op_of(start)
        update = remain * inv * (1.0 / theta)
        field = start + update
    for index in range(steps - 1):
        rho_next = 1.0 / (2.0 * sigma - rho_now)
        remain = source - op_of(field)
        update = rho_next * rho_now * update + (2.0 * rho_next / delta) * (remain * inv)
        field = field + update
        rho_now = rho_next
    return field


def kernel(sizes, dims0, b_hbm, c_hbm, p_ref, q_ref, *scratch):
    (b_ref, c_ref, isem, v0, ys0, zs0, xr0, yr0, zr0, ey0, v1, ys1, zs1, xr1, yr1, zr1, ey1, tile, slots,
     send0, recv0, send1, recv1, gsend, grecv) = scratch
    loads = [pltpu.make_async_copy(src, dst, isem.at[n]) for n, (src, dst) in enumerate(((b_hbm, b_ref), (c_hbm, c_ref)))]
    for load in loads:
        load.start()
    pos = tuple(lax.axis_index(a) for a in AXES)
    dims1 = tuple(d // 2 for d in dims0)
    dims2 = tuple(d // 2 for d in dims1)
    whole2 = tuple(d * n for d, n in zip(dims2, sizes))
    whole3 = tuple(d // 2 for d in whole2)
    nx, ny, nz = sizes
    count = nx * ny * nz
    me = (pos[0] * ny + pos[1]) * nz + pos[2]
    width2, width3 = upl(whole2[2]), upl(whole3[2])

    def coords(index):
        return (index // (ny * nz), (index // nz) % ny, index % nz)

    barrier = pltpu.get_barrier_semaphore()

    def greet(step, unused):
        pl.semaphore_signal(barrier, inc=1, device_id=coords((me + step) % count), device_id_type=MESH)
        return unused

    for ref in (xr0, yr0, zr0, xr1, yr1, zr1, ey0, ey1):
        ref[...] = jnp.zeros_like(ref)
    lax.fori_loop(1, count, greet, 0)

    def exists(axis, side):
        return pos[axis] > 0 if side == 0 else pos[axis] < sizes[axis] - 1

    def peer(axis, side):
        return tuple(p + ((-1, 1)[side] if a == axis else 0) for a, p in enumerate(pos))

    def copies(level, slot):
        x, y, z = (dims0, dims1)[level]
        rows = x * y
        v, ys, zs, xr, yr, zr, send, recv = (
            (v0, ys0, zs0, xr0, yr0, zr0, send0, recv0),
            (v1, ys1, zs1, xr1, yr1, zr1, send1, recv1),
        )[level]
        edge = up8(y)
        for axis in range(3):
            for side in range(2):
                if axis == 0:
                    start = 0 if side == 0 else rows - edge
                    src, dst = v.at[slot, pl.ds(start, edge)], xr.at[slot, 1 - side]
                elif axis == 1:
                    src, dst = ys.at[slot, side], yr.at[slot, 1 - side]
                else:
                    src, dst = zs.at[slot, side], zr.at[slot, 1 - side]
                yield axis, side, pltpu.make_async_remote_copy(
                    src_ref=src, dst_ref=dst,
                    send_sem=send.at[slot, 2 * axis + side],
                    recv_sem=recv.at[slot, 2 * axis + 1 - side],
                    device_id=peer(axis, side), device_id_type=MESH,
                )

    def launch(level, slot, wanted):
        for axis, side, copy in copies(level, slot):
            if axis in wanted:
                @pl.when(exists(axis, side))
                def _():
                    copy.start()

    def post(level, slot, value, now=True):
        x, y, z = (dims0, dims1)[level]
        rows = x * y
        v, ys, zs = ((v0, ys0, zs0), (v1, ys1, zs1))[level]
        v[slot] = value
        if now:
            launch(level, slot, (0,))
        for side in range(2):
            ys[slot, side] = v[slot, pl.ds(0 if side == 0 else y - 1, x, stride=y), :]
        if now:
            launch(level, slot, (1,))
        lane = iota((TILE, LANES), 1)
        for side in range(2):
            packed = jnp.zeros((TILE, LANES), F32)
            for t in range(rows // TILE):
                part = value[t * TILE:(t + 1) * TILE]
                shift = (t if side == 0 else t - (z - 1)) % LANES
                if shift:
                    part = pltpu.roll(part, shift, 1)
                packed = jnp.where(lane == t, part, packed)
            zs[slot, side] = packed
        if now:
            launch(level, slot, (2,))

    def drain(level, slot):
        for axis, side, copy in copies(level, slot):
            @pl.when(exists(axis, side))
            def _():
                copy.wait_send()

    def arrive(level, slot):
        xr, yr, zr, recv = ((xr0, yr0, zr0, recv0), (xr1, yr1, zr1, recv1))[level]
        for axis in range(3):
            for side in range(2):
                dst = (xr, yr, zr)[axis].at[slot, side]
                @pl.when(exists(axis, side))
                def _():
                    pltpu.make_async_copy(dst, dst, recv.at[slot, 2 * axis + side]).wait()

    def unpack(part, place, rows):
        out = []
        for t in range(rows // TILE):
            shift = (place - t) % LANES
            out.append(pltpu.roll(part, shift, 1) if shift else part)
        return jnp.concatenate(out, 0)

    def collect(level, slot, value):
        arrive(level, slot)
        x, y, z = (dims0, dims1)[level]
        rows = x * y
        xr, yr, zr, ey = ((xr0, yr0, zr0, ey0), (xr1, yr1, zr1, ey1))[level]
        edge = up8(y)
        below = jnp.concatenate([xr[slot, 0], value], 0)[edge - y:edge - y + rows]
        above = jnp.concatenate([value, xr[slot, 1]], 0)[y:y + rows]
        ey[slot, 0, pl.ds(0, x, stride=y), :] = yr[slot, 0]
        ey[slot, 1, pl.ds(y - 1, x, stride=y), :] = yr[slot, 1]
        row = mod(iota((rows, LANES), 0), y)
        lane = iota((rows, LANES), 1)
        left = jnp.where(row == 0, ey[slot, 0], pltpu.roll(value, 1, 0))
        right = jnp.where(row == y - 1, ey[slot, 1], pltpu.roll(value, rows - 1, 0))

        front = jnp.where(lane == 0, unpack(zr[slot, 0], 0, rows), pltpu.roll(value, 1, 1))
        back = jnp.where(lane == z - 1, unpack(zr[slot, 1], z - 1, rows), pltpu.roll(value, LANES - 1, 1))
        return (below, above, left, right, front, back)

    def local_edges(dims):
        x, y, z = dims
        rows = x * y
        plane, row, lane = div(iota((rows, LANES), 0), y), mod(iota((rows, LANES), 0), y), iota((rows, LANES), 1)
        return tuple(
            index + pos[axis] * dims[axis] == (0 if side == 0 else dims[axis] * sizes[axis] - 1)
            for axis, index in enumerate((plane, row, lane)) for side in range(2)
        )

    def whole_edges(dims, shape):
        x, y, z = dims
        plane, row, lane = div(iota(shape, 0), y), mod(iota(shape, 0), y), iota(shape, 1)
        return (plane == 0, plane == x - 1, row == 0, row == y - 1, lane == 0, lane >= z - 1)

    def whole_near(dims):
        x, y, z = dims
        rows = x * y

        def near(v):
            return (
                pltpu.roll(v, y, 0), pltpu.roll(v, rows - y, 0),
                pltpu.roll(v, 1, 0), pltpu.roll(v, rows - 1, 0),
                pltpu.roll(v, 1, 1), pltpu.roll(v, v.shape[1] - 1, 1),
            )
        return near

    def gather_copy(kind, step):
        target = coords((me + step) % count)
        return pltpu.make_async_remote_copy(
            src_ref=tile.at[kind], dst_ref=slots.at[kind, me],
            send_sem=gsend.at[kind], recv_sem=grecv.at[kind],
            device_id=target, device_id_type=MESH,
        )

    def gather_start(kind, value):
        tile[kind] = value

        def go(step, unused):
            gather_copy(kind, step).start()
            return unused
        lax.fori_loop(1, count, go, 0)

    def gather_finish(kind):
        part = slots.at[kind, pl.ds(0, count - 1)]
        pltpu.make_async_copy(part, part, grecv.at[kind]).wait()
        slots[kind, me] = tile[kind]
        per = LANES // dims2[2]
        block = dims2[0] * dims2[1]
        columns = []
        for lane_tile in range(width2 // LANES):
            rows = []
            for gx in range(nx):
                for gy in range(ny):
                    total = None
                    for gz in range(lane_tile * per, min((lane_tile + 1) * per, nz)):
                        part = slots[kind, (gx * ny + gy) * nz + gz]
                        total = part if total is None else total + part
                    rows.append(total)
            columns.append(jnp.concatenate(rows, 0))
        stacked = columns[0] if len(columns) == 1 else jnp.concatenate(columns, 1)
        n = whole2[0] * whole2[1]
        r, s = iota((n, n), 0), iota((n, n), 1)
        X, Y = div(r, whole2[1]), mod(r, whole2[1])
        want = (div(X, dims2[0]) * ny + div(Y, dims2[1])) * block + mod(X, dims2[0]) * dims2[1] + mod(Y, dims2[1])
        return pick_rows(chosen(s == want), stacked)

    offset = (pos[2] % (LANES // dims2[2])) * dims2[2]

    def fill(c, dims):
        return jnp.where(iota(c.shape, 1) < dims[2], c, 1.0)

    for load in loads:
        load.wait()
    c0 = c_ref[...].reshape(dims0[0] * dims0[1], LANES)
    b0 = b_ref[...].reshape(dims0[0] * dims0[1], LANES)
    c1 = restrict(c0, dims0, LANES, 0)
    c2_own = restrict(c1, dims1, LANES, offset)
    c1 = fill(c1, dims1)
    post(0, 0, c0, False)
    post(1, 0, c1, False)
    pl.semaphore_wait(barrier, count - 1)

    launch(0, 0, (0, 1, 2))
    launch(1, 0, (0, 1, 2))
    gather_start(0, c2_own)

    lane0, row0, plane0 = (iota((dims0[0] * dims0[1], LANES), 1), mod(iota((dims0[0] * dims0[1], LANES), 0), dims0[1]),
                           div(iota((dims0[0] * dims0[1], LANES), 0), dims0[1]))
    sides0 = (plane0 == 0, plane0 == dims0[0] - 1, row0 == 0, row0 == dims0[1] - 1, lane0 == 0, lane0 == dims0[2] - 1)
    near0 = whole_near(dims0)
    near2, near3 = whole_near(whole2), whole_near(whole3)
    rows0, edge0 = dims0[0] * dims0[1], dims0[1]
    shape2 = (whole2[0] * whole2[1], width2)
    store = {}

    links0, total0, inv0 = make_coefs(c0, collect(0, 0, c0), local_edges(dims0), 1.0)
    inner0 = [jnp.where(side, 0.0, link) for side, link in zip(sides0, links0)]
    outer0 = [jnp.where(side, link, 0.0) for side, link in zip(sides0, links0)]

    def op0(slot, filler=None):
        def op(v):
            post(0, slot, v)
            out = apply_op(v, near0(v), (inner0, total0, None))
            if filler is not None:
                filler()
            arrive(0, slot)
            ey0[slot, 0, pl.ds(0, dims0[0], stride=edge0), :] = yr0[slot, 0]
            ey0[slot, 1, pl.ds(edge0 - 1, dims0[0], stride=edge0), :] = yr0[slot, 1]
            out = out - outer0[2] * ey0[slot, 0] - outer0[3] * ey0[slot, 1]
            out = out - outer0[4] * unpack(zr0[slot, 0], 0, rows0)
            out = out - outer0[5] * unpack(zr0[slot, 1], dims0[2] - 1, rows0)
            return jnp.concatenate([
                out[:edge0] - outer0[0][:edge0] * xr0[slot, 0],
                out[edge0:rows0 - edge0],
                out[rows0 - edge0:] - outer0[1][rows0 - edge0:] * xr0[slot, 1],
            ], 0)
        return op

    def ops(*steps):
        queue = list(steps)
        return lambda v: queue.pop(0)(v)

    def op1(slot, filler=None):
        def op(v):
            post(1, slot, v)
            if filler is not None:
                filler()
            store["near1"] = collect(1, slot, v)
            return apply_op(v, store["near1"], store["coefs1"])
        return op

    def fill_coefs1():
        store["coefs1"] = make_coefs(c1, collect(1, 0, c1), local_edges(dims1), 0.25)

    def fill_gather():
        store["c2"] = gather_finish(0)

    def fill_coefs2():
        c2 = store["c2"]
        store["c3"] = fill(restrict(c2, whole2, width3, 0), whole3)
        c2 = fill(c2, whole2)
        store["coefs2"] = make_coefs(c2, near2(c2), whole_edges(whole2, shape2), 0.25 ** 2)

    def fill_coefs3():
        c3 = store["c3"]
        store["coefs3"] = make_coefs(c3, near3(c3), whole_edges(whole3, c3.shape), 0.25 ** 3)
        store["prolong"] = prolong_near(
            dims1, shape2[0], width2, whole2[1], pos[0] * dims2[0], pos[1] * dims2[1], pos[2] * dims2[2])

    x0 = chebyshev(None, b0, 2, 0.3, 2.0, inv0, op0(1, fill_coefs1))
    r0 = b0 - op0(2, fill_gather)(x0)
    b1 = restrict(r0, dims0, LANES, 0)

    coefs1 = store["coefs1"]
    x1 = chebyshev(None, b1, 2, 0.3, 2.0, coefs1[2], op1(1, fill_coefs2))
    r1 = b1 - op1(2, fill_coefs3)(x1)
    gather_start(1, restrict(r1, dims1, LANES, offset))
    coefs2, coefs3, left5, rights = store["coefs2"], store["coefs3"], *store["prolong"]

    def op2(v):
        return apply_op(v, near2(v), coefs2)

    def op3(v):
        return apply_op(v, near3(v), coefs3)

    b2 = gather_finish(1)
    x2 = chebyshev(None, b2, 2, 0.3, 2.0, coefs2[2], op2)
    r2 = b2 - op2(x2)
    b3 = restrict(r2, whole2, width3, 0)
    x3 = chebyshev(None, b3, COARSE_DEGREE, 0.05, 2.0, coefs3[2], op3)
    x2 = x2 + prolong(x3, whole2, width2, whole3[1], 0, 0, 0)
    x2 = chebyshev(x2, b2, 2, 0.3, 2.0, coefs2[2], op2)

    rows1 = dims1[0] * dims1[1]
    picked = pick_rows(left5, x2)
    spread = pick_lanes(picked, rights[0])
    near_e = [spread[n * rows1:(n + 1) * rows1] for n in range(1, 5)] + [pick_lanes(picked[:rows1], m) for m in rights[1:]]
    near_x = store["near1"]

    def op1_known(v):
        return apply_op(v, [a + b for a, b in zip(near_x, near_e)], coefs1)

    x1 = x1 + spread[:rows1]
    x1 = chebyshev(x1, b1, 2, 0.3, 2.0, coefs1[2], ops(op1_known, op1(3)))
    x0 = x0 + prolong(x1, dims0, LANES, dims1[1], 0, 0, 0)
    x0 = chebyshev(x0, b0, 2, 0.3, 2.0, inv0, ops(op0(3), op0(4)))
    p_ref[...] = x0.reshape(p_ref.shape)
    res = b0 - op0(5)(x0)
    q_ref[...] = res.reshape(q_ref.shape)

    for slot in range(6):
        drain(0, slot)
    for slot in range(4):
        drain(1, slot)
    for kind in range(2):
        part = slots.at[kind, pl.ds(0, count - 1)]
        pltpu.make_async_copy(part, part, gsend.at[kind]).wait()


def finish(p_ref, q_ref, p_out, q_out):
    p_out[...] = p_ref[...]
    q_out[...] = q_ref[...]


def solution(mesh):
    sizes = tuple(mesh.shape[a] for a in AXES)
    count = sizes[0] * sizes[1] * sizes[2]

    def per_device(b, c):
        dims0 = b.shape
        scratch = [pltpu.VMEM(dims0, F32), pltpu.VMEM(dims0, F32), pltpu.SemaphoreType.DMA((2,))]
        for slots, (x, y, z) in ((6, dims0), (4, tuple(d // 2 for d in dims0))):
            scratch += [
                pltpu.VMEM((slots, x * y, LANES), F32),
                pltpu.VMEM((slots, 2, x, LANES), F32),
                pltpu.VMEM((slots, 2, TILE, LANES), F32),
                pltpu.VMEM((slots, 2, up8(y), LANES), F32),
                pltpu.VMEM((slots, 2, x, LANES), F32),
                pltpu.VMEM((slots, 2, TILE, LANES), F32),
                pltpu.VMEM((slots, 2, x * y, LANES), F32),
            ]
        scratch += [
            pltpu.VMEM((2, TILE, LANES), F32),
            pltpu.VMEM((2, count, TILE, LANES), F32),
            pltpu.SemaphoreType.DMA((6, 6)), pltpu.SemaphoreType.DMA((6, 6)),
            pltpu.SemaphoreType.DMA((4, 6)), pltpu.SemaphoreType.DMA((4, 6)),
            pltpu.SemaphoreType.DMA((2,)), pltpu.SemaphoreType.DMA((2,)),
        ]
        shape = jax.ShapeDtypeStruct(dims0, F32)
        p, q = pl.pallas_call(
            functools.partial(kernel, sizes, dims0),
            out_shape=(shape, shape),
            in_specs=[pl.BlockSpec(memory_space=pltpu.HBM)] * 2,
            out_specs=(pl.BlockSpec(memory_space=pltpu.VMEM),) * 2,
            scratch_shapes=scratch,
            compiler_params=pltpu.CompilerParams(collective_id=0, has_side_effects=True,
                                                 vmem_limit_bytes=min(48, 8 * max(1, count // 32)) << 20),
        )(b, c)
        return pl.pallas_call(
            finish,
            out_shape=(shape, shape),
            in_specs=[pl.BlockSpec(memory_space=pltpu.VMEM)] * 2,
            out_specs=(pl.BlockSpec(memory_space=pltpu.VMEM),) * 2,
            compiler_params=pltpu.CompilerParams(vmem_limit_bytes=2 << 20),
        )(p, q)

    spec = P(*AXES)
    return jax.shard_map(per_device, mesh=mesh, in_specs=(spec, spec), out_specs=(spec, spec), check_vma=False)
```

```python
import functools
import itertools

import jax
import jax.numpy as jnp
from jax import lax
from jax.experimental import pallas as pl
from jax.experimental.pallas import tpu as pltpu
from jax.sharding import PartitionSpec as P

COARSE_DEGREE = 6
AXES = ("gx", "gy", "gz")
LANES = 128
TILE = 8
H0 = 3
H1 = 4
MESH = pl.DeviceIdType.MESH
F32 = jnp.float32
FACES = ((0, 1), (0, -1), (1, 0), (-1, 0), (1, 1), (1, -1), (-1, 1), (-1, -1))
DIRS = tuple((dx, dy, 0) for dx, dy in FACES) + tuple(
    (dx, dy, dz) for dz in (1, -1) for dx, dy in ((0, 0),) + FACES
)
CB, C1, B1, X0, X1 = range(5)


def iota(shape, dim):
    return lax.broadcasted_iota(jnp.int32, shape, dim)


def harmonic(a, b):
    return 2.0 * a * b / (a + b)


def factors(lower, upper):
    theta = (upper + lower) / 2.0
    delta = (upper - lower) / 2.0
    sigma = theta / delta
    rho = 1.0 / sigma
    rho_next = 1.0 / (2.0 * sigma - rho)
    return 1.0 / theta, rho_next * rho, 2.0 * rho_next / delta


def chebyshev(start, source, steps, lower, upper, inv, op_of):
    theta = (upper + lower) / 2.0
    delta = (upper - lower) / 2.0
    sigma = theta / delta
    rho_now = 1.0 / sigma
    if start is None:
        update = source * inv * (1.0 / theta)
        field = update
    else:
        remain = source - op_of(start)
        update = remain * inv * (1.0 / theta)
        field = start + update
    for index in range(steps - 1):
        rho_next = 1.0 / (2.0 * sigma - rho_now)
        remain = source - op_of(field)
        update = rho_next * rho_now * update + (2.0 * rho_next / delta) * (remain * inv)
        field = field + update
        rho_now = rho_next
    return field


def make_coefs(c, around, edges, scale):
    links, total = [], None
    for near, edge in zip(around, edges):
        face = harmonic(c, jnp.where(edge, c, near))
        total = face if total is None else total + face
        links.append(jnp.where(edge, 0.0, face) * scale)
    total = total * scale
    return links, total, 1.0 / total


def apply_op(v, around, coefs):
    links, total, unused = coefs
    out = total * v
    for near, link in zip(around, links):
        out = out - link * near
    return out


class Level:
    def __init__(self, refs, dims, halo, width, pos, sizes, scale):
        self.lx, self.ly, self.lz, self.diag, self.inv, self.tmp, self.aux = refs
        self.dims, self.halo, self.width, self.scale = dims, halo, width, scale
        shape = (2 * TILE, width)
        row, lane = iota(shape, 0), iota(shape, 1)

        def inner(axis):
            low = jnp.where(pos[axis] > 0, 1.0, 0.0).astype(F32)
            high = jnp.where(pos[axis] < sizes[axis] - 1, 1.0, 0.0).astype(F32)
            return low, high

        self.xlow, self.xhigh = inner(0)
        self.ymask = self.zmask = None
        outer = None
        masks = []
        for index, axis in ((row, 1), (lane, 2)):
            low, high = inner(axis)
            last = dims[axis] - 1
            end = shape[axis - 1] - 1
            masks.append(jnp.where(index == end, low, jnp.where(index == last, high, 1.0)))
            part = jnp.where(index == 0, 1.0 - low, jnp.where(index == last, 1.0 - high, 0.0))
            outer = part if outer is None else outer + part
        self.ymask, self.zmask = masks
        self.outer = outer

    def planes(self, reach):
        return range(self.halo - reach, self.halo + self.dims[0] + reach)

    def back(self, v, dim):
        n = v.shape[dim]
        return pltpu.roll(v, n - 1, dim)

    def coefs(self, c_of):
        first, last = self.halo, self.halo + self.dims[0] - 1
        reach = self.halo - 1
        for p in range(first - reach - 1, last + reach + 1):
            face = harmonic(c_of(p), c_of(p + 1)) * self.scale
            if p == first - 1:
                face = face * self.xlow
            if p == last:
                face = face * self.xhigh
            self.lx[p] = face
        ymask, zmask, outer = self.ymask * self.scale, self.zmask * self.scale, self.outer * self.scale
        for p in self.planes(reach):
            c = c_of(p)
            ly = harmonic(c, self.back(c, 0)) * ymask
            lz = harmonic(c, self.back(c, 1)) * zmask
            total = (self.lx[p] + self.lx[p - 1]) + (ly + pltpu.roll(ly, 1, 0)) + (lz + pltpu.roll(lz, 1, 1))
            around = outer
            if p == first:
                around = around + (1.0 - self.xlow) * self.scale
            if p == last:
                around = around + (1.0 - self.xhigh) * self.scale
            total = total + c * around
            self.ly[p], self.lz[p], self.diag[p] = ly, lz, total
            self.inv[p] = 1.0 / total

    def op(self, v, p):
        here = v[p]
        ly, lz = self.ly[p], self.lz[p]
        x = self.lx[p] * v[p + 1] + self.lx[p - 1] * v[p - 1]
        y = ly * self.back(here, 0) + pltpu.roll(ly * here, 1, 0)
        z = lz * self.back(here, 1) + pltpu.roll(lz * here, 1, 1)
        return self.diag[p] * here - x - (y + z)

    def own_op(self, v, p):
        own = (slice(0, TILE), slice(0, LANES))
        here = v[p, :, 0:LANES]
        wide = v[p, 0:TILE, :]
        ly, lz = self.ly[p, :, 0:LANES], self.lz[p, 0:TILE, :]
        x = self.lx[p, 0:TILE, 0:LANES] * v[p + 1, 0:TILE, 0:LANES] + self.lx[p - 1, 0:TILE, 0:LANES] * v[p - 1, 0:TILE, 0:LANES]
        y = ly * self.back(here, 0) + pltpu.roll(ly * here, 1, 0)
        z = lz * self.back(wide, 1) + pltpu.roll(lz * wide, 1, 1)
        return self.diag[p, 0:TILE, 0:LANES] * here[own] - x - (y[own] + z[own])

    def before(self, b_of):
        first, mix, gain = factors(0.3, 2.0)
        for p in self.planes(2):
            self.tmp[p] = b_of(p) * self.inv[p] * first
        for p in self.planes(1):
            d = self.tmp[p]
            self.aux[p] = d + (mix * d + gain * ((b_of(p) - self.op(self.tmp, p)) * self.inv[p]))

    def after(self, start, b_of, out, reach):
        first, mix, gain = factors(0.3, 2.0)
        for p in self.planes(reach + 1):
            update = (b_of(p) - self.op(start, p)) * self.inv[p] * first
            self.aux[p] = update
            self.tmp[p] = start[p] + update
        for p in self.planes(reach):
            update = mix * self.aux[p] + gain * ((b_of(p) - self.op(self.tmp, p)) * self.inv[p])
            out[p] = self.tmp[p] + update


def restrict(tiles, lanes, rows):
    out = []
    lane = (2 * iota((TILE, LANES), 1)) % lanes
    row = (2 * iota((TILE, LANES), 0)) % rows
    for a, b in zip(tiles[0::2], tiles[1::2]):
        s = a + b
        s = s + pltpu.roll(s, LANES - 1, 1)
        s = (s + pltpu.roll(s, TILE - 1, 0)) * 0.125
        s = jnp.take_along_axis(s, lane, axis=1)
        out.append(jnp.take_along_axis(s, row, axis=0))
    return out


def kernel(sizes, dims0, b_hbm, c_hbm, p_ref, q_ref, *scratch):
    (e0, x0, zcb, zx0, scb, sx0, c1, b1, x1, z1, s1, c1m, b1m, x1s, slots, tile, pad, x2s) = scratch[:18]
    refs0, refs1 = scratch[18:25], scratch[25:32]
    isem, ssem, rsem, gsend, grecv = scratch[32:]
    pos = tuple(lax.axis_index(a) for a in AXES)
    dims1 = tuple(d // 2 for d in dims0)
    dims2 = tuple(d // 2 for d in dims1)
    whole2 = tuple(d * n for d, n in zip(dims2, sizes))
    nx, ny, nz = sizes
    count = nx * ny * nz
    me = (pos[0] * ny + pos[1]) * nz + pos[2]
    width2 = x2s.shape[1]
    own0 = pl.ds(H0, dims0[0])

    loads = [
        pltpu.make_async_copy(src, e0.at[k, own0, pl.ds(0, TILE), pl.ds(0, LANES)], isem.at[k])
        for k, src in enumerate((c_hbm, b_hbm))
    ]
    for load in loads:
        load.start()

    def coords(index):
        return (index // (ny * nz), (index // nz) % ny, index % nz)

    barrier = pltpu.get_barrier_semaphore()

    def greet(step, unused):
        pl.semaphore_signal(barrier, inc=1, device_id=coords((me + step) % count), device_id_type=MESH)
        return unused

    for k, value in ((0, 1.0), (1, 0.0)):
        for p in range(e0.shape[1]):
            if not H0 <= p < H0 + dims0[0]:
                e0[k, p, 0:TILE, 0:LANES] = jnp.full((TILE, LANES), value, F32)
            e0[k, p, TILE:2 * TILE, 0:LANES] = jnp.full((TILE, LANES), value, F32)
        for side, i, j in itertools.product(range(2), range(3), range(3)):
            zcb[side, i, j, k] = jnp.full((TILE, LANES), value, F32)
    x0[:, :, 0:LANES] = jnp.zeros((x0.shape[0], 2 * TILE, LANES), F32)
    zx0[...] = jnp.zeros_like(zx0)
    c1[...] = jnp.ones_like(c1)
    b1[...] = jnp.zeros_like(b1)
    x1[...] = jnp.zeros_like(x1)
    z1[0] = jnp.ones(z1.shape[1:], F32)
    z1[1:3] = jnp.zeros((2,) + z1.shape[1:], F32)
    lax.fori_loop(1, count, greet, 0)

    def exists(axis, step):
        if step == 0:
            return None
        return pos[axis] < sizes[axis] - 1 if step > 0 else pos[axis] > 0

    def when(conditions, body):
        conditions = [c for c in conditions if c is not None]
        if not conditions:
            body()
            return
        both = conditions[0]
        for c in conditions[1:]:
            both = both & c
        pl.when(both)(body)

    def each(sign, body):
        for dz in (0, 1, -1):
            def group():
                for n, d in enumerate(DIRS):
                    if d[2] == dz:
                        when([exists(0, sign * d[0]), exists(1, sign * d[1])], functools.partial(body, n))
            when([exists(2, sign * dz)], group)

    def cut(step, n, halo, wrap):
        if step == 0:
            return (0, 0, n)
        if step > 0:
            return (n - halo, wrap - halo, halo)
        return (0, n, halo)

    def ends(xid, n):
        dx, dy, dz = DIRS[n]
        if dz:
            packed = {CB: scb, X0: sx0}.get(xid)
            arrived = {CB: zcb, X0: zx0}.get(xid)
            if packed is None:
                at = (C1, B1, X1).index(xid)
                packed, arrived = s1.at[at], z1.at[at]
            return packed, arrived.at[0 if dz > 0 else 1, 1 - dx, 1 - dy]
        low, halo = (xid in (CB, X0)), (H0 if xid in (CB, X0) else H1)
        dims = dims0 if low else dims1
        a, b, planes = cut(dx, dims[0], halo, 0)
        r, s, rows = cut(dy, dims[1], min(halo, dims[1]), 2 * TILE)
        if low:
            ref = e0 if xid == CB else x0
            lead = (slice(None),) if xid == CB else ()
            lanes = (pl.ds(0, LANES),)
        else:
            ref, lead, lanes = {C1: c1, B1: b1, X1: x1}[xid], (), (slice(None),)
        src = ref.at[lead + (pl.ds(halo + a, planes), pl.ds(r, rows)) + lanes]
        dst = ref.at[lead + (pl.ds(halo + b, planes), pl.ds(s, rows)) + lanes]
        return src, dst

    def remote(xid, n):
        src, dst = ends(xid, n)
        return pltpu.make_async_remote_copy(
            src_ref=src, dst_ref=dst, send_sem=ssem.at[xid, n], recv_sem=rsem.at[xid, n],
            device_id=tuple(p + d for p, d in zip(pos, DIRS[n])), device_id_type=MESH,
        )

    def launch(xid):
        each(1, lambda n: remote(xid, n).start())

    def arrive(xid):
        def body(n):
            dst = ends(xid, n)[1]
            pltpu.make_async_copy(dst, dst, rsem.at[xid, n]).wait()
        each(-1, body)

    def drain(xid):
        def body(n):
            src = ends(xid, n)[0]
            pltpu.make_async_copy(src, src, ssem.at[xid, n]).wait()
        each(1, body)

    lane, sub = iota((TILE, LANES), 1), iota((TILE, LANES), 0)

    def pack0(tiles):
        out = tiles[0]
        for t in range(1, len(tiles)):
            part = pltpu.roll(tiles[t], 8 * t, 1)
            out = jnp.where(((lane - (8 * t - 4)) % LANES) < 8, part, out)
        return out

    def pack1(tiles):
        out = tiles[0]
        for t in range(1, len(tiles)):
            part = pltpu.roll(tiles[t], 8 * t, 1)
            place = (lane - 8 * t) % LANES
            out = jnp.where((place < 4) | ((place >= 60) & (place < 64)), part, out)
        return out

    def both_sides(arrived, dx, dy, k=None):
        at = (dx + 1, dy + 1) + (() if k is None else (k,))
        return jnp.where(lane % 8 < 4, arrived[(1,) + at], arrived[(0,) + at])

    def group_planes(n, halo):
        return ((0, [(t, halo + t) for t in range(n)]),
                (-1, [(t, halo + t - n) for t in range(n - halo, n)]),
                (1, [(t, halo + n + t) for t in range(halo)]))

    def unpack0(arrived, k, store):
        for dx, pairs in group_planes(dims0[0], H0):
            first = both_sides(arrived, dx, 0, k)
            second = jnp.where(sub < 4, both_sides(arrived, dx, 1, k), both_sides(arrived, dx, -1, k))
            for t, p in pairs:
                shift = (-8 * t) % LANES
                store(p, 0, pltpu.roll(first, shift, 1) if shift else first)
                store(p, 1, pltpu.roll(second, shift, 1) if shift else second)

    def unpack1(arrived, field, store):
        z = dims1[2]
        for dx, pairs in group_planes(dims1[0], H1):
            first = jnp.where(sub < 4, both_sides(arrived, dx, 0), both_sides(arrived, dx, 1))
            second = both_sides(arrived, dx, -1)
            for t, p in pairs:
                shift = (z - 8 * t) % LANES
                for half, part in enumerate((first, second)):
                    rows = slice(half * TILE, (half + 1) * TILE)
                    part = pltpu.roll(part, shift, 1) if shift else part
                    store(p, rows, jnp.where(lane < z, field[p, rows, :], part))

    def post1(field, packed, tiles):
        for i, v in enumerate(tiles):
            field[H1 + i, 0:dims1[1], :] = v[0:dims1[1]]
        packed[...] = pack1(tiles)

    def message(tiles):
        out = tiles[0]
        for i in range(1, dims2[0]):
            out = jnp.where(lane // dims2[2] == i, tiles[i], out)
        return out

    def slot(kind, x, y, z):
        return slots.at[kind, x, z, pl.ds(dims2[1] * y, dims2[1])]

    def gather_start(kind, value):
        tile[kind] = value
        src = tile.at[kind, pl.ds(0, dims2[1])]

        def go(step, unused):
            pltpu.make_async_remote_copy(
                src_ref=src, dst_ref=slot(kind, *pos), send_sem=gsend.at[kind], recv_sem=grecv.at[kind],
                device_id=coords((me + step) % count), device_id_type=MESH,
            ).start()
            return unused
        lax.fori_loop(1, count, go, 0)
        pltpu.make_async_copy(src, slot(kind, *pos), grecv.at[kind]).start()

    def gather_finish(kind, outside):
        pltpu.make_async_copy(slots.at[kind], slots.at[kind], grecv.at[kind]).wait()
        z = dims2[2]
        per = LANES // z
        spot = iota((whole2[1], LANES), 1)
        planes = []
        for x in range(nx):
            for i in range(dims2[0]):
                columns = []
                for first in range(0, width2 // z, per):
                    total = None
                    for g in range(min(per, nz - first)):
                        shift = (z * (g - i)) % LANES
                        part = slots[kind, x, first + g]
                        part = pltpu.roll(part, shift, 1) if shift else part
                        total = part if total is None else jnp.where(spot // z == g, part, total)
                    columns.append(total)
                planes.append(columns[0] if len(columns) == 1 else jnp.concatenate(columns, 1))
        v = jnp.concatenate(planes, 0)
        if whole2[2] < width2:
            v = jnp.where(iota(v.shape, 1) < whole2[2], v, outside)
        return v

    for load in loads:
        load.wait()
    for k in range(2):
        scb[k] = pack0([e0[k, H0 + t, 0:TILE, 0:LANES] for t in range(dims0[0])])
    pl.semaphore_wait(barrier, count - 1)

    launch(CB)
    tiles = restrict([e0[0, H0 + t, 0:TILE, 0:LANES] for t in range(dims0[0])], dims0[2], dims0[1])
    post1(c1, s1.at[0], tiles)
    launch(C1)
    gather_start(0, message(restrict(tiles, dims1[2], dims1[1])))

    level0 = Level(refs0, dims0, H0, 2 * LANES, pos, sizes, 1.0)
    level1 = Level(refs1, dims1, H1, LANES, pos, sizes, 0.25)

    arrive(CB)
    for k in range(2):
        def put(p, half, value):
            e0[k, p, half * TILE:(half + 1) * TILE, LANES:2 * LANES] = value
        unpack0(zcb, k, put)
    level0.coefs(lambda p: e0[0, p])
    b0 = lambda p: e0[1, p]
    level0.before(b0)
    r0 = [e0[1, p, 0:TILE, 0:LANES] - level0.own_op(level0.aux, p) for p in level0.planes(0)]
    tiles = restrict(r0, dims0[2], dims0[1])
    post1(b1, s1.at[1], tiles)
    launch(B1)

    tiles = [level0.aux[p, 0:TILE, 0:LANES] for p in level0.planes(0)]
    for p, v in zip(level0.planes(0), tiles):
        x0[p, 0:TILE, 0:LANES] = v
    sx0[...] = pack0(tiles)
    launch(X0)
    arrive(C1)

    def put_c1(p, rows, value):
        c1m[p, rows, :] = value
    unpack1(z1.at[0], c1, put_c1)
    level1.coefs(lambda p: c1m[p])

    arrive(B1)

    def put_b1(p, rows, value):
        b1m[p, rows, :] = value
    unpack1(z1.at[1], b1, put_b1)
    b1_of = lambda p: b1m[p]
    level1.before(b1_of)
    r1 = [b1m[p, 0:TILE, :] - level1.own_op(level1.aux, p) for p in level1.planes(0)]
    gather_start(1, message(restrict(r1, dims1[2], dims1[1])))
    tiles = [level1.aux[p, 0:TILE, :] for p in level1.planes(0)]
    tiles = [jnp.where(lane < dims1[2], v, pltpu.roll(v, dims1[2], 1)) for v in tiles]
    tiles = [jnp.where(sub < dims1[1], v, pltpu.roll(v, dims1[1], 0)) for v in tiles]
    post1(x1, s1.at[2], tiles)
    launch(X1)

    y2, z2 = whole2[1], whole2[2]
    shape2 = (whole2[0] * y2, width2)
    shape3 = (shape2[0] // 2, width2)

    def near2(v):
        n = v.shape[0]
        return (pltpu.roll(v, y2, 0), pltpu.roll(v, n - y2, 0), pltpu.roll(v, 1, 0), pltpu.roll(v, n - 1, 0),
                pltpu.roll(v, 1, 1), pltpu.roll(v, width2 - 1, 1))

    def near3(v):
        n = v.shape[0]
        return (pltpu.roll(v, y2, 0), pltpu.roll(v, n - y2, 0), pltpu.roll(v, 2, 0), pltpu.roll(v, n - 2, 0),
                pltpu.roll(v, 2, 1), pltpu.roll(v, width2 - 2, 1))

    def edges(shape, step):
        plane, row, spot = iota(shape, 0) // y2, iota(shape, 0) % y2, iota(shape, 1)
        return (plane == 0, plane == shape[0] // y2 - 1, row == 0, row == y2 - step, spot == 0, spot >= z2 - step)

    def pairs(v):
        return [v[n * y2:(n + 1) * y2] for n in range(v.shape[0] // y2)]

    def restrict2(v):
        planes = pairs(v)
        s = jnp.concatenate([a + b for a, b in zip(planes[0::2], planes[1::2])], 0)
        s = s + pltpu.roll(s, width2 - 1, 1)
        return (s + pltpu.roll(s, s.shape[0] - 1, 0)) * 0.125

    def prolong3(v):
        v = jnp.where((iota(shape3, 0) % 2 == 0) & (iota(shape3, 1) % 2 == 0), v, 0.0)
        v = v + pltpu.roll(v, 1, 1)
        v = v + pltpu.roll(v, 1, 0)
        return jnp.concatenate([part for part in pairs(v) for unused in range(2)], 0)

    c2 = gather_finish(0, 1.0)
    coefs2 = make_coefs(c2, near2(c2), edges(shape2, 1), 0.25 ** 2)
    c3 = restrict2(c2)
    coefs3 = make_coefs(c3, near3(c3), edges(shape3, 2), 0.25 ** 3)

    def op2(v):
        return apply_op(v, near2(v), coefs2)

    def op3(v):
        return apply_op(v, near3(v), coefs3)

    arrive(X0)

    def put_x0(p, half, value):
        x0[p, half * TILE:(half + 1) * TILE, LANES:2 * LANES] = value
    unpack0(zx0, None, put_x0)
    arrive(X1)

    def put_x1(p, rows, value):
        x1s[p, rows, :] = value
    unpack1(z1.at[2], x1, put_x1)
    for xid in (CB, C1, B1, X0, X1):
        drain(xid)

    b2 = gather_finish(1, 0.0)
    x2 = chebyshev(None, b2, 2, 0.3, 2.0, coefs2[2], op2)
    b3 = restrict2(b2 - op2(x2))
    x3 = chebyshev(None, b3, COARSE_DEGREE, 0.05, 2.0, coefs3[2], op3)
    x2 = chebyshev(x2 + prolong3(x3), b2, 2, 0.3, 2.0, coefs2[2], op2)
    x2s[...] = x2

    up_lane = jnp.where(lane < 96, lane // 2, LANES // 2 + lane // 2)
    for i in range(-H1 // 2, (dims1[0] + H1) // 2):
        plane = jnp.clip(pos[0] * dims2[0] + i, 0, whole2[0] - 1)
        v = x2s[pl.ds(pl.multiple_of(plane * y2, TILE), y2), :]
        v = pltpu.roll(v, (y2 - pos[1] * dims2[1]) % y2, 0)
        v = jnp.where(iota((TILE, width2), 0) < 4, v[0:TILE], v[y2 - TILE:y2])
        v = pltpu.roll(v, (width2 - pos[2] * dims2[2]) % width2, 1)
        v = jnp.where(lane < LANES // 2, v[:, 0:LANES], v[:, width2 - LANES:width2])
        v = jnp.take_along_axis(v, up_lane, axis=1)
        for half in range(2):
            part = jnp.take_along_axis(v, 4 * half + sub // 2, axis=0)
            rows = slice(half * TILE, (half + 1) * TILE)
            for p in (2 * i + H1, 2 * i + H1 + 1):
                x1s[p, rows, :] = x1s[p, rows, :] + part
    level1.after(x1s, b1_of, b1, 2)

    for i in range(-2, dims1[0] + 2):
        first, second = b1[H1 + i, 0:TILE, :], b1[H1 + i, TILE:2 * TILE, :]
        second = jnp.where(sub < 6, first, second)
        for half, part in enumerate((first, second)):
            part = jnp.take_along_axis(part, 4 * half + sub // 2, axis=0)
            for side in range(2):
                e = jnp.take_along_axis(part, (LANES // 2) * side + lane // 2, axis=1)
                at = (slice(half * TILE, (half + 1) * TILE), slice(side * LANES, (side + 1) * LANES))
                for p in (2 * i + H0, 2 * i + H0 + 1):
                    if 0 <= p < x0.shape[0]:
                        x0[(p,) + at] = x0[(p,) + at] + e
    level0.after(x0, b0, x0, 1)
    for t, p in enumerate(level0.planes(0)):
        p_ref[t] = x0[p, 0:TILE, 0:LANES]
        q_ref[t] = e0[1, p, 0:TILE, 0:LANES] - level0.own_op(x0, p)
    part = pad.at[pl.ds(0, dims2[1] * (count - 1))]
    for kind in range(2):
        pltpu.make_async_copy(part, part, gsend.at[kind]).wait()


def finish(p_ref, q_ref, p_out, q_out):
    p_out[...] = p_ref[...]
    q_out[...] = q_ref[...]


def solution(mesh):
    sizes = tuple(mesh.shape[a] for a in AXES)
    count = sizes[0] * sizes[1] * sizes[2]

    def per_device(b, c):
        dims0 = b.shape
        dims1 = tuple(d // 2 for d in dims0)
        dims2 = tuple(d // 2 for d in dims1)
        assert dims0[1:] == (TILE, LANES) and dims2[0] * dims2[2] == LANES and 8 * dims0[0] == LANES
        whole2 = tuple(d * n for d, n in zip(dims2, sizes))
        assert whole2[1] % TILE == 0
        width2 = -(-whole2[2] // LANES) * LANES
        planes0, planes1 = dims0[0] + 2 * H0, dims1[0] + 2 * H1
        wide = pltpu.VMEM((planes0, 2 * TILE, 2 * LANES), F32)
        slim = pltpu.VMEM((planes1, 2 * TILE, LANES), F32)
        spot = (TILE, LANES)
        scratch = [
            pltpu.VMEM((2, planes0, 2 * TILE, 2 * LANES), F32), wide,
            pltpu.VMEM((2, 3, 3, 2) + spot, F32), pltpu.VMEM((2, 3, 3) + spot, F32),
            pltpu.VMEM((2,) + spot, F32), pltpu.VMEM(spot, F32),
            slim, slim, slim, pltpu.VMEM((3, 2, 3, 3) + spot, F32), pltpu.VMEM((3,) + spot, F32),
            slim, slim, slim,
            pltpu.VMEM((2, sizes[0], sizes[2], whole2[1], LANES), F32), pltpu.VMEM((2,) + spot, F32),
            pltpu.VMEM((dims2[1] * count, LANES), F32), pltpu.VMEM((whole2[0] * whole2[1], width2), F32),
        ] + [wide] * 7 + [slim] * 7 + [
            pltpu.SemaphoreType.DMA((2,)), pltpu.SemaphoreType.DMA((5, 26)), pltpu.SemaphoreType.DMA((5, 26)),
            pltpu.SemaphoreType.DMA((2,)), pltpu.SemaphoreType.DMA((2,)),
        ]
        shape = jax.ShapeDtypeStruct(dims0, F32)
        p, q = pl.pallas_call(
            functools.partial(kernel, sizes, dims0),
            out_shape=(shape, shape),
            in_specs=[pl.BlockSpec(memory_space=pltpu.HBM)] * 2,
            out_specs=(pl.BlockSpec(memory_space=pltpu.VMEM),) * 2,
            scratch_shapes=scratch,
            compiler_params=pltpu.CompilerParams(
                collective_id=0, has_side_effects=True, vmem_limit_bytes=min(48, 16 * max(1, count // 32)) << 20),
        )(b, c)
        return pl.pallas_call(
            finish,
            out_shape=(shape, shape),
            in_specs=[pl.BlockSpec(memory_space=pltpu.VMEM)] * 2,
            out_specs=(pl.BlockSpec(memory_space=pltpu.VMEM),) * 2,
            compiler_params=pltpu.CompilerParams(vmem_limit_bytes=2 << 20),
        )(p, q)

    spec = P(*AXES)
    return jax.shard_map(per_device, mesh=mesh, in_specs=(spec, spec), out_specs=(spec, spec), check_vma=False)
```

```python
import functools
import itertools
import math

import jax
import jax.numpy as jnp
from jax import lax
from jax.experimental import pallas as pl
from jax.experimental.pallas import tpu as pltpu
from jax.sharding import PartitionSpec as P

COARSE_DEGREE = 6
AXES = ("gx", "gy", "gz")
LANES = 128
TILE = 8
H0 = 3
H1 = 4
MESH = pl.DeviceIdType.MESH
F32 = jnp.float32
FACES = ((0, 1), (0, -1), (1, 0), (-1, 0), (1, 1), (1, -1), (-1, 1), (-1, -1))
DIRS = tuple((dx, dy, 0) for dx, dy in FACES) + tuple(
    (dx, dy, dz) for dz in (1, -1) for dx, dy in ((0, 0),) + FACES
)
KERNEL_VMEM = 55088 << 10
CHUNK0, CHUNK1 = 1, 1
CB, C1, B1, X0, X1 = range(5)


def iota(shape, dim):
    return lax.broadcasted_iota(jnp.int32, shape, dim)


def invert(v):
    r = pl.reciprocal(v, approx=True)
    r = r * (2.0 - v * r)
    return r * (2.0 - v * r)


def harmonic(a, b):
    return (2.0 * a * b) * invert(a + b)


def factors(lower, upper):
    theta = (upper + lower) / 2.0
    delta = (upper - lower) / 2.0
    sigma = theta / delta
    rho = 1.0 / sigma
    rho_next = 1.0 / (2.0 * sigma - rho)
    return 1.0 / theta, rho_next * rho, 2.0 * rho_next / delta


def chebyshev(start, source, steps, lower, upper, inv, op_of):
    theta = (upper + lower) / 2.0
    delta = (upper - lower) / 2.0
    sigma = theta / delta
    rho_now = 1.0 / sigma
    if start is None:
        update = source * inv * (1.0 / theta)
        field = update
    else:
        remain = source - op_of(start)
        update = remain * inv * (1.0 / theta)
        field = start + update
    for index in range(steps - 1):
        rho_next = 1.0 / (2.0 * sigma - rho_now)
        remain = source - op_of(field)
        update = rho_next * rho_now * update + (2.0 * rho_next / delta) * (remain * inv)
        field = field + update
        rho_now = rho_next
    return field


def make_coefs(c, around, edges, scale):
    links, total = [], None
    for near, edge in zip(around, edges):
        face = harmonic(c, jnp.where(edge, c, near))
        total = face if total is None else total + face
        links.append(jnp.where(edge, 0.0, face) * scale)
    total = total * scale
    return links, total, invert(total)


def apply_op(v, around, coefs):
    links, total, unused = coefs
    out = total * v
    for near, link in zip(around, links):
        out = out - link * near
    return out


class Level:
    def __init__(self, refs, dims, halo, width, pos, sizes, scale, chunk):
        self.lx, self.ly, self.lz, self.diag, self.inv, self.tmp, self.aux = refs
        self.dims, self.halo, self.width, self.scale, self.chunk = dims, halo, width, scale, chunk
        shape = (2 * TILE, width)
        row, lane = iota(shape, 0), iota(shape, 1)

        def inner(axis):
            low = jnp.where(pos[axis] > 0, 1.0, 0.0).astype(F32)
            high = jnp.where(pos[axis] < sizes[axis] - 1, 1.0, 0.0).astype(F32)
            return low, high

        self.xlow, self.xhigh = inner(0)
        self.ymask = self.zmask = None
        outer = None
        masks = []
        for index, axis in ((row, 1), (lane, 2)):
            low, high = inner(axis)
            last = dims[axis] - 1
            end = shape[axis - 1] - 1
            masks.append(jnp.where(index == end, low, jnp.where(index == last, high, 1.0)))
            part = jnp.where(index == 0, 1.0 - low, jnp.where(index == last, 1.0 - high, 0.0))
            outer = part if outer is None else outer + part
        self.ymask, self.zmask = masks
        self.outer = outer

    def planes(self, reach):
        return range(self.halo - reach, self.halo + self.dims[0] + reach)

    def each(self, reach, body):
        planes = list(self.planes(reach))
        for n in range(0, len(planes), self.chunk):
            for ref, p, v in [store for p in planes[n:n + self.chunk] for store in body(p)]:
                ref[p] = v

    def back(self, v, dim):
        n = v.shape[dim]
        return pltpu.roll(v, n - 1, dim)

    def coefs(self, c_of):
        first, last = self.halo, self.halo + self.dims[0] - 1
        reach = self.halo - 1
        ymask, zmask, outer = self.ymask * self.scale, self.zmask * self.scale, self.outer * self.scale

        def face_x(p):
            factor = {first - 1: self.xlow, last: self.xhigh}.get(p, 1.0) * self.scale
            return harmonic(c_of(p), c_of(p + 1)) * factor

        def others(p):
            c = c_of(p)
            ly = harmonic(c, self.back(c, 0)) * ymask
            lz = harmonic(c, self.back(c, 1)) * zmask
            face = face_x(p)
            total = (face + self.lx[p - 1]) + (ly + pltpu.roll(ly, 1, 0)) + (lz + pltpu.roll(lz, 1, 1))
            around = outer
            if p in (first, last):
                around = around + (1.0 - (self.xlow if p == first else self.xhigh)) * self.scale
            total = total + c * around
            self.lx[p] = face
            return ((self.ly, p, ly), (self.lz, p, lz), (self.diag, p, total), (self.inv, p, invert(total)))

        self.lx[first - reach - 1] = face_x(first - reach - 1)
        self.each(reach, others)

    def op(self, v, p):
        here = v[p]
        ly, lz = self.ly[p], self.lz[p]
        x = self.lx[p] * v[p + 1] + self.lx[p - 1] * v[p - 1]
        y = ly * self.back(here, 0) + pltpu.roll(ly * here, 1, 0)
        z = lz * self.back(here, 1) + pltpu.roll(lz * here, 1, 1)
        return self.diag[p] * here - x - (y + z)

    def own_op(self, v, p):
        own = (slice(0, TILE), slice(0, LANES))
        here = v[p, :, 0:LANES]
        wide = v[p, 0:TILE, :]
        ly, lz = self.ly[p, :, 0:LANES], self.lz[p, 0:TILE, :]
        x = self.lx[p, 0:TILE, 0:LANES] * v[p + 1, 0:TILE, 0:LANES] + self.lx[p - 1, 0:TILE, 0:LANES] * v[p - 1, 0:TILE, 0:LANES]
        y = ly * self.back(here, 0) + pltpu.roll(ly * here, 1, 0)
        z = lz * self.back(wide, 1) + pltpu.roll(lz * wide, 1, 1)
        return self.diag[p, 0:TILE, 0:LANES] * here[own] - x - (y[own] + z[own])

    def before(self, b_of):
        first, mix, gain = factors(0.3, 2.0)

        def one(p):
            return ((self.tmp, p, b_of(p) * self.inv[p] * first),)

        def two(p):
            d = self.tmp[p]
            return ((self.aux, p, d + (mix * d + gain * ((b_of(p) - self.op(self.tmp, p)) * self.inv[p]))),)
        self.each(2, one)
        self.each(1, two)

    def after(self, start, b_of, out, reach):
        first, mix, gain = factors(0.3, 2.0)

        def one(p):
            update = (b_of(p) - self.op(start, p)) * self.inv[p] * first
            return (self.aux, p, update), (self.tmp, p, start[p] + update)

        def two(p):
            update = mix * self.aux[p] + gain * ((b_of(p) - self.op(self.tmp, p)) * self.inv[p])
            return ((out, p, self.tmp[p] + update),)
        self.each(reach + 1, one)
        self.each(reach, two)


def restrict(tiles, lanes, rows):
    out = []
    lane = (2 * iota((TILE, LANES), 1)) % lanes
    row = (2 * iota((TILE, LANES), 0)) % rows
    for a, b in zip(tiles[0::2], tiles[1::2]):
        s = a + b
        s = s + pltpu.roll(s, LANES - 1, 1)
        s = (s + pltpu.roll(s, TILE - 1, 0)) * 0.125
        s = jnp.take_along_axis(s, lane, axis=1)
        out.append(jnp.take_along_axis(s, row, axis=0))
    return out


def kernel(sizes, dims0, b_hbm, c_hbm, p_ref, q_ref, *scratch):
    (e0, x0, zcb, zx0, scb, sx0, c1, b1, x1, z1, s1, c1m, b1m, x1s, slots, tile, pad, x2s) = scratch[:18]
    refs0, refs1 = scratch[18:25], scratch[25:32]
    isem, xsem, gsem = scratch[32:]
    pos = tuple(lax.axis_index(a) for a in AXES)
    dims1 = tuple(d // 2 for d in dims0)
    dims2 = tuple(d // 2 for d in dims1)
    whole2 = tuple(d * n for d, n in zip(dims2, sizes))
    nx, ny, nz = sizes
    count = nx * ny * nz
    me = (pos[0] * ny + pos[1]) * nz + pos[2]
    width2 = x2s.shape[1]
    own0 = pl.ds(H0, dims0[0])

    loads = [
        pltpu.make_async_copy(src, e0.at[k, own0, pl.ds(0, TILE), pl.ds(0, LANES)], isem.at[k])
        for k, src in enumerate((c_hbm, b_hbm))
    ]
    for load in loads:
        load.start()

    def coords(index):
        return (index // (ny * nz), (index // nz) % ny, index % nz)

    barrier = pltpu.get_barrier_semaphore()

    def greet(step, unused):
        pl.semaphore_signal(barrier, inc=1, device_id=coords((me + step) % count), device_id_type=MESH)
        return unused

    for k, value in ((0, 1.0), (1, 0.0)):
        for p in range(e0.shape[1]):
            if not H0 <= p < H0 + dims0[0]:
                e0[k, p, 0:TILE, 0:LANES] = jnp.full((TILE, LANES), value, F32)
            e0[k, p, TILE:2 * TILE, 0:LANES] = jnp.full((TILE, LANES), value, F32)
        for side, i, j in itertools.product(range(2), range(3), range(3)):
            zcb[side, i, j, k] = jnp.full((TILE, LANES), value, F32)
    x0[:, :, 0:LANES] = jnp.zeros((x0.shape[0], 2 * TILE, LANES), F32)
    zx0[...] = jnp.zeros_like(zx0)
    c1[...] = jnp.ones_like(c1)
    b1[...] = jnp.zeros_like(b1)
    x1[...] = jnp.zeros_like(x1)
    z1[0] = jnp.ones(z1.shape[1:], F32)
    z1[1:3] = jnp.zeros((2,) + z1.shape[1:], F32)
    lax.fori_loop(1, count, greet, 0)

    def exists(axis, step):
        if step == 0:
            return None
        return pos[axis] < sizes[axis] - 1 if step > 0 else pos[axis] > 0

    def when(conditions, body):
        conditions = [c for c in conditions if c is not None]
        if not conditions:
            body()
            return
        both = conditions[0]
        for c in conditions[1:]:
            both = both & c
        pl.when(both)(body)

    def each(body):
        for dz in (0, 1, -1):
            def group():
                for n, d in enumerate(DIRS):
                    if d[2] == dz:
                        when([exists(0, d[0]), exists(1, d[1])], functools.partial(body, n))
            when([exists(2, dz)], group)

    def cut(step, n, halo, wrap):
        if step == 0:
            return (0, 0, n)
        if step > 0:
            return (n - halo, wrap - halo, halo)
        return (0, n, halo)

    def ends(xid, n):
        dx, dy, dz = DIRS[n]
        if dz:
            packed = {CB: scb, X0: sx0}.get(xid)
            arrived = {CB: zcb, X0: zx0}.get(xid)
            if packed is None:
                at = (C1, B1, X1).index(xid)
                packed, arrived = s1.at[at], z1.at[at]
            return packed, arrived.at[0 if dz > 0 else 1, 1 - dx, 1 - dy]
        low, halo = (xid in (CB, X0)), (H0 if xid in (CB, X0) else H1)
        dims = dims0 if low else dims1
        a, b, planes = cut(dx, dims[0], halo, 0)
        r, s, rows = cut(dy, dims[1], min(halo, dims[1]), 2 * TILE)
        if low:
            ref = e0 if xid == CB else x0
            lead = (slice(None),) if xid == CB else ()
            lanes = (pl.ds(0, LANES),)
        else:
            ref, lead, lanes = {C1: c1, B1: b1, X1: x1}[xid], (), (slice(None),)
        src = ref.at[lead + (pl.ds(halo + a, planes), pl.ds(r, rows)) + lanes]
        dst = ref.at[lead + (pl.ds(halo + b, planes), pl.ds(s, rows)) + lanes]
        return src, dst

    def remote(xid, n):
        src, dst = ends(xid, n)
        return pltpu.make_async_remote_copy(
            src_ref=src, dst_ref=dst, send_sem=xsem.at[xid], recv_sem=xsem.at[xid],
            device_id=tuple(p + d for p, d in zip(pos, DIRS[n])), device_id_type=MESH,
        )

    def launch(xid):
        each(lambda n: remote(xid, n).start())

    def settle(xid):
        kinds = []
        for axis, n in enumerate(sizes):
            inside = (pos[axis] > 0) & (pos[axis] < n - 1)
            kinds.append([(0, None)] if n == 1 else [(1, None)] if n == 2 else [(1, jnp.logical_not(inside)), (2, inside)])
        for case in itertools.product(*kinds):
            rows = 0
            for n, d in enumerate(DIRS):
                if min(d) >= 0:
                    shape = ends(xid, n)[0].shape
                    rows += math.prod(shape[:-1]) * math.prod(k for (k, unused), step in zip(case, d) if step)
            part = pad.at[pl.ds(0, 2 * rows)]
            when([c for unused, c in case], pltpu.make_async_copy(part, part, xsem.at[xid]).wait)

    lane, sub = iota((TILE, LANES), 1), iota((TILE, LANES), 0)

    def pack0(tiles):
        out = tiles[0]
        for t in range(1, len(tiles)):
            part = pltpu.roll(tiles[t], 8 * t, 1)
            out = jnp.where(((lane - (8 * t - 4)) % LANES) < 8, part, out)
        return out

    def pack1(tiles):
        out = tiles[0]
        for t in range(1, len(tiles)):
            part = pltpu.roll(tiles[t], 8 * t, 1)
            place = (lane - 8 * t) % LANES
            out = jnp.where((place < 4) | ((place >= 60) & (place < 64)), part, out)
        return out

    def both_sides(arrived, dx, dy, k=None):
        at = (dx + 1, dy + 1) + (() if k is None else (k,))
        return jnp.where(lane % 8 < 4, arrived[(1,) + at], arrived[(0,) + at])

    def group_planes(n, halo):
        return ((0, [(t, halo + t) for t in range(n)]),
                (-1, [(t, halo + t - n) for t in range(n - halo, n)]),
                (1, [(t, halo + n + t) for t in range(halo)]))

    def unpack0(arrived, k, store):
        for dx, pairs in group_planes(dims0[0], H0):
            first = both_sides(arrived, dx, 0, k)
            second = jnp.where(sub < 4, both_sides(arrived, dx, 1, k), both_sides(arrived, dx, -1, k))
            for t, p in pairs:
                shift = (-8 * t) % LANES
                store(p, 0, pltpu.roll(first, shift, 1) if shift else first)
                store(p, 1, pltpu.roll(second, shift, 1) if shift else second)

    def unpack1(arrived, field, store):
        z = dims1[2]
        for dx, pairs in group_planes(dims1[0], H1):
            first = jnp.where(sub < 4, both_sides(arrived, dx, 0), both_sides(arrived, dx, 1))
            second = both_sides(arrived, dx, -1)
            for t, p in pairs:
                shift = (z - 8 * t) % LANES
                for half, part in enumerate((first, second)):
                    rows = slice(half * TILE, (half + 1) * TILE)
                    part = pltpu.roll(part, shift, 1) if shift else part
                    store(p, rows, jnp.where(lane < z, field[p, rows, :], part))

    def post1(field, packed, tiles):
        for i, v in enumerate(tiles):
            field[H1 + i, 0:dims1[1], :] = v[0:dims1[1]]
        packed[...] = pack1(tiles)

    def message(tiles):
        out = tiles[0]
        for i in range(1, dims2[0]):
            out = jnp.where(lane // dims2[2] == i, tiles[i], out)
        return out

    def slot(kind, x, y, z):
        return slots.at[kind, x, z, pl.ds(dims2[1] * y, dims2[1])]

    def gather_start(kind, value):
        tile[kind] = value
        src = tile.at[kind, pl.ds(0, dims2[1])]

        def go(step, unused):
            pltpu.make_async_remote_copy(
                src_ref=src, dst_ref=slot(kind, *pos), send_sem=gsem.at[kind], recv_sem=gsem.at[kind],
                device_id=coords((me + step) % count), device_id_type=MESH,
            ).start()
            return unused
        lax.fori_loop(1, count, go, 0)
        pltpu.make_async_copy(src, slot(kind, *pos), gsem.at[kind]).start()

    def gather_finish(kind, outside):
        part = pad.at[pl.ds(0, dims2[1] * (2 * count - 1))]
        pltpu.make_async_copy(part, part, gsem.at[kind]).wait()
        z = dims2[2]
        per = LANES // z
        spot = iota((whole2[1], LANES), 1)
        planes = []
        for x in range(nx):
            for i in range(dims2[0]):
                columns = []
                for first in range(0, width2 // z, per):
                    total = None
                    for g in range(min(per, nz - first)):
                        shift = (z * (g - i)) % LANES
                        part = slots[kind, x, first + g]
                        part = pltpu.roll(part, shift, 1) if shift else part
                        total = part if total is None else jnp.where(spot // z == g, part, total)
                    columns.append(total)
                planes.append(columns[0] if len(columns) == 1 else jnp.concatenate(columns, 1))
        v = jnp.concatenate(planes, 0)
        if whole2[2] < width2:
            v = jnp.where(iota(v.shape, 1) < whole2[2], v, outside)
        return v

    for load in loads:
        load.wait()
    for k in range(2):
        scb[k] = pack0([e0[k, H0 + t, 0:TILE, 0:LANES] for t in range(dims0[0])])
    pl.semaphore_wait(barrier, count - 1)

    launch(CB)
    tiles = restrict([e0[0, H0 + t, 0:TILE, 0:LANES] for t in range(dims0[0])], dims0[2], dims0[1])
    post1(c1, s1.at[0], tiles)
    launch(C1)
    gather_start(0, message(restrict(tiles, dims1[2], dims1[1])))

    level0 = Level(refs0, dims0, H0, 2 * LANES, pos, sizes, 1.0, CHUNK0)
    level1 = Level(refs1, dims1, H1, LANES, pos, sizes, 0.25, CHUNK1)

    settle(CB)
    for k in range(2):
        def put(p, half, value):
            e0[k, p, half * TILE:(half + 1) * TILE, LANES:2 * LANES] = value
        unpack0(zcb, k, put)
    level0.coefs(lambda p: e0[0, p])
    b0 = lambda p: e0[1, p]
    level0.before(b0)
    r0 = [e0[1, p, 0:TILE, 0:LANES] - level0.own_op(level0.aux, p) for p in level0.planes(0)]
    tiles = restrict(r0, dims0[2], dims0[1])
    post1(b1, s1.at[1], tiles)
    launch(B1)

    tiles = [level0.aux[p, 0:TILE, 0:LANES] for p in level0.planes(0)]
    for p, v in zip(level0.planes(0), tiles):
        x0[p, 0:TILE, 0:LANES] = v
    sx0[...] = pack0(tiles)
    launch(X0)
    settle(C1)

    def put_c1(p, rows, value):
        c1m[p, rows, :] = value
    unpack1(z1.at[0], c1, put_c1)
    level1.coefs(lambda p: c1m[p])

    settle(B1)

    def put_b1(p, rows, value):
        b1m[p, rows, :] = value
    unpack1(z1.at[1], b1, put_b1)
    b1_of = lambda p: b1m[p]
    level1.before(b1_of)
    r1 = [b1m[p, 0:TILE, :] - level1.own_op(level1.aux, p) for p in level1.planes(0)]
    gather_start(1, message(restrict(r1, dims1[2], dims1[1])))
    tiles = [level1.aux[p, 0:TILE, :] for p in level1.planes(0)]
    tiles = [jnp.where(lane < dims1[2], v, pltpu.roll(v, dims1[2], 1)) for v in tiles]
    tiles = [jnp.where(sub < dims1[1], v, pltpu.roll(v, dims1[1], 0)) for v in tiles]
    post1(x1, s1.at[2], tiles)
    launch(X1)

    y2, z2 = whole2[1], whole2[2]
    shape2 = (whole2[0] * y2, width2)
    shape3 = (shape2[0] // 2, width2)

    def near2(v):
        n = v.shape[0]
        return (pltpu.roll(v, y2, 0), pltpu.roll(v, n - y2, 0), pltpu.roll(v, 1, 0), pltpu.roll(v, n - 1, 0),
                pltpu.roll(v, 1, 1), pltpu.roll(v, width2 - 1, 1))

    def near3(v):
        n = v.shape[0]
        return (pltpu.roll(v, y2, 0), pltpu.roll(v, n - y2, 0), pltpu.roll(v, 2, 0), pltpu.roll(v, n - 2, 0),
                pltpu.roll(v, 2, 1), pltpu.roll(v, width2 - 2, 1))

    def edges(shape, step):
        plane, row, spot = iota(shape, 0) // y2, iota(shape, 0) % y2, iota(shape, 1)
        return (plane == 0, plane == shape[0] // y2 - 1, row == 0, row == y2 - step, spot == 0, spot >= z2 - step)

    def pairs(v):
        return [v[n * y2:(n + 1) * y2] for n in range(v.shape[0] // y2)]

    def restrict2(v):
        planes = pairs(v)
        s = jnp.concatenate([a + b for a, b in zip(planes[0::2], planes[1::2])], 0)
        s = s + pltpu.roll(s, width2 - 1, 1)
        return (s + pltpu.roll(s, s.shape[0] - 1, 0)) * 0.125

    def prolong3(v):
        v = jnp.where((iota(shape3, 0) % 2 == 0) & (iota(shape3, 1) % 2 == 0), v, 0.0)
        v = v + pltpu.roll(v, 1, 1)
        v = v + pltpu.roll(v, 1, 0)
        return jnp.concatenate([part for part in pairs(v) for unused in range(2)], 0)

    c2 = gather_finish(0, 1.0)
    coefs2 = make_coefs(c2, near2(c2), edges(shape2, 1), 0.25 ** 2)
    c3 = restrict2(c2)
    coefs3 = make_coefs(c3, near3(c3), edges(shape3, 2), 0.25 ** 3)

    def op2(v):
        return apply_op(v, near2(v), coefs2)

    def op3(v):
        return apply_op(v, near3(v), coefs3)

    settle(X0)

    def put_x0(p, half, value):
        x0[p, half * TILE:(half + 1) * TILE, LANES:2 * LANES] = value
    unpack0(zx0, None, put_x0)
    settle(X1)

    def put_x1(p, rows, value):
        x1s[p, rows, :] = value
    unpack1(z1.at[2], x1, put_x1)

    b2 = gather_finish(1, 0.0)
    x2 = chebyshev(None, b2, 2, 0.3, 2.0, coefs2[2], op2)
    b3 = restrict2(b2 - op2(x2))
    x3 = chebyshev(None, b3, COARSE_DEGREE, 0.05, 2.0, coefs3[2], op3)
    x2 = chebyshev(x2 + prolong3(x3), b2, 2, 0.3, 2.0, coefs2[2], op2)
    x2s[...] = x2

    quarter = LANES // 4
    first_lane, first_row = pos[2] * dims2[2], pos[1] * dims2[1]
    lanes = (first_lane + width2 + jnp.where(lane < 3 * quarter, lane // 2, lane // 2 - 2 * quarter)) % width2
    rows = [sub // 2 + 4 * half for half in range(2)]
    rows = [(first_row + y2 + jnp.where(r < 6, r, r - TILE)) % y2 for r in rows]
    low = ((first_row + y2 - 2) % y2) // TILE, ((first_lane + width2 - quarter // 2) % width2) // LANES
    high = ((first_row + 5) % y2) // TILE, ((first_lane + quarter + quarter // 2 - 1) % width2) // LANES
    window = range(-H1 // 2, (dims1[0] + H1) // 2)
    spread = []
    for i in window:
        plane = jnp.clip(pos[0] * dims2[0] + i, 0, whole2[0] - 1)

        def wide(row_tile):
            at = pl.ds(pl.multiple_of(plane * y2 + row_tile * TILE, TILE), TILE)
            if width2 == LANES:
                return jnp.take_along_axis(x2s[at, :], lanes, axis=1)
            parts = [x2s[at, pl.ds(pl.multiple_of(t * LANES, LANES), LANES)] for t in (low[1], high[1])]
            parts = [jnp.take_along_axis(v, lanes % LANES, axis=1) for v in parts]
            return jnp.where(lanes // LANES == low[1], *parts)
        if y2 == TILE:
            v = wide(0)
            spread.append([jnp.take_along_axis(v, r, axis=0) for r in rows])
        else:
            v, w = wide(low[0]), wide(high[0])
            spread.append([
                jnp.where(r // TILE == low[0], *(jnp.take_along_axis(u, r % TILE, axis=0) for u in (v, w))) for r in rows])
    for i, halves in zip(window, spread):
        for half, part in enumerate(halves):
            rows = slice(half * TILE, (half + 1) * TILE)
            for p in (2 * i + H1, 2 * i + H1 + 1):
                x1s[p, rows, :] = x1s[p, rows, :] + part
    level1.after(x1s, b1_of, b1, 2)

    window = range(-2, dims1[0] + 2)
    for group in range(0, len(window), 4):
        results = []
        for i in window[group:group + 4]:
            first, second = b1[H1 + i, 0:TILE, :], b1[H1 + i, TILE:2 * TILE, :]
            second = jnp.where(sub < 6, first, second)
            for half, part in enumerate((first, second)):
                part = jnp.take_along_axis(part, 4 * half + sub // 2, axis=0)
                for side in range(2):
                    e = jnp.take_along_axis(part, (LANES // 2) * side + lane // 2, axis=1)
                    at = (slice(half * TILE, (half + 1) * TILE), slice(side * LANES, (side + 1) * LANES))
                    for p in (2 * i + H0, 2 * i + H0 + 1):
                        if 0 <= p < x0.shape[0]:
                            results.append(((p,) + at, x0[(p,) + at] + e))
        for at, v in results:
            x0[at] = v
    level0.after(x0, b0, x0, 1)
    for t, p in enumerate(level0.planes(0)):
        p_ref[t] = x0[p, 0:TILE, 0:LANES]
        q_ref[t] = e0[1, p, 0:TILE, 0:LANES] - level0.own_op(x0, p)


def finish(p_ref, q_ref, p_out, q_out):
    p_out[...] = p_ref[...]
    q_out[...] = q_ref[...]


def solution(mesh):
    sizes = tuple(mesh.shape[a] for a in AXES)
    count = sizes[0] * sizes[1] * sizes[2]

    def per_device(b, c):
        dims0 = b.shape
        dims1 = tuple(d // 2 for d in dims0)
        dims2 = tuple(d // 2 for d in dims1)
        assert dims0[1:] == (TILE, LANES) and dims2[0] * dims2[2] == LANES and 8 * dims0[0] == LANES
        whole2 = tuple(d * n for d, n in zip(dims2, sizes))
        assert whole2[1] % TILE == 0
        width2 = -(-whole2[2] // LANES) * LANES
        planes0, planes1 = dims0[0] + 2 * H0, dims1[0] + 2 * H1
        wide = pltpu.VMEM((planes0, 2 * TILE, 2 * LANES), F32)
        slim = pltpu.VMEM((planes1, 2 * TILE, LANES), F32)
        spot = (TILE, LANES)
        scratch = [
            pltpu.VMEM((2, planes0, 2 * TILE, 2 * LANES), F32), wide,
            pltpu.VMEM((2, 3, 3, 2) + spot, F32), pltpu.VMEM((2, 3, 3) + spot, F32),
            pltpu.VMEM((2,) + spot, F32), pltpu.VMEM(spot, F32),
            slim, slim, slim, pltpu.VMEM((3, 2, 3, 3) + spot, F32), pltpu.VMEM((3,) + spot, F32),
            slim, slim, slim,
            pltpu.VMEM((2, sizes[0], sizes[2], whole2[1], LANES), F32), pltpu.VMEM((2,) + spot, F32),
            pltpu.VMEM((max(2 * dims2[1] * count, 32 * dims0[0] * TILE), LANES), F32), pltpu.VMEM((whole2[0] * whole2[1], width2), F32),
        ] + [wide] * 7 + [slim] * 7 + [
            pltpu.SemaphoreType.DMA((2,)), pltpu.SemaphoreType.DMA((5,)), pltpu.SemaphoreType.DMA((2,)),
        ]
        shape = jax.ShapeDtypeStruct(dims0, F32)
        p, q = pl.pallas_call(
            functools.partial(kernel, sizes, dims0),
            out_shape=(shape, shape),
            in_specs=[pl.BlockSpec(memory_space=pltpu.HBM)] * 2,
            out_specs=(pl.BlockSpec(memory_space=pltpu.VMEM),) * 2,
            scratch_shapes=scratch,
            compiler_params=pltpu.CompilerParams(
                collective_id=0, has_side_effects=True, vmem_limit_bytes=KERNEL_VMEM),
        )(b, c)
        return pl.pallas_call(
            finish,
            out_shape=(shape, shape),
            in_specs=[pl.BlockSpec(memory_space=pltpu.VMEM)] * 2,
            out_specs=(pl.BlockSpec(memory_space=pltpu.VMEM),) * 2,
            compiler_params=pltpu.CompilerParams(vmem_limit_bytes=2 << 20),
        )(p, q)

    spec = P(*AXES)
    return jax.shard_map(per_device, mesh=mesh, in_specs=(spec, spec), out_specs=(spec, spec), check_vma=False)
```

```python
import functools
import itertools
import math

import jax
import jax.numpy as jnp
from jax import lax
from jax.experimental import pallas as pl
from jax.experimental.pallas import tpu as pltpu
from jax.sharding import PartitionSpec as P

COARSE_DEGREE = 6
AXES = ("gx", "gy", "gz")
LANES = 128
TILE = 8
H0 = 3
H1 = 4
MESH = pl.DeviceIdType.MESH
F32 = jnp.float32
FACES = ((0, 1), (0, -1), (1, 0), (-1, 0), (1, 1), (1, -1), (-1, 1), (-1, -1))
DIRS = tuple((dx, dy, 0) for dx, dy in FACES) + tuple(
    (dx, dy, dz) for dz in (1, -1) for dx, dy in ((0, 0),) + FACES
)
KERNEL_VMEM = 55088 << 10
CB, C1, B1, X0, X1 = range(5)


def iota(shape, dim):
    return lax.broadcasted_iota(jnp.int32, shape, dim)


def invert(v):
    r = pl.reciprocal(v, approx=True)
    return r * (2.0 - v * r)


def factors(lower, upper):
    theta = (upper + lower) / 2.0
    delta = (upper - lower) / 2.0
    sigma = theta / delta
    rho = 1.0 / sigma
    rho_next = 1.0 / (2.0 * sigma - rho)
    return 1.0 / theta, rho_next * rho, 2.0 * rho_next / delta


def chebyshev(start, source, steps, lower, upper, level):
    op_of, inv = level.op, level.inv()
    theta = (upper + lower) / 2.0
    delta = (upper - lower) / 2.0
    sigma = theta / delta
    rho_now = 1.0 / sigma
    if start is None:
        update = source * inv * (1.0 / theta)
        field = update
    else:
        remain = source - op_of(start)
        update = remain * inv * (1.0 / theta)
        field = start + update
    for index in range(steps - 1):
        rho_next = 1.0 / (2.0 * sigma - rho_now)
        remain = source - op_of(field)
        update = rho_next * rho_now * update + (2.0 * rho_next / delta) * (remain * inv)
        field = field + update
        rho_now = rho_next
    return field


class Flat:
    def __init__(self, refs, rows, lanes, step, scale):
        self.refs, self.rows, self.lanes, self.step, self.scale = refs, rows, lanes, step, scale

    def ahead(self, v, axis):
        if axis == 2:
            return pltpu.roll(v, v.shape[1] - self.step, 1)
        return pltpu.roll(v, v.shape[0] - (self.step if axis else self.rows), 0)

    def behind(self, v, axis):
        if axis == 2:
            return pltpu.roll(v, self.step, 1)
        return pltpu.roll(v, self.step if axis else self.rows, 0)

    def coefs(self, c):
        n = c.shape[0] // self.rows
        row, lane = iota(c.shape, 0), iota(c.shape, 1)
        spots = ((row // self.rows, 1, n), (row % self.rows, self.step, self.rows), (lane, self.step, self.lanes))
        half = invert(c * (2.0 * self.scale))
        total = None
        for axis, (spot, step, end) in enumerate(spots):
            link = jnp.where(spot >= end - step, 0.0, invert(half + self.ahead(half, axis)))
            self.refs[axis][...] = link
            around = jnp.where(spot < step, 1.0, 0.0) + jnp.where(spot >= end - step, 1.0, 0.0)
            part = link + self.behind(link, axis) + c * (around * self.scale)
            total = part if total is None else total + part
        self.refs[3][...] = total
        self.refs[4][...] = invert(total)

    def inv(self):
        return self.refs[4][...]

    def op(self, v):
        out = self.refs[3][...] * v
        for axis in range(3):
            link = self.refs[axis][...]
            out = out - (link * self.ahead(v, axis) + self.behind(link * v, axis))
        return out


class Level:
    def __init__(self, refs, dims, halo, width, pos, sizes, scale):
        self.lx, self.ly, self.lz, self.diag, self.inv, self.tmp, self.aux = refs
        self.dims, self.halo, self.width, self.scale = dims, halo, width, scale
        shape = (2 * TILE, width)
        row, lane = iota(shape, 0), iota(shape, 1)

        def inner(axis):
            low = jnp.where(pos[axis] > 0, 1.0, 0.0).astype(F32)
            high = jnp.where(pos[axis] < sizes[axis] - 1, 1.0, 0.0).astype(F32)
            return low, high

        self.xlow, self.xhigh = inner(0)
        self.ymask = self.zmask = None
        outer = None
        masks = []
        for index, axis in ((row, 1), (lane, 2)):
            low, high = inner(axis)
            last = dims[axis] - 1
            end = shape[axis - 1] - 1
            masks.append(jnp.where(index == end, low, jnp.where(index == last, high, 1.0)))
            part = jnp.where(index == 0, 1.0 - low, jnp.where(index == last, 1.0 - high, 0.0))
            outer = part if outer is None else outer + part
        self.ymask, self.zmask = masks
        self.outer = outer

    def planes(self, reach):
        return range(self.halo - reach, self.halo + self.dims[0] + reach)

    def put(self, ref, p, v, budget, kind=""):
        own, row_side = slice(0, TILE), slice(TILE, 2 * TILE)
        lanes = slice(0, LANES)
        if self.width == LANES or budget >= 2 or (budget == 1 and kind in ("y", "z")):
            ref[p] = v
        elif kind == "y":
            ref[p, :, lanes] = v[:, lanes]
        elif budget == 1:
            ref[p, own, :] = v[own, :]
            ref[p, row_side, lanes] = v[row_side, lanes]
        elif kind == "z":
            ref[p, own, :] = v[own, :]
        else:
            ref[p, own, lanes] = v[own, lanes]

    def each(self, reach, body):
        first, last = self.halo, self.halo + self.dims[0] - 1
        for p in self.planes(reach):
            for ref, q, v, *kind in body(p):
                near = p + 1 if kind == ["x"] and p < first else p
                self.put(ref, q, v, reach - max(0, first - near, near - last), *kind)

    def back(self, v, dim):
        n = v.shape[dim]
        return pltpu.roll(v, n - 1, dim)

    def coefs(self, c_of):
        first, last = self.halo, self.halo + self.dims[0] - 1
        reach = self.halo - 1
        outer = self.outer * self.scale

        half = {}

        def half_of(p):
            if p not in half:
                half[p] = invert(c_of(p) * (2.0 * self.scale))
            return half[p]

        def face_x(p):
            face = invert(half_of(p) + half_of(p + 1))
            factor = {first - 1: self.xlow, last: self.xhigh}.get(p)
            return face if factor is None else face * factor

        def others(p):
            h = half_of(p)
            ly = invert(h + self.back(h, 0)) * self.ymask
            lz = invert(h + self.back(h, 1)) * self.zmask
            face = face_x(p)
            total = (face + faces.pop()) + (ly + pltpu.roll(ly, 1, 0)) + (lz + pltpu.roll(lz, 1, 1))
            faces.append(face)
            around = outer
            if p in (first, last):
                around = around + (1.0 - (self.xlow if p == first else self.xhigh)) * self.scale
            total = total + c_of(p) * around
            return (self.lx, p, face, "x"), (self.ly, p, ly, "y"), (self.lz, p, lz, "z"), (self.diag, p, total), (self.inv, p, invert(total))

        faces = [face_x(first - reach - 1)]
        self.put(self.lx, first - reach - 1, faces[0], 0)
        self.each(reach, others)

    def op(self, v, p):
        here = v[p]
        ly, lz = self.ly[p], self.lz[p]
        x = self.lx[p] * v[p + 1] + self.lx[p - 1] * v[p - 1]
        y = ly * self.back(here, 0) + pltpu.roll(ly * here, 1, 0)
        z = lz * self.back(here, 1) + pltpu.roll(lz * here, 1, 1)
        return self.diag[p] * here - x - (y + z)

    def own_op(self, v, p):
        own = (slice(0, TILE), slice(0, LANES))
        here = v[p, :, 0:LANES]
        wide = v[p, 0:TILE, :]
        ly, lz = self.ly[p, :, 0:LANES], self.lz[p, 0:TILE, :]
        x = self.lx[p, 0:TILE, 0:LANES] * v[p + 1, 0:TILE, 0:LANES] + self.lx[p - 1, 0:TILE, 0:LANES] * v[p - 1, 0:TILE, 0:LANES]
        y = ly * self.back(here, 0) + pltpu.roll(ly * here, 1, 0)
        z = lz * self.back(wide, 1) + pltpu.roll(lz * wide, 1, 1)
        return self.diag[p, 0:TILE, 0:LANES] * here[own] - x - (y[own] + z[own])

    def before(self, b_of):
        first, mix, gain = factors(0.3, 2.0)

        def one(p):
            return ((self.tmp, p, b_of(p) * self.inv[p] * first),)

        def two(p):
            d = self.tmp[p]
            return ((self.aux, p, d + (mix * d + gain * ((b_of(p) - self.op(self.tmp, p)) * self.inv[p]))),)
        self.each(2, one)
        self.each(1, two)

    def after(self, start, b_of, out, reach):
        first, mix, gain = factors(0.3, 2.0)

        def one(p):
            update = (b_of(p) - self.op(start, p)) * self.inv[p] * first
            return (self.aux, p, update), (self.tmp, p, start[p] + update)

        def two(p):
            update = mix * self.aux[p] + gain * ((b_of(p) - self.op(self.tmp, p)) * self.inv[p])
            return ((out, p, self.tmp[p] + update),)
        self.each(reach + 1, one)
        self.each(reach, two)


def restrict(tiles, lanes, rows):
    out = []
    lane = (2 * iota((TILE, LANES), 1)) % lanes
    row = (2 * iota((TILE, LANES), 0)) % rows
    for a, b in zip(tiles[0::2], tiles[1::2]):
        s = a + b
        s = s + pltpu.roll(s, LANES - 1, 1)
        s = (s + pltpu.roll(s, TILE - 1, 0)) * 0.125
        s = jnp.take_along_axis(s, lane, axis=1)
        out.append(jnp.take_along_axis(s, row, axis=0))
    return out


def kernel(sizes, dims0, b_hbm, c_hbm, p_ref, q_ref, *scratch):
    (e0, x0, zcb, zx0, scb, sx0, c1, b1, x1, z1, s1, c1m, b1m, x1s, slots, tile, pad, x2s) = scratch[:18]
    refs0, refs1, refs2, refs3 = scratch[18:25], scratch[25:32], scratch[32:37], scratch[37:42]
    isem, xsem, gsem = scratch[42:]
    pos = tuple(lax.axis_index(a) for a in AXES)
    dims1 = tuple(d // 2 for d in dims0)
    dims2 = tuple(d // 2 for d in dims1)
    whole2 = tuple(d * n for d, n in zip(dims2, sizes))
    nx, ny, nz = sizes
    count = nx * ny * nz
    me = (pos[0] * ny + pos[1]) * nz + pos[2]
    width2 = x2s.shape[1]
    own0 = pl.ds(H0, dims0[0])

    loads = [
        pltpu.make_async_copy(src, e0.at[k, own0, pl.ds(0, TILE), pl.ds(0, LANES)], isem.at[k])
        for k, src in enumerate((c_hbm, b_hbm))
    ]
    for load in loads:
        load.start()

    def coords(index):
        return (index // (ny * nz), (index // nz) % ny, index % nz)

    barrier = pltpu.get_barrier_semaphore()

    def greet(step, unused):
        pl.semaphore_signal(barrier, inc=1, device_id=coords((me + step) % count), device_id_type=MESH)
        return unused

    for k, value in ((0, 1.0), (1, 0.0)):
        for p in range(e0.shape[1]):
            if not H0 <= p < H0 + dims0[0]:
                e0[k, p, 0:TILE, 0:LANES] = jnp.full((TILE, LANES), value, F32)
            e0[k, p, TILE:2 * TILE, 0:LANES] = jnp.full((TILE, LANES), value, F32)
        for side, i, j in itertools.product(range(2), range(3), range(3)):
            zcb[side, i, j, k] = jnp.full((TILE, LANES), value, F32)
    x0[:, :, 0:LANES] = jnp.zeros((x0.shape[0], 2 * TILE, LANES), F32)
    zx0[...] = jnp.zeros_like(zx0)
    c1[...] = jnp.ones_like(c1)
    b1[...] = jnp.zeros_like(b1)
    x1[...] = jnp.zeros_like(x1)
    z1[0] = jnp.ones(z1.shape[1:], F32)
    z1[1:3] = jnp.zeros((2,) + z1.shape[1:], F32)
    lax.fori_loop(1, count, greet, 0)

    def exists(axis, step):
        if step == 0:
            return None
        return pos[axis] < sizes[axis] - 1 if step > 0 else pos[axis] > 0

    def when(conditions, body):
        conditions = [c for c in conditions if c is not None]
        if not conditions:
            body()
            return
        both = conditions[0]
        for c in conditions[1:]:
            both = both & c
        pl.when(both)(body)

    def each(body):
        for dz in (0, 1, -1):
            def group():
                for n, d in enumerate(DIRS):
                    if d[2] == dz:
                        when([exists(0, d[0]), exists(1, d[1])], functools.partial(body, n))
            when([exists(2, dz)], group)

    def cut(step, n, halo, wrap):
        if step == 0:
            return (0, 0, n)
        if step > 0:
            return (n - halo, wrap - halo, halo)
        return (0, n, halo)

    def ends(xid, n):
        dx, dy, dz = DIRS[n]
        if dz:
            packed = {CB: scb, X0: sx0}.get(xid)
            arrived = {CB: zcb, X0: zx0}.get(xid)
            if packed is None:
                at = (C1, B1, X1).index(xid)
                packed, arrived = s1.at[at], z1.at[at]
            return packed, arrived.at[0 if dz > 0 else 1, 1 - dx, 1 - dy]
        low, halo = (xid in (CB, X0)), (H0 if xid in (CB, X0) else H1)
        dims = dims0 if low else dims1
        a, b, planes = cut(dx, dims[0], halo, 0)
        r, s, rows = cut(dy, dims[1], min(halo, dims[1]), 2 * TILE)
        if low:
            ref = e0 if xid == CB else x0
            lead = (slice(None),) if xid == CB else ()
            lanes = (pl.ds(0, LANES),)
        else:
            ref, lead, lanes = {C1: c1, B1: b1, X1: x1}[xid], (), (slice(None),)
        src = ref.at[lead + (pl.ds(halo + a, planes), pl.ds(r, rows)) + lanes]
        dst = ref.at[lead + (pl.ds(halo + b, planes), pl.ds(s, rows)) + lanes]
        return src, dst

    def remote(xid, n):
        src, dst = ends(xid, n)
        return pltpu.make_async_remote_copy(
            src_ref=src, dst_ref=dst, send_sem=xsem.at[xid], recv_sem=xsem.at[xid],
            device_id=tuple(p + d for p, d in zip(pos, DIRS[n])), device_id_type=MESH,
        )

    def launch(xid):
        each(lambda n: remote(xid, n).start())

    def settle(xid):
        kinds = []
        for axis, n in enumerate(sizes):
            inside = (pos[axis] > 0) & (pos[axis] < n - 1)
            kinds.append([(0, None)] if n == 1 else [(1, None)] if n == 2 else [(1, jnp.logical_not(inside)), (2, inside)])
        for case in itertools.product(*kinds):
            rows = 0
            for n, d in enumerate(DIRS):
                if min(d) >= 0:
                    shape = ends(xid, n)[0].shape
                    rows += math.prod(shape[:-1]) * math.prod(k for (k, unused), step in zip(case, d) if step)
            part = pad.at[pl.ds(0, 2 * rows)]
            when([c for unused, c in case], pltpu.make_async_copy(part, part, xsem.at[xid]).wait)

    lane, sub = iota((TILE, LANES), 1), iota((TILE, LANES), 0)

    def pack0(tiles):
        out = tiles[0]
        for t in range(1, len(tiles)):
            part = pltpu.roll(tiles[t], 8 * t, 1)
            out = jnp.where(((lane - (8 * t - 4)) % LANES) < 8, part, out)
        return out

    def pack1(tiles):
        out = tiles[0]
        for t in range(1, len(tiles)):
            part = pltpu.roll(tiles[t], 8 * t, 1)
            place = (lane - 8 * t) % LANES
            out = jnp.where((place < 4) | ((place >= 60) & (place < 64)), part, out)
        return out

    def both_sides(arrived, dx, dy, k=None):
        at = (dx + 1, dy + 1) + (() if k is None else (k,))
        return jnp.where(lane % 8 < 4, arrived[(1,) + at], arrived[(0,) + at])

    def group_planes(n, halo):
        return ((0, [(t, halo + t) for t in range(n)]),
                (-1, [(t, halo + t - n) for t in range(n - halo, n)]),
                (1, [(t, halo + n + t) for t in range(halo)]))

    def unpack0(arrived, k, store):
        for dx, pairs in group_planes(dims0[0], H0):
            first = both_sides(arrived, dx, 0, k)
            second = jnp.where(sub < 4, both_sides(arrived, dx, 1, k), both_sides(arrived, dx, -1, k))
            for t, p in pairs:
                shift = (-8 * t) % LANES
                beyond = max(0, H0 - p, p - (H0 + dims0[0] - 1))
                if beyond < H0:
                    store(p, 0, pltpu.roll(first, shift, 1) if shift else first)
                if beyond < H0 - 1:
                    store(p, 1, pltpu.roll(second, shift, 1) if shift else second)

    def unpack1(arrived, field, store):
        z = dims1[2]
        for dx, pairs in group_planes(dims1[0], H1):
            first = jnp.where(sub < 4, both_sides(arrived, dx, 0), both_sides(arrived, dx, 1))
            second = both_sides(arrived, dx, -1)
            for t, p in pairs:
                shift = (z - 8 * t) % LANES
                for half, part in enumerate((first, second)):
                    rows = slice(half * TILE, (half + 1) * TILE)
                    part = pltpu.roll(part, shift, 1) if shift else part
                    store(p, rows, jnp.where(lane < z, field[p, rows, :], part))

    def post1(field, packed, tiles):
        for i, v in enumerate(tiles):
            field[H1 + i, 0:dims1[1], :] = v[0:dims1[1]]
        packed[...] = pack1(tiles)

    def message(tiles):
        out = tiles[0]
        for i in range(1, dims2[0]):
            out = jnp.where(lane // dims2[2] == i, tiles[i], out)
        return out

    def slot(kind, x, y, z):
        return slots.at[kind, x, z, pl.ds(dims2[1] * y, dims2[1])]

    def gather_start(kind, value):
        tile[kind] = value
        src = tile.at[kind, pl.ds(0, dims2[1])]

        def go(step, unused):
            pltpu.make_async_remote_copy(
                src_ref=src, dst_ref=slot(kind, *pos), send_sem=gsem.at[kind], recv_sem=gsem.at[kind],
                device_id=coords((me + step) % count), device_id_type=MESH,
            ).start()
            return unused
        lax.fori_loop(1, count, go, 0)
        pltpu.make_async_copy(src, slot(kind, *pos), gsem.at[kind]).start()

    def gather_finish(kind, outside):
        part = pad.at[pl.ds(0, dims2[1] * (2 * count - 1))]
        pltpu.make_async_copy(part, part, gsem.at[kind]).wait()
        z = dims2[2]
        per = LANES // z
        spot = iota((whole2[1], LANES), 1)
        planes = []
        for x in range(nx):
            for i in range(dims2[0]):
                columns = []
                for first in range(0, width2 // z, per):
                    total = None
                    for g in range(min(per, nz - first)):
                        shift = (z * (g - i)) % LANES
                        part = slots[kind, x, first + g]
                        part = pltpu.roll(part, shift, 1) if shift else part
                        total = part if total is None else jnp.where(spot // z == g, part, total)
                    columns.append(total)
                planes.append(columns[0] if len(columns) == 1 else jnp.concatenate(columns, 1))
        v = jnp.concatenate(planes, 0)
        if whole2[2] < width2:
            v = jnp.where(iota(v.shape, 1) < whole2[2], v, outside)
        return v

    for load in loads:
        load.wait()
    for k in range(2):
        scb[k] = pack0([e0[k, H0 + t, 0:TILE, 0:LANES] for t in range(dims0[0])])
    pl.semaphore_wait(barrier, count - 1)

    launch(CB)
    tiles = restrict([e0[0, H0 + t, 0:TILE, 0:LANES] for t in range(dims0[0])], dims0[2], dims0[1])
    post1(c1, s1.at[0], tiles)
    launch(C1)
    gather_start(0, message(restrict(tiles, dims1[2], dims1[1])))

    level0 = Level(refs0, dims0, H0, 2 * LANES, pos, sizes, 1.0)
    level1 = Level(refs1, dims1, H1, LANES, pos, sizes, 0.25)

    settle(CB)
    for k in range(2):
        def put(p, half, value):
            e0[k, p, half * TILE:(half + 1) * TILE, LANES:2 * LANES] = value
        unpack0(zcb, k, put)
    level0.coefs(lambda p: e0[0, p])
    b0 = lambda p: e0[1, p]
    level0.before(b0)
    r0 = [e0[1, p, 0:TILE, 0:LANES] - level0.own_op(level0.aux, p) for p in level0.planes(0)]
    tiles = restrict(r0, dims0[2], dims0[1])
    post1(b1, s1.at[1], tiles)
    launch(B1)

    tiles = [level0.aux[p, 0:TILE, 0:LANES] for p in level0.planes(0)]
    for p, v in zip(level0.planes(0), tiles):
        x0[p, 0:TILE, 0:LANES] = v
    sx0[...] = pack0(tiles)
    launch(X0)
    settle(C1)

    def put_c1(p, rows, value):
        c1m[p, rows, :] = value
    unpack1(z1.at[0], c1, put_c1)
    level1.coefs(lambda p: c1m[p])

    settle(B1)

    def put_b1(p, rows, value):
        b1m[p, rows, :] = value
    unpack1(z1.at[1], b1, put_b1)
    b1_of = lambda p: b1m[p]
    level1.before(b1_of)
    r1 = [b1m[p, 0:TILE, :] - level1.own_op(level1.aux, p) for p in level1.planes(0)]
    gather_start(1, message(restrict(r1, dims1[2], dims1[1])))
    tiles = [level1.aux[p, 0:TILE, :] for p in level1.planes(0)]
    tiles = [jnp.where(lane < dims1[2], v, pltpu.roll(v, dims1[2], 1)) for v in tiles]
    tiles = [jnp.where(sub < dims1[1], v, pltpu.roll(v, dims1[1], 0)) for v in tiles]
    post1(x1, s1.at[2], tiles)
    launch(X1)

    y2, z2 = whole2[1], whole2[2]
    shape2 = (whole2[0] * y2, width2)
    shape3 = (shape2[0] // 2, width2)

    def pairs(v):
        return [v[n * y2:(n + 1) * y2] for n in range(v.shape[0] // y2)]

    def restrict2(v):
        planes = pairs(v)
        s = jnp.concatenate([a + b for a, b in zip(planes[0::2], planes[1::2])], 0)
        s = s + pltpu.roll(s, width2 - 1, 1)
        return (s + pltpu.roll(s, s.shape[0] - 1, 0)) * 0.125

    def prolong3(v):
        v = jnp.where((iota(shape3, 0) % 2 == 0) & (iota(shape3, 1) % 2 == 0), v, 0.0)
        v = v + pltpu.roll(v, 1, 1)
        v = v + pltpu.roll(v, 1, 0)
        return jnp.concatenate([part for part in pairs(v) for unused in range(2)], 0)

    c2 = gather_finish(0, 1.0)
    level2 = Flat(refs2, y2, z2, 1, 0.25 ** 2)
    level2.coefs(c2)
    level3 = Flat(refs3, y2, z2, 2, 0.25 ** 3)
    level3.coefs(restrict2(c2))

    settle(X0)

    def put_x0(p, half, value):
        x0[p, half * TILE:(half + 1) * TILE, LANES:2 * LANES] = value
    unpack0(zx0, None, put_x0)
    settle(X1)

    def put_x1(p, rows, value):
        x1s[p, rows, :] = value
    unpack1(z1.at[2], x1, put_x1)

    b2 = gather_finish(1, 0.0)
    x2 = chebyshev(None, b2, 2, 0.3, 2.0, level2)
    b3 = restrict2(b2 - level2.op(x2))
    x3 = chebyshev(None, b3, COARSE_DEGREE, 0.05, 2.0, level3)
    x2 = chebyshev(x2 + prolong3(x3), b2, 2, 0.3, 2.0, level2)
    x2s[...] = x2

    quarter = LANES // 4
    first_lane, first_row = pos[2] * dims2[2], pos[1] * dims2[1]
    lanes = (first_lane + width2 + jnp.where(lane < 3 * quarter, lane // 2, lane // 2 - 2 * quarter)) % width2
    rows = [sub // 2 + 4 * half for half in range(2)]
    rows = [(first_row + y2 + jnp.where(r < 6, r, r - TILE)) % y2 for r in rows]
    low = ((first_row + y2 - 2) % y2) // TILE, ((first_lane + width2 - quarter // 2) % width2) // LANES
    high = ((first_row + 5) % y2) // TILE, ((first_lane + quarter + quarter // 2 - 1) % width2) // LANES
    window = range(-H1 // 2, (dims1[0] + H1) // 2)
    spread = []
    for i in window:
        plane = jnp.clip(pos[0] * dims2[0] + i, 0, whole2[0] - 1)

        def wide(row_tile):
            at = pl.ds(pl.multiple_of(plane * y2 + row_tile * TILE, TILE), TILE)
            if width2 == LANES:
                return jnp.take_along_axis(x2s[at, :], lanes, axis=1)
            parts = [x2s[at, pl.ds(pl.multiple_of(t * LANES, LANES), LANES)] for t in (low[1], high[1])]
            parts = [jnp.take_along_axis(v, lanes % LANES, axis=1) for v in parts]
            return jnp.where(lanes // LANES == low[1], *parts)
        if y2 == TILE:
            v = wide(0)
            spread.append([jnp.take_along_axis(v, r, axis=0) for r in rows])
        else:
            v, w = wide(low[0]), wide(high[0])
            spread.append([
                jnp.where(r // TILE == low[0], *(jnp.take_along_axis(u, r % TILE, axis=0) for u in (v, w))) for r in rows])
    for i, halves in zip(window, spread):
        for half, part in enumerate(halves):
            rows = slice(half * TILE, (half + 1) * TILE)
            for p in (2 * i + H1, 2 * i + H1 + 1):
                x1s[p, rows, :] = x1s[p, rows, :] + part
    level1.after(x1s, b1_of, b1, 2)

    window = range(-2, dims1[0] + 2)
    for group in range(0, len(window), 4):
        results = []
        for i in window[group:group + 4]:
            first, second = b1[H1 + i, 0:TILE, :], b1[H1 + i, TILE:2 * TILE, :]
            second = jnp.where(sub < 6, first, second)
            for half, part in enumerate((first, second)):
                part = jnp.take_along_axis(part, 4 * half + sub // 2, axis=0)
                for side in range(2):
                    e = jnp.take_along_axis(part, (LANES // 2) * side + lane // 2, axis=1)
                    at = (slice(half * TILE, (half + 1) * TILE), slice(side * LANES, (side + 1) * LANES))
                    for p in (2 * i + H0, 2 * i + H0 + 1):
                        if max(0, H0 - p, p - (H0 + dims0[0] - 1)) + half + side <= H0:
                            results.append(((p,) + at, x0[(p,) + at] + e))
        for at, v in results:
            x0[at] = v
    level0.after(x0, b0, x0, 1)
    for t, p in enumerate(level0.planes(0)):
        p_ref[t] = x0[p, 0:TILE, 0:LANES]
        q_ref[t] = e0[1, p, 0:TILE, 0:LANES] - level0.own_op(x0, p)


def finish(p_ref, q_ref, p_out, q_out):
    p_out[...] = p_ref[...]
    q_out[...] = q_ref[...]


def solution(mesh):
    sizes = tuple(mesh.shape[a] for a in AXES)
    count = sizes[0] * sizes[1] * sizes[2]

    def per_device(b, c):
        dims0 = b.shape
        dims1 = tuple(d // 2 for d in dims0)
        dims2 = tuple(d // 2 for d in dims1)
        assert dims0[1:] == (TILE, LANES) and dims2[0] * dims2[2] == LANES and 8 * dims0[0] == LANES
        whole2 = tuple(d * n for d, n in zip(dims2, sizes))
        assert whole2[1] % TILE == 0
        width2 = -(-whole2[2] // LANES) * LANES
        planes0, planes1 = dims0[0] + 2 * H0, dims1[0] + 2 * H1
        wide = pltpu.VMEM((planes0, 2 * TILE, 2 * LANES), F32)
        slim = pltpu.VMEM((planes1, 2 * TILE, LANES), F32)
        flat2 = pltpu.VMEM((whole2[0] * whole2[1], width2), F32)
        flat3 = pltpu.VMEM((whole2[0] // 2 * whole2[1], width2), F32)
        spot = (TILE, LANES)
        scratch = [
            pltpu.VMEM((2, planes0, 2 * TILE, 2 * LANES), F32), wide,
            pltpu.VMEM((2, 3, 3, 2) + spot, F32), pltpu.VMEM((2, 3, 3) + spot, F32),
            pltpu.VMEM((2,) + spot, F32), pltpu.VMEM(spot, F32),
            slim, slim, slim, pltpu.VMEM((3, 2, 3, 3) + spot, F32), pltpu.VMEM((3,) + spot, F32),
            slim, slim, slim,
            pltpu.VMEM((2, sizes[0], sizes[2], whole2[1], LANES), F32), pltpu.VMEM((2,) + spot, F32),
            pltpu.VMEM((max(2 * dims2[1] * count, 32 * dims0[0] * TILE), LANES), F32), pltpu.VMEM((whole2[0] * whole2[1], width2), F32),
        ] + [wide] * 7 + [slim] * 7 + [flat2] * 5 + [flat3] * 5 + [
            pltpu.SemaphoreType.DMA((2,)), pltpu.SemaphoreType.DMA((5,)), pltpu.SemaphoreType.DMA((2,)),
        ]
        shape = jax.ShapeDtypeStruct(dims0, F32)
        p, q = pl.pallas_call(
            functools.partial(kernel, sizes, dims0),
            out_shape=(shape, shape),
            in_specs=[pl.BlockSpec(memory_space=pltpu.HBM)] * 2,
            out_specs=(pl.BlockSpec(memory_space=pltpu.VMEM),) * 2,
            scratch_shapes=scratch,
            compiler_params=pltpu.CompilerParams(
                collective_id=0, has_side_effects=True, vmem_limit_bytes=KERNEL_VMEM),
        )(b, c)
        return pl.pallas_call(
            finish,
            out_shape=(shape, shape),
            in_specs=[pl.BlockSpec(memory_space=pltpu.VMEM)] * 2,
            out_specs=(pl.BlockSpec(memory_space=pltpu.VMEM),) * 2,
            compiler_params=pltpu.CompilerParams(vmem_limit_bytes=2 << 20),
        )(p, q)

    spec = P(*AXES)
    return jax.shard_map(per_device, mesh=mesh, in_specs=(spec, spec), out_specs=(spec, spec), check_vma=False)
```

```python
import functools
import itertools
import math

import jax
import jax.numpy as jnp
from jax import lax
from jax.experimental import pallas as pl
from jax.experimental.pallas import tpu as pltpu
from jax.sharding import PartitionSpec as P

COARSE_DEGREE = 6
AXES = ("gx", "gy", "gz")
LANES = 128
TILE = 8
H0 = 3
H1 = 4
MESH = pl.DeviceIdType.MESH
F32 = jnp.float32
FACES = ((0, 1), (0, -1), (1, 0), (-1, 0), (1, 1), (1, -1), (-1, 1), (-1, -1))
DIRS = tuple((dx, dy, 0) for dx, dy in FACES) + tuple(
    (dx, dy, dz) for dz in (1, -1) for dx, dy in ((0, 0),) + FACES
)
KERNEL_VMEM = 55088 << 10
CB, C1, B1, X0, X1 = range(5)


def iota(shape, dim):
    return lax.broadcasted_iota(jnp.int32, shape, dim)


def invert(v):
    r = pl.reciprocal(v, approx=True)
    return r * (2.0 - v * r)


def factors(lower, upper):
    theta = (upper + lower) / 2.0
    delta = (upper - lower) / 2.0
    sigma = theta / delta
    rho = 1.0 / sigma
    rho_next = 1.0 / (2.0 * sigma - rho)
    return 1.0 / theta, rho_next * rho, 2.0 * rho_next / delta


def chebyshev(start, source, steps, lower, upper, level):
    op_of, inv = level.op, level.inv()
    theta = (upper + lower) / 2.0
    delta = (upper - lower) / 2.0
    sigma = theta / delta
    rho_now = 1.0 / sigma
    if start is None:
        update = source * inv * (1.0 / theta)
        field = update
    else:
        remain = source - op_of(start)
        update = remain * inv * (1.0 / theta)
        field = start + update
    for index in range(steps - 1):
        rho_next = 1.0 / (2.0 * sigma - rho_now)
        remain = source - op_of(field)
        update = rho_next * rho_now * update + (2.0 * rho_next / delta) * (remain * inv)
        field = field + update
        rho_now = rho_next
    return field


class Flat:
    def __init__(self, refs, rows, lanes, step, scale, fold):
        self.refs, self.rows, self.lanes, self.step, self.scale, self.fold = refs, rows, lanes, step, scale, fold

    def ahead(self, v, axis):
        if axis == 2:
            return pltpu.roll(v, v.shape[1] - self.step, 1)
        if axis == 1:
            return pltpu.roll(v, v.shape[0] - self.step, 0)
        end = v[:self.rows]
        if self.fold == 2:
            end = pltpu.roll(end, self.lanes, 1)
        return jnp.concatenate([v[self.rows:], end], 0)

    def behind(self, v, axis):
        if axis == 2:
            return pltpu.roll(v, self.step, 1)
        if axis == 1:
            return pltpu.roll(v, self.step, 0)
        end = v[v.shape[0] - self.rows:]
        if self.fold == 2:
            end = pltpu.roll(end, self.lanes, 1)
        return jnp.concatenate([end, v[:v.shape[0] - self.rows]], 0)

    def coefs(self, c):
        n = c.shape[0] // self.rows
        row, lane = iota(c.shape, 0), iota(c.shape, 1)
        plane = row // self.rows
        if self.fold == 2:
            plane, lane = plane + jnp.where(lane < self.lanes, 0, n), lane % self.lanes
        spots = ((plane, 1, n * self.fold), (row % self.rows, self.step, self.rows), (lane, self.step, self.lanes))
        half = invert(c * (2.0 * self.scale))
        total = None
        for axis, (spot, step, end) in enumerate(spots):
            link = jnp.where(spot >= end - step, 0.0, invert(half + self.ahead(half, axis)))
            self.refs[axis][...] = link
            around = jnp.where(spot < step, 1.0, 0.0) + jnp.where(spot >= end - step, 1.0, 0.0)
            part = link + self.behind(link, axis) + c * (around * self.scale)
            total = part if total is None else total + part
        self.refs[3][...] = total
        self.refs[4][...] = invert(total)

    def inv(self):
        return self.refs[4][...]

    def op(self, v):
        out = self.refs[3][...] * v
        for axis in range(3):
            link = self.refs[axis][...]
            out = out - (link * self.ahead(v, axis) + self.behind(link * v, axis))
        return out


class Level:
    def __init__(self, refs, dims, halo, width, pos, sizes, scale):
        self.lx, self.ly, self.lz, self.diag, self.inv, self.tmp, self.aux = refs
        self.dims, self.halo, self.width, self.scale = dims, halo, width, scale
        shape = (2 * TILE, width)
        row, lane = iota(shape, 0), iota(shape, 1)

        def inner(axis):
            low = jnp.where(pos[axis] > 0, 1.0, 0.0).astype(F32)
            high = jnp.where(pos[axis] < sizes[axis] - 1, 1.0, 0.0).astype(F32)
            return low, high

        self.xlow, self.xhigh = inner(0)
        self.ymask = self.zmask = None
        outer = None
        masks = []
        for index, axis in ((row, 1), (lane, 2)):
            low, high = inner(axis)
            last = dims[axis] - 1
            end = shape[axis - 1] - 1
            masks.append(jnp.where(index == end, low, jnp.where(index == last, high, 1.0)))
            part = jnp.where(index == 0, 1.0 - low, jnp.where(index == last, 1.0 - high, 0.0))
            outer = part if outer is None else outer + part
        self.ymask, self.zmask = masks
        self.outer = outer

    def planes(self, reach):
        return range(self.halo - reach, self.halo + self.dims[0] + reach)

    def put(self, ref, p, v, budget, kind=""):
        own, row_side = slice(0, TILE), slice(TILE, 2 * TILE)
        lanes = slice(0, LANES)
        if self.width == LANES or budget >= 2 or (budget == 1 and kind in ("y", "z")):
            ref[p] = v
        elif kind == "y":
            ref[p, :, lanes] = v[:, lanes]
        elif budget == 1:
            ref[p, own, :] = v[own, :]
            ref[p, row_side, lanes] = v[row_side, lanes]
        elif kind == "z":
            ref[p, own, :] = v[own, :]
        else:
            ref[p, own, lanes] = v[own, lanes]

    def each(self, reach, body):
        first, last = self.halo, self.halo + self.dims[0] - 1
        for p in self.planes(reach):
            for ref, q, v, *kind in body(p):
                near = p + 1 if kind == ["x"] and p < first else p
                self.put(ref, q, v, reach - max(0, first - near, near - last), *kind)

    def back(self, v, dim):
        n = v.shape[dim]
        return pltpu.roll(v, n - 1, dim)

    def coefs(self, c_of):
        first, last = self.halo, self.halo + self.dims[0] - 1
        reach = self.halo - 1
        outer = self.outer * self.scale

        half = {}

        def half_of(p):
            if p not in half:
                half[p] = invert(c_of(p) * (2.0 * self.scale))
            return half[p]

        def face_x(p):
            face = invert(half_of(p) + half_of(p + 1))
            factor = {first - 1: self.xlow, last: self.xhigh}.get(p)
            return face if factor is None else face * factor

        def others(p):
            h = half_of(p)
            ly = invert(h + self.back(h, 0)) * self.ymask
            lz = invert(h + self.back(h, 1)) * self.zmask
            face = face_x(p)
            total = (face + faces.pop()) + (ly + pltpu.roll(ly, 1, 0)) + (lz + pltpu.roll(lz, 1, 1))
            faces.append(face)
            around = outer
            if p in (first, last):
                around = around + (1.0 - (self.xlow if p == first else self.xhigh)) * self.scale
            total = total + c_of(p) * around
            return (self.lx, p, face, "x"), (self.ly, p, ly, "y"), (self.lz, p, lz, "z"), (self.diag, p, total), (self.inv, p, invert(total))

        faces = [face_x(first - reach - 1)]
        self.put(self.lx, first - reach - 1, faces[0], 0)
        self.each(reach, others)

    def op(self, v, p):
        here = v[p]
        ly, lz = self.ly[p], self.lz[p]
        x = self.lx[p] * v[p + 1] + self.lx[p - 1] * v[p - 1]
        y = ly * self.back(here, 0) + pltpu.roll(ly * here, 1, 0)
        z = lz * self.back(here, 1) + pltpu.roll(lz * here, 1, 1)
        return self.diag[p] * here - x - (y + z)

    def own_op(self, v, p):
        own = (slice(0, TILE), slice(0, LANES))
        here = v[p, :, 0:LANES]
        wide = v[p, 0:TILE, :]
        ly, lz = self.ly[p, :, 0:LANES], self.lz[p, 0:TILE, :]
        x = self.lx[p, 0:TILE, 0:LANES] * v[p + 1, 0:TILE, 0:LANES] + self.lx[p - 1, 0:TILE, 0:LANES] * v[p - 1, 0:TILE, 0:LANES]
        y = ly * self.back(here, 0) + pltpu.roll(ly * here, 1, 0)
        z = lz * self.back(wide, 1) + pltpu.roll(lz * wide, 1, 1)
        return self.diag[p, 0:TILE, 0:LANES] * here[own] - x - (y[own] + z[own])

    def before(self, b_of):
        first, mix, gain = factors(0.3, 2.0)

        def one(p):
            return ((self.tmp, p, b_of(p) * self.inv[p] * first),)

        def two(p):
            d = self.tmp[p]
            return ((self.aux, p, d + (mix * d + gain * ((b_of(p) - self.op(self.tmp, p)) * self.inv[p]))),)
        self.each(2, one)
        self.each(1, two)

    def after(self, start, b_of, out, reach):
        first, mix, gain = factors(0.3, 2.0)

        def one(p):
            update = (b_of(p) - self.op(start, p)) * self.inv[p] * first
            return (self.aux, p, update), (self.tmp, p, start[p] + update)

        def two(p):
            update = mix * self.aux[p] + gain * ((b_of(p) - self.op(self.tmp, p)) * self.inv[p])
            return ((out, p, self.tmp[p] + update),)
        self.each(reach + 1, one)
        self.each(reach, two)


def restrict(tiles, lanes, rows):
    out = []
    lane = (2 * iota((TILE, LANES), 1)) % lanes
    row = (2 * iota((TILE, LANES), 0)) % rows
    for a, b in zip(tiles[0::2], tiles[1::2]):
        s = a + b
        s = s + pltpu.roll(s, LANES - 1, 1)
        s = (s + pltpu.roll(s, TILE - 1, 0)) * 0.125
        s = jnp.take_along_axis(s, lane, axis=1)
        out.append(jnp.take_along_axis(s, row, axis=0))
    return out


def kernel(sizes, dims0, b_hbm, c_hbm, p_ref, q_ref, *scratch):
    (e0, x0, zcb, zx0, scb, sx0, c1, b1, x1, z1, s1, c1m, b1m, x1s, slots, tile, pad, x2s) = scratch[:18]
    refs0, refs1, refs2, refs3 = scratch[18:25], scratch[25:32], scratch[32:37], scratch[37:42]
    isem, xsem, gsem = scratch[42:]
    pos = tuple(lax.axis_index(a) for a in AXES)
    dims1 = tuple(d // 2 for d in dims0)
    dims2 = tuple(d // 2 for d in dims1)
    whole2 = tuple(d * n for d, n in zip(dims2, sizes))
    nx, ny, nz = sizes
    count = nx * ny * nz
    me = (pos[0] * ny + pos[1]) * nz + pos[2]
    width2 = x2s.shape[1]
    fold = 2 if 2 * whole2[2] == width2 and whole2[0] % 4 == 0 else 1
    own0 = pl.ds(H0, dims0[0])

    loads = [
        pltpu.make_async_copy(src, e0.at[k, own0, pl.ds(0, TILE), pl.ds(0, LANES)], isem.at[k])
        for k, src in enumerate((c_hbm, b_hbm))
    ]
    for load in loads:
        load.start()

    def coords(index):
        return (index // (ny * nz), (index // nz) % ny, index % nz)

    barrier = pltpu.get_barrier_semaphore()


    def exists(axis, step):
        if step == 0:
            return None
        return pos[axis] < sizes[axis] - 1 if step > 0 else pos[axis] > 0

    def when(conditions, body):
        conditions = [c for c in conditions if c is not None]
        if not conditions:
            body()
            return
        both = conditions[0]
        for c in conditions[1:]:
            both = both & c
        pl.when(both)(body)

    def each(body):
        for dz in (0, 1, -1):
            def group():
                for n, d in enumerate(DIRS):
                    if d[2] == dz:
                        when([exists(0, d[0]), exists(1, d[1])], functools.partial(body, n))
            when([exists(2, dz)], group)

    def greet_near(n):
        pl.semaphore_signal(barrier, inc=1, device_id=tuple(p + d for p, d in zip(pos, DIRS[n])), device_id_type=MESH)

    def greet_all(step, unused):
        pl.semaphore_signal(barrier, inc=1, device_id=coords((me + step) % count), device_id_type=MESH)
        return unused

    if max(sizes) <= 4:
        each(greet_near)
        greeted = 1
        for axis, n in enumerate(sizes):
            greeted = greeted * (1 + jnp.where(pos[axis] > 0, 1, 0) + jnp.where(pos[axis] < n - 1, 1, 0))
        greeted = greeted - 1
    else:
        lax.fori_loop(1, count, greet_all, 0)
        greeted = count - 1

    def cut(step, n, halo, wrap):
        if step == 0:
            return (0, 0, n)
        if step > 0:
            return (n - halo, wrap - halo, halo)
        return (0, n, halo)

    def ends(xid, n):
        dx, dy, dz = DIRS[n]
        if dz:
            packed = {CB: scb, X0: sx0}.get(xid)
            arrived = {CB: zcb, X0: zx0}.get(xid)
            if packed is None:
                at = (C1, B1, X1).index(xid)
                packed, arrived = s1.at[at], z1.at[at]
            return packed, arrived.at[0 if dz > 0 else 1, 1 - dx, 1 - dy]
        low, halo = (xid in (CB, X0)), (H0 if xid in (CB, X0) else H1)
        dims = dims0 if low else dims1
        a, b, planes = cut(dx, dims[0], halo, 0)
        r, s, rows = cut(dy, dims[1], min(halo, dims[1]), 2 * TILE)
        if low:
            ref = e0 if xid == CB else x0
            lead = (slice(None),) if xid == CB else ()
            lanes = (pl.ds(0, LANES),)
        else:
            ref, lead, lanes = {C1: c1, B1: b1, X1: x1}[xid], (), (slice(None),)
        src = ref.at[lead + (pl.ds(halo + a, planes), pl.ds(r, rows)) + lanes]
        dst = ref.at[lead + (pl.ds(halo + b, planes), pl.ds(s, rows)) + lanes]
        return src, dst

    def remote(xid, n):
        src, dst = ends(xid, n)
        return pltpu.make_async_remote_copy(
            src_ref=src, dst_ref=dst, send_sem=xsem.at[xid], recv_sem=xsem.at[xid],
            device_id=tuple(p + d for p, d in zip(pos, DIRS[n])), device_id_type=MESH,
        )

    def launch(xid):
        each(lambda n: remote(xid, n).start())

    def fill(xid):
        def one(n):
            dst = ends(xid, n)[1]
            if xid == CB:
                dst[0] = jnp.ones(dst.shape[1:], F32)
                dst[1] = jnp.zeros(dst.shape[1:], F32)
            else:
                dst[...] = jnp.full(dst.shape, 1.0 if xid == C1 else 0.0, F32)
        for n, d in enumerate(DIRS):
            sources = [exists(axis, -step) for axis, step in enumerate(d) if step]
            present = functools.reduce(jnp.logical_and, sources)
            pl.when(jnp.logical_not(present))(functools.partial(one, n))

    def settle(xid):
        kinds = []
        for axis, n in enumerate(sizes):
            inside = (pos[axis] > 0) & (pos[axis] < n - 1)
            kinds.append([(0, None)] if n == 1 else [(1, None)] if n == 2 else [(1, jnp.logical_not(inside)), (2, inside)])
        for case in itertools.product(*kinds):
            rows = 0
            for n, d in enumerate(DIRS):
                if min(d) >= 0:
                    shape = ends(xid, n)[0].shape
                    rows += math.prod(shape[:-1]) * math.prod(k for (k, unused), step in zip(case, d) if step)
            part = pad.at[pl.ds(0, 2 * rows)]
            when([c for unused, c in case], pltpu.make_async_copy(part, part, xsem.at[xid]).wait)

    lane, sub = iota((TILE, LANES), 1), iota((TILE, LANES), 0)

    def pack0(tiles):
        out = tiles[0]
        for t in range(1, len(tiles)):
            part = pltpu.roll(tiles[t], 8 * t, 1)
            out = jnp.where(((lane - (8 * t - 4)) % LANES) < 8, part, out)
        return out

    def pack1(tiles):
        out = tiles[0]
        for t in range(1, len(tiles)):
            part = pltpu.roll(tiles[t], 8 * t, 1)
            place = (lane - 8 * t) % LANES
            out = jnp.where((place < 4) | ((place >= 60) & (place < 64)), part, out)
        return out

    def both_sides(arrived, dx, dy, k=None):
        at = (dx + 1, dy + 1) + (() if k is None else (k,))
        return jnp.where(lane % 8 < 4, arrived[(1,) + at], arrived[(0,) + at])

    def group_planes(n, halo):
        return ((0, [(t, halo + t) for t in range(n)]),
                (-1, [(t, halo + t - n) for t in range(n - halo, n)]),
                (1, [(t, halo + n + t) for t in range(halo)]))

    def unpack0(arrived, k, store):
        for dx, pairs in group_planes(dims0[0], H0):
            first = both_sides(arrived, dx, 0, k)
            second = jnp.where(sub < 4, both_sides(arrived, dx, 1, k), both_sides(arrived, dx, -1, k))
            for t, p in pairs:
                shift = (-8 * t) % LANES
                beyond = max(0, H0 - p, p - (H0 + dims0[0] - 1))
                if beyond < H0:
                    store(p, 0, pltpu.roll(first, shift, 1) if shift else first)
                if beyond < H0 - 1:
                    store(p, 1, pltpu.roll(second, shift, 1) if shift else second)

    def unpack1(arrived, field, store):
        z = dims1[2]
        for dx, pairs in group_planes(dims1[0], H1):
            first = jnp.where(sub < 4, both_sides(arrived, dx, 0), both_sides(arrived, dx, 1))
            second = both_sides(arrived, dx, -1)
            for t, p in pairs:
                shift = (z - 8 * t) % LANES
                for half, part in enumerate((first, second)):
                    rows = slice(half * TILE, (half + 1) * TILE)
                    part = pltpu.roll(part, shift, 1) if shift else part
                    store(p, rows, jnp.where(lane < z, field[p, rows, :], part))

    def post1(field, packed, tiles):
        for i, v in enumerate(tiles):
            field[H1 + i, 0:dims1[1], :] = v[0:dims1[1]]
        packed[...] = pack1(tiles)

    def message(tiles):
        out = tiles[0]
        for i in range(1, dims2[0]):
            out = jnp.where(lane // dims2[2] == i, tiles[i], out)
        return out

    def gather_start():
        src = tile.at[:, pl.ds(0, dims2[1])]
        dst = slots.at[:, pos[0], pos[2], pl.ds(dims2[1] * pos[1], dims2[1])]

        def go(step, unused):
            pltpu.make_async_remote_copy(
                src_ref=src, dst_ref=dst, send_sem=gsem, recv_sem=gsem,
                device_id=coords((me + step) % count), device_id_type=MESH,
            ).start()
            return unused
        lax.fori_loop(1, count, go, 0)
        pltpu.make_async_copy(src, dst, gsem).start()

    def gather_wait():
        part = pad.at[pl.ds(0, 2 * dims2[1] * (2 * count - 1))]
        pltpu.make_async_copy(part, part, gsem).wait()

    def gathered(kind, outside):
        z = dims2[2]
        per = LANES // z
        spot = iota((whole2[1], LANES), 1)
        planes = []
        for n in range(whole2[0] // fold):
            columns = []
            for first in range(0, width2 // z, per):
                total = None
                for g in range(min(per, fold * nz - first)):
                    plane = n + (first + g) // nz * (whole2[0] // fold)
                    x, i = divmod(plane, dims2[0])
                    shift = (z * (g - i)) % LANES
                    part = slots[kind, x, (first + g) % nz]
                    part = pltpu.roll(part, shift, 1) if shift else part
                    total = part if total is None else jnp.where(spot // z == g, part, total)
                columns.append(total)
            planes.append(columns[0] if len(columns) == 1 else jnp.concatenate(columns, 1))
        v = jnp.concatenate(planes, 0)
        if fold * whole2[2] < width2:
            v = jnp.where(iota(v.shape, 1) < fold * whole2[2], v, outside)
        return v

    for load in loads:
        load.wait()
    for k in range(2):
        scb[k] = pack0([e0[k, H0 + t, 0:TILE, 0:LANES] for t in range(dims0[0])])
    pl.semaphore_wait(barrier, greeted)

    launch(CB)
    for k, value in ((0, 1.0), (1, 0.0)):
        rows = slice(TILE + H0, 2 * TILE - H0)
        e0[k, :, rows, 0:LANES] = jnp.full((e0.shape[1], rows.stop - rows.start, LANES), value, F32)
    fill(CB)
    tiles = restrict([e0[0, H0 + t, 0:TILE, 0:LANES] for t in range(dims0[0])], dims0[2], dims0[1])
    post1(c1, s1.at[0], tiles)
    launch(C1)
    tile[0] = message(restrict(tiles, dims1[2], dims1[1]))
    for ref, value in ((c1, 1.0), (b1, 0.0), (x1, 0.0)):
        ref[:, 2 * dims1[1]:3 * dims1[1], :] = jnp.full((ref.shape[0], dims1[1], LANES), value, F32)
    rows = slice(TILE + H0, 2 * TILE - H0)
    x0[:, rows, 0:LANES] = jnp.zeros((x0.shape[0], rows.stop - rows.start, LANES), F32)
    for xid in (C1, B1, X0, X1):
        fill(xid)

    level0 = Level(refs0, dims0, H0, 2 * LANES, pos, sizes, 1.0)
    level1 = Level(refs1, dims1, H1, LANES, pos, sizes, 0.25)

    settle(CB)
    for k in range(2):
        def put(p, half, value):
            e0[k, p, half * TILE:(half + 1) * TILE, LANES:2 * LANES] = value
        unpack0(zcb, k, put)
    level0.coefs(lambda p: e0[0, p])
    b0 = lambda p: e0[1, p]
    level0.before(b0)
    r0 = [e0[1, p, 0:TILE, 0:LANES] - level0.own_op(level0.aux, p) for p in level0.planes(0)]
    tiles = restrict(r0, dims0[2], dims0[1])
    post1(b1, s1.at[1], tiles)
    launch(B1)

    tiles = [level0.aux[p, 0:TILE, 0:LANES] for p in level0.planes(0)]
    for p, v in zip(level0.planes(0), tiles):
        x0[p, 0:TILE, 0:LANES] = v
    sx0[...] = pack0(tiles)
    launch(X0)
    settle(C1)

    def put_c1(p, rows, value):
        c1m[p, rows, :] = value
    unpack1(z1.at[0], c1, put_c1)
    level1.coefs(lambda p: c1m[p])

    settle(B1)

    def put_b1(p, rows, value):
        b1m[p, rows, :] = value
    unpack1(z1.at[1], b1, put_b1)
    b1_of = lambda p: b1m[p]
    level1.before(b1_of)
    r1 = [b1m[p, 0:TILE, :] - level1.own_op(level1.aux, p) for p in level1.planes(0)]
    tile[1] = message(restrict(r1, dims1[2], dims1[1]))
    gather_start()
    tiles = [level1.aux[p, 0:TILE, :] for p in level1.planes(0)]
    tiles = [jnp.where(lane < dims1[2], v, pltpu.roll(v, dims1[2], 1)) for v in tiles]
    tiles = [jnp.where(sub < dims1[1], v, pltpu.roll(v, dims1[1], 0)) for v in tiles]
    post1(x1, s1.at[2], tiles)
    launch(X1)

    y2, z2 = whole2[1], whole2[2]
    shape3 = (whole2[0] * y2 // (2 * fold), width2)

    def pairs(v):
        return [v[n * y2:(n + 1) * y2] for n in range(v.shape[0] // y2)]

    def restrict2(v):
        planes = pairs(v)
        s = jnp.concatenate([a + b for a, b in zip(planes[0::2], planes[1::2])], 0)
        s = s + pltpu.roll(s, width2 - 1, 1)
        return (s + pltpu.roll(s, s.shape[0] - 1, 0)) * 0.125

    def prolong3(v):
        v = jnp.where((iota(shape3, 0) % 2 == 0) & (iota(shape3, 1) % 2 == 0), v, 0.0)
        v = v + pltpu.roll(v, 1, 1)
        v = v + pltpu.roll(v, 1, 0)
        return jnp.concatenate([part for part in pairs(v) for unused in range(2)], 0)

    settle(X0)

    def put_x0(p, half, value):
        x0[p, half * TILE:(half + 1) * TILE, LANES:2 * LANES] = value
    unpack0(zx0, None, put_x0)
    settle(X1)

    def put_x1(p, rows, value):
        x1s[p, rows, :] = value
    unpack1(z1.at[2], x1, put_x1)

    gather_wait()
    c2 = gathered(0, 1.0)
    level2 = Flat(refs2, y2, z2, 1, 0.25 ** 2, fold)
    level2.coefs(c2)
    level3 = Flat(refs3, y2, z2, 2, 0.25 ** 3, fold)
    level3.coefs(restrict2(c2))
    b2 = gathered(1, 0.0)
    x2 = chebyshev(None, b2, 2, 0.3, 2.0, level2)
    b3 = restrict2(b2 - level2.op(x2))
    x3 = chebyshev(None, b3, COARSE_DEGREE, 0.05, 2.0, level3)
    x2 = chebyshev(x2 + prolong3(x3), b2, 2, 0.3, 2.0, level2)
    for k in range(fold):
        x2s[pl.ds(k * x2.shape[0], x2.shape[0]), :] = pltpu.roll(x2, z2, 1) if k else x2

    quarter = LANES // 4
    first_lane, first_row = pos[2] * dims2[2], pos[1] * dims2[1]
    lanes = (first_lane + width2 + jnp.where(lane < 3 * quarter, lane // 2, lane // 2 - 2 * quarter)) % width2
    rows = [sub // 2 + 4 * half for half in range(2)]
    rows = [(first_row + y2 + jnp.where(r < 6, r, r - TILE)) % y2 for r in rows]
    low = ((first_row + y2 - 2) % y2) // TILE, ((first_lane + width2 - quarter // 2) % width2) // LANES
    high = ((first_row + 5) % y2) // TILE, ((first_lane + quarter + quarter // 2 - 1) % width2) // LANES
    window = range(-H1 // 2, (dims1[0] + H1) // 2)
    spread = []
    for i in window:
        plane = jnp.clip(pos[0] * dims2[0] + i, 0, whole2[0] - 1)

        def wide(row_tile):
            at = pl.ds(pl.multiple_of(plane * y2 + row_tile * TILE, TILE), TILE)
            if width2 == LANES:
                return jnp.take_along_axis(x2s[at, :], lanes, axis=1)
            parts = [x2s[at, pl.ds(pl.multiple_of(t * LANES, LANES), LANES)] for t in (low[1], high[1])]
            parts = [jnp.take_along_axis(v, lanes % LANES, axis=1) for v in parts]
            return jnp.where(lanes // LANES == low[1], *parts)
        if y2 == TILE:
            v = wide(0)
            spread.append([jnp.take_along_axis(v, r, axis=0) for r in rows])
        else:
            v, w = wide(low[0]), wide(high[0])
            spread.append([
                jnp.where(r // TILE == low[0], *(jnp.take_along_axis(u, r % TILE, axis=0) for u in (v, w))) for r in rows])
    for i, halves in zip(window, spread):
        for half, part in enumerate(halves):
            rows = slice(half * TILE, (half + 1) * TILE)
            for p in (2 * i + H1, 2 * i + H1 + 1):
                x1s[p, rows, :] = x1s[p, rows, :] + part
    level1.after(x1s, b1_of, b1, 2)

    window = range(-2, dims1[0] + 2)
    for group in range(0, len(window), 4):
        results = []
        for i in window[group:group + 4]:
            first, second = b1[H1 + i, 0:TILE, :], b1[H1 + i, TILE:2 * TILE, :]
            second = jnp.where(sub < 6, first, second)
            for half, part in enumerate((first, second)):
                part = jnp.take_along_axis(part, 4 * half + sub // 2, axis=0)
                for side in range(2):
                    e = jnp.take_along_axis(part, (LANES // 2) * side + lane // 2, axis=1)
                    at = (slice(half * TILE, (half + 1) * TILE), slice(side * LANES, (side + 1) * LANES))
                    for p in (2 * i + H0, 2 * i + H0 + 1):
                        if max(0, H0 - p, p - (H0 + dims0[0] - 1)) + half + side <= H0:
                            results.append(((p,) + at, x0[(p,) + at] + e))
        for at, v in results:
            x0[at] = v
    level0.after(x0, b0, x0, 1)
    for t, p in enumerate(level0.planes(0)):
        p_ref[t] = x0[p, 0:TILE, 0:LANES]
        q_ref[t] = e0[1, p, 0:TILE, 0:LANES] - level0.own_op(x0, p)


def finish(p_ref, q_ref, p_out, q_out):
    p_out[...] = p_ref[...]
    q_out[...] = q_ref[...]


def solution(mesh):
    sizes = tuple(mesh.shape[a] for a in AXES)
    count = sizes[0] * sizes[1] * sizes[2]

    def per_device(b, c):
        dims0 = b.shape
        dims1 = tuple(d // 2 for d in dims0)
        dims2 = tuple(d // 2 for d in dims1)
        assert dims0[1:] == (TILE, LANES) and dims2[0] * dims2[2] == LANES and 8 * dims0[0] == LANES
        whole2 = tuple(d * n for d, n in zip(dims2, sizes))
        assert whole2[1] % TILE == 0
        width2 = -(-whole2[2] // LANES) * LANES
        planes0, planes1 = dims0[0] + 2 * H0, dims1[0] + 2 * H1
        wide = pltpu.VMEM((planes0, 2 * TILE, 2 * LANES), F32)
        slim = pltpu.VMEM((planes1, 2 * TILE, LANES), F32)
        fold = 2 if 2 * whole2[2] == width2 and whole2[0] % 4 == 0 else 1
        flat2 = pltpu.VMEM((whole2[0] // fold * whole2[1], width2), F32)
        flat3 = pltpu.VMEM((whole2[0] // (2 * fold) * whole2[1], width2), F32)
        spot = (TILE, LANES)
        scratch = [
            pltpu.VMEM((2, planes0, 2 * TILE, 2 * LANES), F32), wide,
            pltpu.VMEM((2, 3, 3, 2) + spot, F32), pltpu.VMEM((2, 3, 3) + spot, F32),
            pltpu.VMEM((2,) + spot, F32), pltpu.VMEM(spot, F32),
            slim, slim, slim, pltpu.VMEM((3, 2, 3, 3) + spot, F32), pltpu.VMEM((3,) + spot, F32),
            slim, slim, slim,
            pltpu.VMEM((2, sizes[0], sizes[2], whole2[1], LANES), F32), pltpu.VMEM((2,) + spot, F32),
            pltpu.VMEM((max(4 * dims2[1] * count, 32 * dims0[0] * TILE), LANES), F32), pltpu.VMEM((whole2[0] * whole2[1], width2), F32),
        ] + [wide] * 7 + [slim] * 7 + [flat2] * 5 + [flat3] * 5 + [
            pltpu.SemaphoreType.DMA((2,)), pltpu.SemaphoreType.DMA((5,)), pltpu.SemaphoreType.DMA,
        ]
        shape = jax.ShapeDtypeStruct(dims0, F32)
        p, q = pl.pallas_call(
            functools.partial(kernel, sizes, dims0),
            out_shape=(shape, shape),
            in_specs=[pl.BlockSpec(memory_space=pltpu.HBM)] * 2,
            out_specs=(pl.BlockSpec(memory_space=pltpu.VMEM),) * 2,
            scratch_shapes=scratch,
            compiler_params=pltpu.CompilerParams(
                collective_id=0, has_side_effects=True, vmem_limit_bytes=KERNEL_VMEM),
        )(b, c)
        return pl.pallas_call(
            finish,
            out_shape=(shape, shape),
            in_specs=[pl.BlockSpec(memory_space=pltpu.VMEM)] * 2,
            out_specs=(pl.BlockSpec(memory_space=pltpu.VMEM),) * 2,
            compiler_params=pltpu.CompilerParams(vmem_limit_bytes=2 << 20),
        )(p, q)

    spec = P(*AXES)
    return jax.shard_map(per_device, mesh=mesh, in_specs=(spec, spec), out_specs=(spec, spec), check_vma=False)
```

```python
import functools
import itertools
import math

import jax
import jax.numpy as jnp
from jax import lax
from jax.experimental import pallas as pl
from jax.experimental.pallas import tpu as pltpu
from jax.sharding import PartitionSpec as P

COARSE_DEGREE = 6
AXES = ("gx", "gy", "gz")
LANES = 128
TILE = 8
H0 = 3
H1 = 4
MESH = pl.DeviceIdType.MESH
F32 = jnp.float32
FACES = ((0, 1), (0, -1), (1, 0), (-1, 0), (1, 1), (1, -1), (-1, 1), (-1, -1))
DIRS = tuple((dx, dy, 0) for dx, dy in FACES) + tuple(
    (dx, dy, dz) for dz in (1, -1) for dx, dy in ((0, 0),) + FACES
)
KERNEL_VMEM = 55088 << 10
CB, C1, B1, X0, X1 = range(5)


def iota(shape, dim):
    return lax.broadcasted_iota(jnp.int32, shape, dim)


def invert(v):
    r = pl.reciprocal(v, approx=True)
    return r * (2.0 - v * r)


def factors(lower, upper):
    theta = (upper + lower) / 2.0
    delta = (upper - lower) / 2.0
    sigma = theta / delta
    rho = 1.0 / sigma
    rho_next = 1.0 / (2.0 * sigma - rho)
    return 1.0 / theta, rho_next * rho, 2.0 * rho_next / delta


def chebyshev(start, source, steps, lower, upper, level):
    op_of, inv = level.op, level.inv()
    theta = (upper + lower) / 2.0
    delta = (upper - lower) / 2.0
    sigma = theta / delta
    rho_now = 1.0 / sigma
    if start is None:
        update = source * inv * (1.0 / theta)
        field = update
    else:
        remain = source - op_of(start)
        update = remain * inv * (1.0 / theta)
        field = start + update
    for index in range(steps - 1):
        rho_next = 1.0 / (2.0 * sigma - rho_now)
        remain = source - op_of(field)
        update = rho_next * rho_now * update + (2.0 * rho_next / delta) * (remain * inv)
        field = field + update
        rho_now = rho_next
    return field


class Flat:
    def __init__(self, refs, rows, lanes, step, scale, fold):
        self.refs, self.rows, self.lanes, self.step, self.scale, self.fold = refs, rows, lanes, step, scale, fold

    def ahead(self, v, axis):
        if axis == 2:
            return pltpu.roll(v, v.shape[1] - self.step, 1)
        if axis == 1:
            return pltpu.roll(v, v.shape[0] - self.step, 0)
        end = v[:self.rows]
        if self.fold == 2:
            end = pltpu.roll(end, self.lanes, 1)
        return jnp.concatenate([v[self.rows:], end], 0)

    def behind(self, v, axis):
        if axis == 2:
            return pltpu.roll(v, self.step, 1)
        if axis == 1:
            return pltpu.roll(v, self.step, 0)
        end = v[v.shape[0] - self.rows:]
        if self.fold == 2:
            end = pltpu.roll(end, self.lanes, 1)
        return jnp.concatenate([end, v[:v.shape[0] - self.rows]], 0)

    def coefs(self, c):
        n = c.shape[0] // self.rows
        row, lane = iota(c.shape, 0), iota(c.shape, 1)
        plane = row // self.rows
        if self.fold == 2:
            plane, lane = plane + jnp.where(lane < self.lanes, 0, n), lane % self.lanes
        spots = ((plane, 1, n * self.fold), (row % self.rows, self.step, self.rows), (lane, self.step, self.lanes))
        half = invert(c * (2.0 * self.scale))
        total = None
        for axis, (spot, step, end) in enumerate(spots):
            link = jnp.where(spot >= end - step, 0.0, invert(half + self.ahead(half, axis)))
            self.refs[axis][...] = link
            around = jnp.where(spot < step, 1.0, 0.0) + jnp.where(spot >= end - step, 1.0, 0.0)
            part = link + self.behind(link, axis) + c * (around * self.scale)
            total = part if total is None else total + part
        self.refs[3][...] = total
        self.refs[4][...] = invert(total)

    def inv(self):
        return self.refs[4][...]

    def op(self, v):
        out = self.refs[3][...] * v
        for axis in range(3):
            link = self.refs[axis][...]
            out = out - (link * self.ahead(v, axis) + self.behind(link * v, axis))
        return out


class Level:
    def __init__(self, refs, dims, halo, width, pos, sizes, scale):
        self.lx, self.ly, self.lz, self.diag, self.inv, self.tmp, self.aux = refs
        self.dims, self.halo, self.width, self.scale = dims, halo, width, scale
        shape = (2 * TILE, width)
        row, lane = iota(shape, 0), iota(shape, 1)

        def inner(axis):
            low = jnp.where(pos[axis] > 0, 1.0, 0.0).astype(F32)
            high = jnp.where(pos[axis] < sizes[axis] - 1, 1.0, 0.0).astype(F32)
            return low, high

        self.xlow, self.xhigh = inner(0)
        self.ymask = self.zmask = None
        outer = None
        masks = []
        for index, axis in ((row, 1), (lane, 2)):
            low, high = inner(axis)
            last = dims[axis] - 1
            end = shape[axis - 1] - 1
            masks.append(jnp.where(index == end, low, jnp.where(index == last, high, 1.0)))
            part = jnp.where(index == 0, 1.0 - low, jnp.where(index == last, 1.0 - high, 0.0))
            outer = part if outer is None else outer + part
        self.ymask, self.zmask = masks
        self.outer = outer

    def planes(self, reach):
        return range(self.halo - reach, self.halo + self.dims[0] + reach)

    def put(self, ref, p, v, budget, kind=""):
        own, row_side = slice(0, TILE), slice(TILE, 2 * TILE)
        lanes = slice(0, LANES)
        if self.width == LANES or budget >= 2 or (budget == 1 and kind in ("y", "z")):
            ref[p] = v
        elif kind == "y":
            ref[p, :, lanes] = v[:, lanes]
        elif budget == 1:
            ref[p, own, :] = v[own, :]
            ref[p, row_side, lanes] = v[row_side, lanes]
        elif kind == "z":
            ref[p, own, :] = v[own, :]
        else:
            ref[p, own, lanes] = v[own, lanes]

    def each(self, reach, body):
        first, last = self.halo, self.halo + self.dims[0] - 1
        for p in self.planes(reach):
            for ref, q, v, *kind in body(p):
                near = p + 1 if kind == ["x"] and p < first else p
                self.put(ref, q, v, reach - max(0, first - near, near - last), *kind)

    def back(self, v, dim):
        n = v.shape[dim]
        return pltpu.roll(v, n - 1, dim)

    def coefs(self, c_of):
        first, last = self.halo, self.halo + self.dims[0] - 1
        reach = self.halo - 1
        outer = self.outer * self.scale

        half = {}

        def half_of(p):
            if p not in half:
                half[p] = invert(c_of(p) * (2.0 * self.scale))
            return half[p]

        def face_x(p):
            face = invert(half_of(p) + half_of(p + 1))
            factor = {first - 1: self.xlow, last: self.xhigh}.get(p)
            return face if factor is None else face * factor

        def others(p):
            h = half_of(p)
            ly = invert(h + self.back(h, 0)) * self.ymask
            lz = invert(h + self.back(h, 1)) * self.zmask
            face = face_x(p)
            total = (face + faces.pop()) + (ly + pltpu.roll(ly, 1, 0)) + (lz + pltpu.roll(lz, 1, 1))
            faces.append(face)
            around = outer
            if p in (first, last):
                around = around + (1.0 - (self.xlow if p == first else self.xhigh)) * self.scale
            total = total + c_of(p) * around
            return (self.lx, p, face, "x"), (self.ly, p, ly, "y"), (self.lz, p, lz, "z"), (self.diag, p, total), (self.inv, p, invert(total))

        faces = [face_x(first - reach - 1)]
        self.put(self.lx, first - reach - 1, faces[0], 0)
        self.each(reach, others)

    def op(self, v, p):
        here = v[p]
        ly, lz = self.ly[p], self.lz[p]
        x = self.lx[p] * v[p + 1] + self.lx[p - 1] * v[p - 1]
        y = ly * self.back(here, 0) + pltpu.roll(ly * here, 1, 0)
        z = lz * self.back(here, 1) + pltpu.roll(lz * here, 1, 1)
        return self.diag[p] * here - x - (y + z)

    def own_op(self, v, p):
        own = (slice(0, TILE), slice(0, LANES))
        here = v[p, :, 0:LANES]
        wide = v[p, 0:TILE, :]
        ly, lz = self.ly[p, :, 0:LANES], self.lz[p, 0:TILE, :]
        x = self.lx[p, 0:TILE, 0:LANES] * v[p + 1, 0:TILE, 0:LANES] + self.lx[p - 1, 0:TILE, 0:LANES] * v[p - 1, 0:TILE, 0:LANES]
        y = ly * self.back(here, 0) + pltpu.roll(ly * here, 1, 0)
        z = lz * self.back(wide, 1) + pltpu.roll(lz * wide, 1, 1)
        return self.diag[p, 0:TILE, 0:LANES] * here[own] - x - (y[own] + z[own])

    def before(self, b_of):
        first, mix, gain = factors(0.3, 2.0)

        def one(p):
            return ((self.tmp, p, b_of(p) * self.inv[p] * first),)

        def two(p):
            d = self.tmp[p]
            return ((self.aux, p, d + (mix * d + gain * ((b_of(p) - self.op(self.tmp, p)) * self.inv[p]))),)
        self.each(2, one)
        self.each(1, two)

    def after(self, start, b_of, out, reach):
        first, mix, gain = factors(0.3, 2.0)

        def one(p):
            update = (b_of(p) - self.op(start, p)) * self.inv[p] * first
            return (self.aux, p, update), (self.tmp, p, start[p] + update)

        def two(p):
            update = mix * self.aux[p] + gain * ((b_of(p) - self.op(self.tmp, p)) * self.inv[p])
            return ((out, p, self.tmp[p] + update),)
        self.each(reach + 1, one)
        self.each(reach, two)


def restrict(tiles, lanes, rows):
    out = []
    lane = (2 * iota((TILE, LANES), 1)) % lanes
    row = (2 * iota((TILE, LANES), 0)) % rows
    for a, b in zip(tiles[0::2], tiles[1::2]):
        s = a + b
        s = s + pltpu.roll(s, LANES - 1, 1)
        s = (s + pltpu.roll(s, TILE - 1, 0)) * 0.125
        s = jnp.take_along_axis(s, lane, axis=1)
        out.append(jnp.take_along_axis(s, row, axis=0))
    return out


def kernel(sizes, dims0, b_hbm, c_hbm, p_ref, q_ref, *scratch):
    (e0, x0, zcb, zx0, scb, sx0, c1, b1, x1, z1, s1, c1m, b1m, x1s, slots, tile, pad, x2s) = scratch[:18]
    refs0, refs1, refs2, refs3 = scratch[18:25], scratch[25:32], scratch[32:37], scratch[37:42]
    isem, xsem, gsem = scratch[42:]
    pos = tuple(lax.axis_index(a) for a in AXES)
    dims1 = tuple(d // 2 for d in dims0)
    dims2 = tuple(d // 2 for d in dims1)
    whole2 = tuple(d * n for d, n in zip(dims2, sizes))
    nx, ny, nz = sizes
    count = nx * ny * nz
    me = (pos[0] * ny + pos[1]) * nz + pos[2]
    width2 = x2s.shape[1]
    fold = 2 if 2 * whole2[2] == width2 and whole2[0] % 4 == 0 else 1
    own0 = pl.ds(H0, dims0[0])

    loads = [
        pltpu.make_async_copy(src, e0.at[k, own0, pl.ds(0, TILE), pl.ds(0, LANES)], isem.at[k])
        for k, src in enumerate((c_hbm, b_hbm))
    ]
    for load in loads:
        load.start()

    def coords(index):
        return (index // (ny * nz), (index // nz) % ny, index % nz)

    barrier = pltpu.get_barrier_semaphore()


    def exists(axis, step):
        if step == 0:
            return None
        return pos[axis] < sizes[axis] - 1 if step > 0 else pos[axis] > 0

    def when(conditions, body):
        conditions = [c for c in conditions if c is not None]
        if not conditions:
            body()
            return
        both = conditions[0]
        for c in conditions[1:]:
            both = both & c
        pl.when(both)(body)

    def each(body):
        for dz in (0, 1, -1):
            def group():
                for n, d in enumerate(DIRS):
                    if d[2] == dz:
                        when([exists(0, d[0]), exists(1, d[1])], functools.partial(body, n))
            when([exists(2, dz)], group)

    def greet_near(n):
        pl.semaphore_signal(barrier, inc=1, device_id=tuple(p + d for p, d in zip(pos, DIRS[n])), device_id_type=MESH)

    def greet_all(step, unused):
        pl.semaphore_signal(barrier, inc=1, device_id=coords((me + step) % count), device_id_type=MESH)
        return unused

    if max(sizes) <= 4:
        each(greet_near)
        greeted = 1
        for axis, n in enumerate(sizes):
            greeted = greeted * (1 + jnp.where(pos[axis] > 0, 1, 0) + jnp.where(pos[axis] < n - 1, 1, 0))
        greeted = greeted - 1
    else:
        lax.fori_loop(1, count, greet_all, 0)
        greeted = count - 1

    def cut(step, n, halo, wrap):
        if step == 0:
            return (0, 0, n)
        if step > 0:
            return (n - halo, wrap - halo, halo)
        return (0, n, halo)

    def ends(xid, n):
        dx, dy, dz = DIRS[n]
        if dz:
            packed = {CB: scb, X0: sx0}.get(xid)
            arrived = {CB: zcb, X0: zx0}.get(xid)
            if packed is None:
                at = (C1, B1, X1).index(xid)
                packed, arrived = s1.at[at], z1.at[at]
            return packed, arrived.at[0 if dz > 0 else 1, 1 - dx, 1 - dy]
        low, halo = (xid in (CB, X0)), (H0 if xid in (CB, X0) else H1)
        dims = dims0 if low else dims1
        a, b, planes = cut(dx, dims[0], halo, 0)
        r, s, rows = cut(dy, dims[1], min(halo, dims[1]), 2 * TILE)
        if low:
            ref = e0 if xid == CB else x0
            lead = (slice(None),) if xid == CB else ()
            lanes = (pl.ds(0, LANES),)
        else:
            ref, lead, lanes = {C1: c1, B1: b1, X1: x1}[xid], (), (slice(None),)
        src = ref.at[lead + (pl.ds(halo + a, planes), pl.ds(r, rows)) + lanes]
        dst = ref.at[lead + (pl.ds(halo + b, planes), pl.ds(s, rows)) + lanes]
        return src, dst

    def remote(xid, n):
        src, dst = ends(xid, n)
        return pltpu.make_async_remote_copy(
            src_ref=src, dst_ref=dst, send_sem=xsem.at[xid], recv_sem=xsem.at[xid],
            device_id=tuple(p + d for p, d in zip(pos, DIRS[n])), device_id_type=MESH,
        )

    def launch(xid):
        each(lambda n: remote(xid, n).start())

    def fill(xid):
        def one(n):
            dst = ends(xid, n)[1]
            if xid == CB:
                dst[0] = jnp.ones(dst.shape[1:], F32)
                dst[1] = jnp.zeros(dst.shape[1:], F32)
            else:
                dst[...] = jnp.full(dst.shape, 1.0 if xid == C1 else 0.0, F32)
        for n, d in enumerate(DIRS):
            sources = [exists(axis, -step) for axis, step in enumerate(d) if step]
            present = functools.reduce(jnp.logical_and, sources)
            pl.when(jnp.logical_not(present))(functools.partial(one, n))

    def settle(xid):
        kinds = []
        for axis, n in enumerate(sizes):
            inside = (pos[axis] > 0) & (pos[axis] < n - 1)
            kinds.append([(0, None)] if n == 1 else [(1, None)] if n == 2 else [(1, jnp.logical_not(inside)), (2, inside)])
        for case in itertools.product(*kinds):
            rows = 0
            for n, d in enumerate(DIRS):
                if min(d) >= 0:
                    shape = ends(xid, n)[0].shape
                    rows += math.prod(shape[:-1]) * math.prod(k for (k, unused), step in zip(case, d) if step)
            part = pad.at[pl.ds(0, 2 * rows)]
            when([c for unused, c in case], pltpu.make_async_copy(part, part, xsem.at[xid]).wait)

    lane, sub = iota((TILE, LANES), 1), iota((TILE, LANES), 0)

    def pack0(tiles):
        out = tiles[0]
        for t in range(1, len(tiles)):
            part = pltpu.roll(tiles[t], 8 * t, 1)
            out = jnp.where(((lane - (8 * t - 4)) % LANES) < 8, part, out)
        return out

    def pack1(tiles):
        out = tiles[0]
        for t in range(1, len(tiles)):
            part = pltpu.roll(tiles[t], 8 * t, 1)
            place = (lane - 8 * t) % LANES
            out = jnp.where((place < 4) | ((place >= 60) & (place < 64)), part, out)
        return out

    def both_sides(arrived, dx, dy, k=None):
        at = (dx + 1, dy + 1) + (() if k is None else (k,))
        return jnp.where(lane % 8 < 4, arrived[(1,) + at], arrived[(0,) + at])

    def group_planes(n, halo):
        return ((0, [(t, halo + t) for t in range(n)]),
                (-1, [(t, halo + t - n) for t in range(n - halo, n)]),
                (1, [(t, halo + n + t) for t in range(halo)]))

    def unpack0(arrived, k, store):
        for dx, pairs in group_planes(dims0[0], H0):
            first = both_sides(arrived, dx, 0, k)
            second = jnp.where(sub < 4, both_sides(arrived, dx, 1, k), both_sides(arrived, dx, -1, k))
            for t, p in pairs:
                shift = (-8 * t) % LANES
                beyond = max(0, H0 - p, p - (H0 + dims0[0] - 1))
                if beyond < H0:
                    store(p, 0, pltpu.roll(first, shift, 1) if shift else first)
                if beyond < H0 - 1:
                    store(p, 1, pltpu.roll(second, shift, 1) if shift else second)

    def unpack1(arrived, field, store):
        z = dims1[2]
        for dx, pairs in group_planes(dims1[0], H1):
            first = jnp.where(sub < 4, both_sides(arrived, dx, 0), both_sides(arrived, dx, 1))
            second = both_sides(arrived, dx, -1)
            for t, p in pairs:
                shift = (z - 8 * t) % LANES
                for half, part in enumerate((first, second)):
                    rows = slice(half * TILE, (half + 1) * TILE)
                    part = pltpu.roll(part, shift, 1) if shift else part
                    store(p, rows, jnp.where(lane < z, field[p, rows, :], part))

    def post1(field, packed, tiles):
        for i, v in enumerate(tiles):
            field[H1 + i, 0:dims1[1], :] = v[0:dims1[1]]
        packed[...] = pack1(tiles)

    def message(tiles):
        out = tiles[0]
        for i in range(1, dims2[0]):
            out = jnp.where(lane // dims2[2] == i, tiles[i], out)
        return out

    def gather_start():
        src = tile.at[:, pl.ds(0, dims2[1])]
        dst = slots.at[:, pos[0], pos[2], pl.ds(dims2[1] * pos[1], dims2[1])]

        def go(step, unused):
            pltpu.make_async_remote_copy(
                src_ref=src, dst_ref=dst, send_sem=gsem, recv_sem=gsem,
                device_id=coords((me + step) % count), device_id_type=MESH,
            ).start()
            return unused
        lax.fori_loop(1, count, go, 0)
        pltpu.make_async_copy(src, dst, gsem).start()

    def gather_wait():
        part = pad.at[pl.ds(0, 2 * dims2[1] * (2 * count - 1))]
        pltpu.make_async_copy(part, part, gsem).wait()

    def gathered(kind, outside):
        z = dims2[2]
        per = LANES // z
        spot = iota((whole2[1], LANES), 1)
        planes = []
        for n in range(whole2[0] // fold):
            columns = []
            for first in range(0, width2 // z, per):
                total = None
                for g in range(min(per, fold * nz - first)):
                    plane = n + (first + g) // nz * (whole2[0] // fold)
                    x, i = divmod(plane, dims2[0])
                    shift = (z * (g - i)) % LANES
                    part = slots[kind, x, (first + g) % nz]
                    part = pltpu.roll(part, shift, 1) if shift else part
                    total = part if total is None else jnp.where(spot // z == g, part, total)
                columns.append(total)
            planes.append(columns[0] if len(columns) == 1 else jnp.concatenate(columns, 1))
        v = jnp.concatenate(planes, 0)
        if fold * whole2[2] < width2:
            v = jnp.where(iota(v.shape, 1) < fold * whole2[2], v, outside)
        return v

    for load in loads:
        load.wait()
    for k in range(2):
        scb[k] = pack0([e0[k, H0 + t, 0:TILE, 0:LANES] for t in range(dims0[0])])
    pl.semaphore_wait(barrier, greeted)

    launch(CB)
    for k, value in ((0, 1.0), (1, 0.0)):
        rows = slice(TILE + H0, 2 * TILE - H0)
        e0[k, :, rows, 0:LANES] = jnp.full((e0.shape[1], rows.stop - rows.start, LANES), value, F32)
    fill(CB)
    tiles = restrict([e0[0, H0 + t, 0:TILE, 0:LANES] for t in range(dims0[0])], dims0[2], dims0[1])
    post1(c1, s1.at[0], tiles)
    launch(C1)
    tile[0] = message(restrict(tiles, dims1[2], dims1[1]))
    for ref, value in ((c1, 1.0), (b1, 0.0), (x1, 0.0)):
        ref[:, 2 * dims1[1]:3 * dims1[1], :] = jnp.full((ref.shape[0], dims1[1], LANES), value, F32)
    rows = slice(TILE + H0, 2 * TILE - H0)
    x0[:, rows, 0:LANES] = jnp.zeros((x0.shape[0], rows.stop - rows.start, LANES), F32)
    for xid in (C1, B1, X0, X1):
        fill(xid)

    level0 = Level(refs0, dims0, H0, 2 * LANES, pos, sizes, 1.0)
    level1 = Level(refs1, dims1, H1, LANES, pos, sizes, 0.25)

    settle(CB)
    for k in range(2):
        def put(p, half, value):
            e0[k, p, half * TILE:(half + 1) * TILE, LANES:2 * LANES] = value
        unpack0(zcb, k, put)
    level0.coefs(lambda p: e0[0, p])
    b0 = lambda p: e0[1, p]
    level0.before(b0)
    r0 = [e0[1, p, 0:TILE, 0:LANES] - level0.own_op(level0.aux, p) for p in level0.planes(0)]
    tiles = restrict(r0, dims0[2], dims0[1])
    post1(b1, s1.at[1], tiles)
    launch(B1)

    tiles = [level0.aux[p, 0:TILE, 0:LANES] for p in level0.planes(0)]
    for p, v in zip(level0.planes(0), tiles):
        x0[p, 0:TILE, 0:LANES] = v
    sx0[...] = pack0(tiles)
    launch(X0)
    settle(C1)

    def put_c1(p, rows, value):
        c1m[p, rows, :] = value
    unpack1(z1.at[0], c1, put_c1)
    level1.coefs(lambda p: c1m[p])

    settle(B1)

    def put_b1(p, rows, value):
        b1m[p, rows, :] = value
    unpack1(z1.at[1], b1, put_b1)
    b1_of = lambda p: b1m[p]
    level1.before(b1_of)
    r1 = [b1m[p, 0:TILE, :] - level1.own_op(level1.aux, p) for p in level1.planes(0)]
    tile[1] = message(restrict(r1, dims1[2], dims1[1]))
    gather_start()
    tiles = [level1.aux[p, 0:TILE, :] for p in level1.planes(0)]
    tiles = [jnp.where(lane < dims1[2], v, pltpu.roll(v, dims1[2], 1)) for v in tiles]
    tiles = [jnp.where(sub < dims1[1], v, pltpu.roll(v, dims1[1], 0)) for v in tiles]
    post1(x1, s1.at[2], tiles)
    launch(X1)

    y2, z2 = whole2[1], whole2[2]
    shape3 = (whole2[0] * y2 // (2 * fold), width2)

    def pairs(v):
        return [v[n * y2:(n + 1) * y2] for n in range(v.shape[0] // y2)]

    def restrict2(v):
        planes = pairs(v)
        s = jnp.concatenate([a + b for a, b in zip(planes[0::2], planes[1::2])], 0)
        s = s + pltpu.roll(s, width2 - 1, 1)
        return (s + pltpu.roll(s, s.shape[0] - 1, 0)) * 0.125

    def prolong3(v):
        v = jnp.where((iota(shape3, 0) % 2 == 0) & (iota(shape3, 1) % 2 == 0), v, 0.0)
        v = v + pltpu.roll(v, 1, 1)
        v = v + pltpu.roll(v, 1, 0)
        return jnp.concatenate([part for part in pairs(v) for unused in range(2)], 0)

    settle(X0)

    def put_x0(p, half, value):
        x0[p, half * TILE:(half + 1) * TILE, LANES:2 * LANES] = value
    unpack0(zx0, None, put_x0)
    gather_wait()
    c2 = gathered(0, 1.0)
    level2 = Flat(refs2, y2, z2, 1, 0.25 ** 2, fold)
    level2.coefs(c2)
    level3 = Flat(refs3, y2, z2, 2, 0.25 ** 3, fold)
    level3.coefs(restrict2(c2))
    b2 = gathered(1, 0.0)
    x2 = chebyshev(None, b2, 2, 0.3, 2.0, level2)
    b3 = restrict2(b2 - level2.op(x2))
    x3 = chebyshev(None, b3, COARSE_DEGREE, 0.05, 2.0, level3)
    x2 = chebyshev(x2 + prolong3(x3), b2, 2, 0.3, 2.0, level2)
    for k in range(fold):
        x2s[pl.ds(k * x2.shape[0], x2.shape[0]), :] = pltpu.roll(x2, z2, 1) if k else x2

    settle(X1)

    def put_x1(p, rows, value):
        x1s[p, rows, :] = value
    unpack1(z1.at[2], x1, put_x1)

    quarter = LANES // 4
    first_lane, first_row = pos[2] * dims2[2], pos[1] * dims2[1]
    lanes = (first_lane + width2 + jnp.where(lane < 3 * quarter, lane // 2, lane // 2 - 2 * quarter)) % width2
    rows = [sub // 2 + 4 * half for half in range(2)]
    rows = [(first_row + y2 + jnp.where(r < 6, r, r - TILE)) % y2 for r in rows]
    low = ((first_row + y2 - 2) % y2) // TILE, ((first_lane + width2 - quarter // 2) % width2) // LANES
    high = ((first_row + 5) % y2) // TILE, ((first_lane + quarter + quarter // 2 - 1) % width2) // LANES
    window = range(-H1 // 2, (dims1[0] + H1) // 2)
    spread = []
    for i in window:
        plane = jnp.clip(pos[0] * dims2[0] + i, 0, whole2[0] - 1)

        def wide(row_tile):
            at = pl.ds(pl.multiple_of(plane * y2 + row_tile * TILE, TILE), TILE)
            if width2 == LANES:
                return jnp.take_along_axis(x2s[at, :], lanes, axis=1)
            parts = [x2s[at, pl.ds(pl.multiple_of(t * LANES, LANES), LANES)] for t in (low[1], high[1])]
            parts = [jnp.take_along_axis(v, lanes % LANES, axis=1) for v in parts]
            return jnp.where(lanes // LANES == low[1], *parts)
        if y2 == TILE:
            v = wide(0)
            spread.append([jnp.take_along_axis(v, r, axis=0) for r in rows])
        else:
            v, w = wide(low[0]), wide(high[0])
            spread.append([
                jnp.where(r // TILE == low[0], *(jnp.take_along_axis(u, r % TILE, axis=0) for u in (v, w))) for r in rows])
    for i, halves in zip(window, spread):
        for half, part in enumerate(halves):
            rows = slice(half * TILE, (half + 1) * TILE)
            for p in (2 * i + H1, 2 * i + H1 + 1):
                x1s[p, rows, :] = x1s[p, rows, :] + part
    level1.after(x1s, b1_of, b1, 2)

    window = range(-2, dims1[0] + 2)
    for group in range(0, len(window), 4):
        results = []
        for i in window[group:group + 4]:
            first, second = b1[H1 + i, 0:TILE, :], b1[H1 + i, TILE:2 * TILE, :]
            second = jnp.where(sub < 6, first, second)
            for half, part in enumerate((first, second)):
                part = jnp.take_along_axis(part, 4 * half + sub // 2, axis=0)
                for side in range(2):
                    e = jnp.take_along_axis(part, (LANES // 2) * side + lane // 2, axis=1)
                    at = (slice(half * TILE, (half + 1) * TILE), slice(side * LANES, (side + 1) * LANES))
                    for p in (2 * i + H0, 2 * i + H0 + 1):
                        if max(0, H0 - p, p - (H0 + dims0[0] - 1)) + half + side <= H0:
                            results.append(((p,) + at, x0[(p,) + at] + e))
        for at, v in results:
            x0[at] = v
    level0.after(x0, b0, x0, 1)
    for t, p in enumerate(level0.planes(0)):
        p_ref[t] = x0[p, 0:TILE, 0:LANES]
        q_ref[t] = e0[1, p, 0:TILE, 0:LANES] - level0.own_op(x0, p)


def finish(p_ref, q_ref, p_out, q_out):
    p_out[...] = p_ref[...]
    q_out[...] = q_ref[...]


def solution(mesh):
    sizes = tuple(mesh.shape[a] for a in AXES)
    count = sizes[0] * sizes[1] * sizes[2]

    def per_device(b, c):
        dims0 = b.shape
        dims1 = tuple(d // 2 for d in dims0)
        dims2 = tuple(d // 2 for d in dims1)
        assert dims0[1:] == (TILE, LANES) and dims2[0] * dims2[2] == LANES and 8 * dims0[0] == LANES
        whole2 = tuple(d * n for d, n in zip(dims2, sizes))
        assert whole2[1] % TILE == 0
        width2 = -(-whole2[2] // LANES) * LANES
        planes0, planes1 = dims0[0] + 2 * H0, dims1[0] + 2 * H1
        wide = pltpu.VMEM((planes0, 2 * TILE, 2 * LANES), F32)
        slim = pltpu.VMEM((planes1, 2 * TILE, LANES), F32)
        fold = 2 if 2 * whole2[2] == width2 and whole2[0] % 4 == 0 else 1
        flat2 = pltpu.VMEM((whole2[0] // fold * whole2[1], width2), F32)
        flat3 = pltpu.VMEM((whole2[0] // (2 * fold) * whole2[1], width2), F32)
        spot = (TILE, LANES)
        scratch = [
            pltpu.VMEM((2, planes0, 2 * TILE, 2 * LANES), F32), wide,
            pltpu.VMEM((2, 3, 3, 2) + spot, F32), pltpu.VMEM((2, 3, 3) + spot, F32),
            pltpu.VMEM((2,) + spot, F32), pltpu.VMEM(spot, F32),
            slim, slim, slim, pltpu.VMEM((3, 2, 3, 3) + spot, F32), pltpu.VMEM((3,) + spot, F32),
            slim, slim, slim,
            pltpu.VMEM((2, sizes[0], sizes[2], whole2[1], LANES), F32), pltpu.VMEM((2,) + spot, F32),
            pltpu.VMEM((max(4 * dims2[1] * count, 32 * dims0[0] * TILE), LANES), F32), pltpu.VMEM((whole2[0] * whole2[1], width2), F32),
        ] + [wide] * 7 + [slim] * 7 + [flat2] * 5 + [flat3] * 5 + [
            pltpu.SemaphoreType.DMA((2,)), pltpu.SemaphoreType.DMA((5,)), pltpu.SemaphoreType.DMA,
        ]
        shape = jax.ShapeDtypeStruct(dims0, F32)
        p, q = pl.pallas_call(
            functools.partial(kernel, sizes, dims0),
            out_shape=(shape, shape),
            in_specs=[pl.BlockSpec(memory_space=pltpu.HBM)] * 2,
            out_specs=(pl.BlockSpec(memory_space=pltpu.VMEM),) * 2,
            scratch_shapes=scratch,
            compiler_params=pltpu.CompilerParams(
                collective_id=0, has_side_effects=True, vmem_limit_bytes=KERNEL_VMEM),
        )(b, c)
        return pl.pallas_call(
            finish,
            out_shape=(shape, shape),
            in_specs=[pl.BlockSpec(memory_space=pltpu.VMEM)] * 2,
            out_specs=(pl.BlockSpec(memory_space=pltpu.VMEM),) * 2,
            compiler_params=pltpu.CompilerParams(vmem_limit_bytes=2 << 20),
        )(p, q)

    spec = P(*AXES)
    return jax.shard_map(per_device, mesh=mesh, in_specs=(spec, spec), out_specs=(spec, spec), check_vma=False)
```

```python
import functools
import itertools
import math

import jax
import jax.numpy as jnp
from jax import lax
from jax.experimental import pallas as pl
from jax.experimental.pallas import tpu as pltpu
from jax.sharding import PartitionSpec as P

COARSE_DEGREE = 6
AXES = ("gx", "gy", "gz")
LANES = 128
TILE = 8
H0 = 3
H1 = 4
MESH = pl.DeviceIdType.MESH
F32 = jnp.float32
FACES = ((1, 1), (1, -1), (-1, 1), (-1, -1), (0, 1), (0, -1), (1, 0), (-1, 0))
DIRS = tuple((dx, dy, 0) for dx, dy in FACES) + tuple(
    (dx, dy, dz) for dz in (1, -1) for dx, dy in FACES + ((0, 0),)
)
KERNEL_VMEM = 55088 << 10
CB, C1, B1, X0, X1 = range(5)


def iota(shape, dim):
    return lax.broadcasted_iota(jnp.int32, shape, dim)


def invert(v):
    r = pl.reciprocal(v, approx=True)
    return r * (2.0 - v * r)


def factors(lower, upper):
    theta = (upper + lower) / 2.0
    delta = (upper - lower) / 2.0
    sigma = theta / delta
    rho = 1.0 / sigma
    rho_next = 1.0 / (2.0 * sigma - rho)
    return 1.0 / theta, rho_next * rho, 2.0 * rho_next / delta


def chebyshev(start, source, steps, lower, upper, level):
    op_of, inv = level.op, level.inv()
    theta = (upper + lower) / 2.0
    delta = (upper - lower) / 2.0
    sigma = theta / delta
    rho_now = 1.0 / sigma
    if start is None:
        update = source * inv * (1.0 / theta)
        field = update
    else:
        remain = source - op_of(start)
        update = remain * inv * (1.0 / theta)
        field = start + update
    for index in range(steps - 1):
        rho_next = 1.0 / (2.0 * sigma - rho_now)
        remain = source - op_of(field)
        update = rho_next * rho_now * update + (2.0 * rho_next / delta) * (remain * inv)
        field = field + update
        rho_now = rho_next
    return field


class Flat:
    def __init__(self, refs, rows, lanes, step, scale, fold):
        self.refs, self.rows, self.lanes, self.step, self.scale, self.fold = refs, rows, lanes, step, scale, fold

    def ahead(self, v, axis):
        if axis == 2:
            return pltpu.roll(v, v.shape[1] - self.step, 1)
        if axis == 1:
            return pltpu.roll(v, v.shape[0] - self.step, 0)
        end = v[:self.rows]
        if self.fold == 2:
            end = pltpu.roll(end, self.lanes, 1)
        return jnp.concatenate([v[self.rows:], end], 0)

    def behind(self, v, axis):
        if axis == 2:
            return pltpu.roll(v, self.step, 1)
        if axis == 1:
            return pltpu.roll(v, self.step, 0)
        end = v[v.shape[0] - self.rows:]
        if self.fold == 2:
            end = pltpu.roll(end, self.lanes, 1)
        return jnp.concatenate([end, v[:v.shape[0] - self.rows]], 0)

    def coefs(self, c):
        n = c.shape[0] // self.rows
        row, lane = iota(c.shape, 0), iota(c.shape, 1)
        plane = row // self.rows
        if self.fold == 2:
            plane, lane = plane + jnp.where(lane < self.lanes, 0, n), lane % self.lanes
        spots = ((plane, 1, n * self.fold), (row % self.rows, self.step, self.rows), (lane, self.step, self.lanes))
        half = invert(c * (2.0 * self.scale))
        total = None
        for axis, (spot, step, end) in enumerate(spots):
            link = jnp.where(spot >= end - step, 0.0, invert(half + self.ahead(half, axis)))
            self.refs[axis][...] = link
            around = jnp.where(spot < step, 1.0, 0.0) + jnp.where(spot >= end - step, 1.0, 0.0)
            part = link + self.behind(link, axis) + c * (around * self.scale)
            total = part if total is None else total + part
        self.refs[3][...] = total
        self.refs[4][...] = invert(total)

    def inv(self):
        return self.refs[4][...]

    def op(self, v):
        out = self.refs[3][...] * v
        for axis in range(3):
            link = self.refs[axis][...]
            out = out - (link * self.ahead(v, axis) + self.behind(link * v, axis))
        return out


class Level:
    def __init__(self, refs, dims, halo, width, pos, sizes, scale):
        self.lx, self.ly, self.lz, self.diag, self.inv, self.tmp, self.aux = refs
        self.dims, self.halo, self.width, self.scale = dims, halo, width, scale
        shape = (2 * TILE, width)
        row, lane = iota(shape, 0), iota(shape, 1)

        def inner(axis):
            low = jnp.where(pos[axis] > 0, 1.0, 0.0).astype(F32)
            high = jnp.where(pos[axis] < sizes[axis] - 1, 1.0, 0.0).astype(F32)
            return low, high

        self.xlow, self.xhigh = inner(0)
        self.ymask = self.zmask = None
        outer = None
        masks = []
        for index, axis in ((row, 1), (lane, 2)):
            low, high = inner(axis)
            last = dims[axis] - 1
            end = shape[axis - 1] - 1
            masks.append(jnp.where(index == end, low, jnp.where(index == last, high, 1.0)))
            part = jnp.where(index == 0, 1.0 - low, jnp.where(index == last, 1.0 - high, 0.0))
            outer = part if outer is None else outer + part
        self.ymask, self.zmask = masks
        self.outer = outer

    def planes(self, reach):
        return range(self.halo - reach, self.halo + self.dims[0] + reach)

    def put(self, ref, p, v, budget, kind=""):
        own, row_side = slice(0, TILE), slice(TILE, 2 * TILE)
        lanes = slice(0, LANES)
        if self.width == LANES or budget >= 2 or (budget == 1 and kind in ("y", "z")):
            ref[p] = v
        elif kind == "y":
            ref[p, :, lanes] = v[:, lanes]
        elif budget == 1:
            ref[p, own, :] = v[own, :]
            ref[p, row_side, lanes] = v[row_side, lanes]
        elif kind == "z":
            ref[p, own, :] = v[own, :]
        else:
            ref[p, own, lanes] = v[own, lanes]

    def each(self, reach, body):
        first, last = self.halo, self.halo + self.dims[0] - 1
        for p in self.planes(reach):
            for ref, q, v, *kind in body(p):
                near = p + 1 if kind == ["x"] and p < first else p
                self.put(ref, q, v, reach - max(0, first - near, near - last), *kind)

    def back(self, v, dim):
        n = v.shape[dim]
        return pltpu.roll(v, n - 1, dim)

    def coefs(self, c_of):
        first, last = self.halo, self.halo + self.dims[0] - 1
        reach = self.halo - 1
        outer = self.outer * self.scale

        half = {}

        def half_of(p):
            if p not in half:
                half[p] = invert(c_of(p) * (2.0 * self.scale))
            return half[p]

        def face_x(p):
            face = invert(half_of(p) + half_of(p + 1))
            factor = {first - 1: self.xlow, last: self.xhigh}.get(p)
            return face if factor is None else face * factor

        def others(p):
            h = half_of(p)
            ly = invert(h + self.back(h, 0)) * self.ymask
            lz = invert(h + self.back(h, 1)) * self.zmask
            face = face_x(p)
            total = (face + faces.pop()) + (ly + pltpu.roll(ly, 1, 0)) + (lz + pltpu.roll(lz, 1, 1))
            faces.append(face)
            around = outer
            if p in (first, last):
                around = around + (1.0 - (self.xlow if p == first else self.xhigh)) * self.scale
            total = total + c_of(p) * around
            return (self.lx, p, face, "x"), (self.ly, p, ly, "y"), (self.lz, p, lz, "z"), (self.diag, p, total), (self.inv, p, invert(total))

        faces = [face_x(first - reach - 1)]
        self.put(self.lx, first - reach - 1, faces[0], 0)
        self.each(reach, others)

    def op(self, v, p):
        here = v[p]
        ly, lz = self.ly[p], self.lz[p]
        x = self.lx[p] * v[p + 1] + self.lx[p - 1] * v[p - 1]
        y = ly * self.back(here, 0) + pltpu.roll(ly * here, 1, 0)
        z = lz * self.back(here, 1) + pltpu.roll(lz * here, 1, 1)
        return self.diag[p] * here - x - (y + z)

    def own_op(self, v, p):
        own = (slice(0, TILE), slice(0, LANES))
        here = v[p, :, 0:LANES]
        wide = v[p, 0:TILE, :]
        ly, lz = self.ly[p, :, 0:LANES], self.lz[p, 0:TILE, :]
        x = self.lx[p, 0:TILE, 0:LANES] * v[p + 1, 0:TILE, 0:LANES] + self.lx[p - 1, 0:TILE, 0:LANES] * v[p - 1, 0:TILE, 0:LANES]
        y = ly * self.back(here, 0) + pltpu.roll(ly * here, 1, 0)
        z = lz * self.back(wide, 1) + pltpu.roll(lz * wide, 1, 1)
        return self.diag[p, 0:TILE, 0:LANES] * here[own] - x - (y[own] + z[own])

    def before(self, b_of):
        first, mix, gain = factors(0.3, 2.0)

        def one(p):
            return ((self.tmp, p, b_of(p) * self.inv[p] * first),)

        def two(p):
            d = self.tmp[p]
            return ((self.aux, p, d + (mix * d + gain * ((b_of(p) - self.op(self.tmp, p)) * self.inv[p]))),)
        self.each(2, one)
        self.each(1, two)

    def after(self, start, b_of, out, reach):
        first, mix, gain = factors(0.3, 2.0)

        def one(p):
            update = (b_of(p) - self.op(start, p)) * self.inv[p] * first
            return (self.aux, p, update), (self.tmp, p, start[p] + update)

        def two(p):
            update = mix * self.aux[p] + gain * ((b_of(p) - self.op(self.tmp, p)) * self.inv[p])
            return ((out, p, self.tmp[p] + update),)
        self.each(reach + 1, one)
        self.each(reach, two)


def restrict(tiles, lanes, rows):
    out = []
    lane = (2 * iota((TILE, LANES), 1)) % lanes
    row = (2 * iota((TILE, LANES), 0)) % rows
    for a, b in zip(tiles[0::2], tiles[1::2]):
        s = a + b
        s = s + pltpu.roll(s, LANES - 1, 1)
        s = (s + pltpu.roll(s, TILE - 1, 0)) * 0.125
        s = jnp.take_along_axis(s, lane, axis=1)
        out.append(jnp.take_along_axis(s, row, axis=0))
    return out


def kernel(sizes, dims0, b_hbm, c_hbm, p_ref, q_ref, *scratch):
    (e0, x0, zcb, zx0, scb, sx0, c1, b1, x1, z1, s1, c1m, b1m, x1s, slots, tile, pad, x2s) = scratch[:18]
    refs0, refs1, refs2, refs3 = scratch[18:25], scratch[25:32], scratch[32:37], scratch[37:42]
    isem, xsem, gsem = scratch[42:]
    pos = tuple(lax.axis_index(a) for a in AXES)
    dims1 = tuple(d // 2 for d in dims0)
    dims2 = tuple(d // 2 for d in dims1)
    whole2 = tuple(d * n for d, n in zip(dims2, sizes))
    nx, ny, nz = sizes
    count = nx * ny * nz
    me = (pos[0] * ny + pos[1]) * nz + pos[2]
    width2 = x2s.shape[1]
    fold = 2 if 2 * whole2[2] == width2 and whole2[0] % 4 == 0 else 1
    own0 = pl.ds(H0, dims0[0])

    loads = [
        pltpu.make_async_copy(src, e0.at[k, own0, pl.ds(0, TILE), pl.ds(0, LANES)], isem.at[k])
        for k, src in enumerate((c_hbm, b_hbm))
    ]
    for load in loads:
        load.start()

    def coords(index):
        return (index // (ny * nz), (index // nz) % ny, index % nz)

    barrier = pltpu.get_barrier_semaphore()


    def exists(axis, step):
        if step == 0:
            return None
        return pos[axis] < sizes[axis] - 1 if step > 0 else pos[axis] > 0

    def when(conditions, body):
        conditions = [c for c in conditions if c is not None]
        if not conditions:
            body()
            return
        both = conditions[0]
        for c in conditions[1:]:
            both = both & c
        pl.when(both)(body)

    def each(body):
        for dz in (1, -1, 0):
            def group():
                for n, d in enumerate(DIRS):
                    if d[2] == dz:
                        when([exists(0, d[0]), exists(1, d[1])], functools.partial(body, n))
            when([exists(2, dz)], group)

    def greet_near(n):
        pl.semaphore_signal(barrier, inc=1, device_id=tuple(p + d for p, d in zip(pos, DIRS[n])), device_id_type=MESH)

    def greet_all(step, unused):
        pl.semaphore_signal(barrier, inc=1, device_id=coords((me + step) % count), device_id_type=MESH)
        return unused

    if max(sizes) <= 4:
        each(greet_near)
        greeted = 1
        for axis, n in enumerate(sizes):
            greeted = greeted * (1 + jnp.where(pos[axis] > 0, 1, 0) + jnp.where(pos[axis] < n - 1, 1, 0))
        greeted = greeted - 1
    else:
        lax.fori_loop(1, count, greet_all, 0)
        greeted = count - 1

    def cut(step, n, halo, wrap):
        if step == 0:
            return (0, 0, n)
        if step > 0:
            return (n - halo, wrap - halo, halo)
        return (0, n, halo)

    def ends(xid, n):
        dx, dy, dz = DIRS[n]
        if dz:
            packed = {CB: scb, X0: sx0}.get(xid)
            arrived = {CB: zcb, X0: zx0}.get(xid)
            if packed is None:
                at = (C1, B1, X1).index(xid)
                packed, arrived = s1.at[at], z1.at[at]
            return packed, arrived.at[0 if dz > 0 else 1, 1 - dx, 1 - dy]
        low, halo = (xid in (CB, X0)), (H0 if xid in (CB, X0) else H1)
        dims = dims0 if low else dims1
        a, b, planes = cut(dx, dims[0], halo, 0)
        r, s, rows = cut(dy, dims[1], min(halo, dims[1]), 2 * TILE)
        if low:
            ref = e0 if xid == CB else x0
            lead = (slice(None),) if xid == CB else ()
            lanes = (pl.ds(0, LANES),)
        else:
            ref, lead, lanes = {C1: c1, B1: b1, X1: x1}[xid], (), (slice(None),)
        src = ref.at[lead + (pl.ds(halo + a, planes), pl.ds(r, rows)) + lanes]
        dst = ref.at[lead + (pl.ds(halo + b, planes), pl.ds(s, rows)) + lanes]
        return src, dst

    def remote(xid, n):
        src, dst = ends(xid, n)
        return pltpu.make_async_remote_copy(
            src_ref=src, dst_ref=dst, send_sem=xsem.at[xid], recv_sem=xsem.at[xid],
            device_id=tuple(p + d for p, d in zip(pos, DIRS[n])), device_id_type=MESH,
        )

    def launch(xid):
        each(lambda n: remote(xid, n).start())

    def fill(xid):
        def one(n):
            dst = ends(xid, n)[1]
            if xid == CB:
                dst[0] = jnp.ones(dst.shape[1:], F32)
                dst[1] = jnp.zeros(dst.shape[1:], F32)
            else:
                dst[...] = jnp.full(dst.shape, 1.0 if xid == C1 else 0.0, F32)
        for n, d in enumerate(DIRS):
            sources = [exists(axis, -step) for axis, step in enumerate(d) if step]
            present = functools.reduce(jnp.logical_and, sources)
            pl.when(jnp.logical_not(present))(functools.partial(one, n))

    def settle(xid):
        kinds = []
        for axis, n in enumerate(sizes):
            inside = (pos[axis] > 0) & (pos[axis] < n - 1)
            kinds.append([(0, None)] if n == 1 else [(1, None)] if n == 2 else [(1, jnp.logical_not(inside)), (2, inside)])
        for case in itertools.product(*kinds):
            rows = 0
            for n, d in enumerate(DIRS):
                if min(d) >= 0:
                    shape = ends(xid, n)[0].shape
                    rows += math.prod(shape[:-1]) * math.prod(k for (k, unused), step in zip(case, d) if step)
            part = pad.at[pl.ds(0, 2 * rows)]
            when([c for unused, c in case], pltpu.make_async_copy(part, part, xsem.at[xid]).wait)

    lane, sub = iota((TILE, LANES), 1), iota((TILE, LANES), 0)

    def pack0(tiles):
        out = tiles[0]
        for t in range(1, len(tiles)):
            part = pltpu.roll(tiles[t], 8 * t, 1)
            out = jnp.where(((lane - (8 * t - 4)) % LANES) < 8, part, out)
        return out

    def pack1(tiles):
        out = tiles[0]
        for t in range(1, len(tiles)):
            part = pltpu.roll(tiles[t], 8 * t, 1)
            place = (lane - 8 * t) % LANES
            out = jnp.where((place < 4) | ((place >= 60) & (place < 64)), part, out)
        return out

    def both_sides(arrived, dx, dy, k=None):
        at = (dx + 1, dy + 1) + (() if k is None else (k,))
        return jnp.where(lane % 8 < 4, arrived[(1,) + at], arrived[(0,) + at])

    def group_planes(n, halo):
        return ((0, [(t, halo + t) for t in range(n)]),
                (-1, [(t, halo + t - n) for t in range(n - halo, n)]),
                (1, [(t, halo + n + t) for t in range(halo)]))

    def unpack0(arrived, k, store):
        for dx, pairs in group_planes(dims0[0], H0):
            first = both_sides(arrived, dx, 0, k)
            second = jnp.where(sub < 4, both_sides(arrived, dx, 1, k), both_sides(arrived, dx, -1, k))
            for t, p in pairs:
                shift = (-8 * t) % LANES
                beyond = max(0, H0 - p, p - (H0 + dims0[0] - 1))
                if beyond < H0:
                    store(p, 0, pltpu.roll(first, shift, 1) if shift else first)
                if beyond < H0 - 1:
                    store(p, 1, pltpu.roll(second, shift, 1) if shift else second)

    def unpack1(arrived, field, store):
        z = dims1[2]
        for dx, pairs in group_planes(dims1[0], H1):
            first = jnp.where(sub < 4, both_sides(arrived, dx, 0), both_sides(arrived, dx, 1))
            second = both_sides(arrived, dx, -1)
            for t, p in pairs:
                shift = (z - 8 * t) % LANES
                for half, part in enumerate((first, second)):
                    rows = slice(half * TILE, (half + 1) * TILE)
                    part = pltpu.roll(part, shift, 1) if shift else part
                    store(p, rows, jnp.where(lane < z, field[p, rows, :], part))

    def post1(field, packed, tiles):
        for i, v in enumerate(tiles):
            field[H1 + i, 0:dims1[1], :] = v[0:dims1[1]]
        packed[...] = pack1(tiles)

    def message(tiles):
        out = tiles[0]
        for i in range(1, dims2[0]):
            out = jnp.where(lane // dims2[2] == i, tiles[i], out)
        return out

    def gather_start():
        src = tile.at[:, pl.ds(0, dims2[1])]
        dst = slots.at[:, pos[0], pos[2], pl.ds(dims2[1] * pos[1], dims2[1])]

        def go(step, unused):
            pltpu.make_async_remote_copy(
                src_ref=src, dst_ref=dst, send_sem=gsem, recv_sem=gsem,
                device_id=coords((me + step) % count), device_id_type=MESH,
            ).start()
            return unused
        lax.fori_loop(1, count, go, 0)
        pltpu.make_async_copy(src, dst, gsem).start()

    def gather_wait():
        part = pad.at[pl.ds(0, 2 * dims2[1] * (2 * count - 1))]
        pltpu.make_async_copy(part, part, gsem).wait()

    def gathered(kind, outside):
        z = dims2[2]
        per = LANES // z
        spot = iota((whole2[1], LANES), 1)
        planes = []
        for n in range(whole2[0] // fold):
            columns = []
            for first in range(0, width2 // z, per):
                total = None
                for g in range(min(per, fold * nz - first)):
                    plane = n + (first + g) // nz * (whole2[0] // fold)
                    x, i = divmod(plane, dims2[0])
                    shift = (z * (g - i)) % LANES
                    part = slots[kind, x, (first + g) % nz]
                    part = pltpu.roll(part, shift, 1) if shift else part
                    total = part if total is None else jnp.where(spot // z == g, part, total)
                columns.append(total)
            planes.append(columns[0] if len(columns) == 1 else jnp.concatenate(columns, 1))
        v = jnp.concatenate(planes, 0)
        if fold * whole2[2] < width2:
            v = jnp.where(iota(v.shape, 1) < fold * whole2[2], v, outside)
        return v

    for load in loads:
        load.wait()
    for k in range(2):
        scb[k] = pack0([e0[k, H0 + t, 0:TILE, 0:LANES] for t in range(dims0[0])])
    pl.semaphore_wait(barrier, greeted)

    launch(CB)
    for k, value in ((0, 1.0), (1, 0.0)):
        rows = slice(TILE + H0, 2 * TILE - H0)
        e0[k, :, rows, 0:LANES] = jnp.full((e0.shape[1], rows.stop - rows.start, LANES), value, F32)
    fill(CB)
    tiles = restrict([e0[0, H0 + t, 0:TILE, 0:LANES] for t in range(dims0[0])], dims0[2], dims0[1])
    post1(c1, s1.at[0], tiles)
    launch(C1)
    tile[0] = message(restrict(tiles, dims1[2], dims1[1]))
    for ref, value in ((c1, 1.0), (b1, 0.0), (x1, 0.0)):
        ref[:, 2 * dims1[1]:3 * dims1[1], :] = jnp.full((ref.shape[0], dims1[1], LANES), value, F32)
    rows = slice(TILE + H0, 2 * TILE - H0)
    x0[:, rows, 0:LANES] = jnp.zeros((x0.shape[0], rows.stop - rows.start, LANES), F32)
    for xid in (C1, B1, X0, X1):
        fill(xid)

    level0 = Level(refs0, dims0, H0, 2 * LANES, pos, sizes, 1.0)
    level1 = Level(refs1, dims1, H1, LANES, pos, sizes, 0.25)

    settle(CB)
    for k in range(2):
        def put(p, half, value):
            e0[k, p, half * TILE:(half + 1) * TILE, LANES:2 * LANES] = value
        unpack0(zcb, k, put)
    level0.coefs(lambda p: e0[0, p])
    b0 = lambda p: e0[1, p]
    level0.before(b0)
    r0 = [e0[1, p, 0:TILE, 0:LANES] - level0.own_op(level0.aux, p) for p in level0.planes(0)]
    tiles = restrict(r0, dims0[2], dims0[1])
    post1(b1, s1.at[1], tiles)
    launch(B1)

    tiles = [level0.aux[p, 0:TILE, 0:LANES] for p in level0.planes(0)]
    for p, v in zip(level0.planes(0), tiles):
        x0[p, 0:TILE, 0:LANES] = v
    sx0[...] = pack0(tiles)
    settle(C1)

    def put_c1(p, rows, value):
        c1m[p, rows, :] = value
    unpack1(z1.at[0], c1, put_c1)
    level1.coefs(lambda p: c1m[p])

    settle(B1)

    def put_b1(p, rows, value):
        b1m[p, rows, :] = value
    unpack1(z1.at[1], b1, put_b1)
    b1_of = lambda p: b1m[p]
    level1.before(b1_of)
    r1 = [b1m[p, 0:TILE, :] - level1.own_op(level1.aux, p) for p in level1.planes(0)]
    tile[1] = message(restrict(r1, dims1[2], dims1[1]))
    gather_start()
    tiles = [level1.aux[p, 0:TILE, :] for p in level1.planes(0)]
    tiles = [jnp.where(lane < dims1[2], v, pltpu.roll(v, dims1[2], 1)) for v in tiles]
    tiles = [jnp.where(sub < dims1[1], v, pltpu.roll(v, dims1[1], 0)) for v in tiles]
    post1(x1, s1.at[2], tiles)
    launch(X1)
    launch(X0)

    y2, z2 = whole2[1], whole2[2]
    shape3 = (whole2[0] * y2 // (2 * fold), width2)

    def pairs(v):
        return [v[n * y2:(n + 1) * y2] for n in range(v.shape[0] // y2)]

    def restrict2(v):
        planes = pairs(v)
        s = jnp.concatenate([a + b for a, b in zip(planes[0::2], planes[1::2])], 0)
        s = s + pltpu.roll(s, width2 - 1, 1)
        return (s + pltpu.roll(s, s.shape[0] - 1, 0)) * 0.125

    def prolong3(v):
        v = jnp.where((iota(shape3, 0) % 2 == 0) & (iota(shape3, 1) % 2 == 0), v, 0.0)
        v = v + pltpu.roll(v, 1, 1)
        v = v + pltpu.roll(v, 1, 0)
        return jnp.concatenate([part for part in pairs(v) for unused in range(2)], 0)

    gather_wait()
    c2 = gathered(0, 1.0)
    level2 = Flat(refs2, y2, z2, 1, 0.25 ** 2, fold)
    level2.coefs(c2)
    level3 = Flat(refs3, y2, z2, 2, 0.25 ** 3, fold)
    level3.coefs(restrict2(c2))
    b2 = gathered(1, 0.0)
    x2 = chebyshev(None, b2, 2, 0.3, 2.0, level2)
    b3 = restrict2(b2 - level2.op(x2))
    x3 = chebyshev(None, b3, COARSE_DEGREE, 0.05, 2.0, level3)
    x2 = chebyshev(x2 + prolong3(x3), b2, 2, 0.3, 2.0, level2)
    for k in range(fold):
        x2s[pl.ds(k * x2.shape[0], x2.shape[0]), :] = pltpu.roll(x2, z2, 1) if k else x2

    settle(X1)

    def put_x1(p, rows, value):
        x1s[p, rows, :] = value
    unpack1(z1.at[2], x1, put_x1)

    quarter = LANES // 4
    first_lane, first_row = pos[2] * dims2[2], pos[1] * dims2[1]
    lanes = (first_lane + width2 + jnp.where(lane < 3 * quarter, lane // 2, lane // 2 - 2 * quarter)) % width2
    rows = [sub // 2 + 4 * half for half in range(2)]
    rows = [(first_row + y2 + jnp.where(r < 6, r, r - TILE)) % y2 for r in rows]
    low = ((first_row + y2 - 2) % y2) // TILE, ((first_lane + width2 - quarter // 2) % width2) // LANES
    high = ((first_row + 5) % y2) // TILE, ((first_lane + quarter + quarter // 2 - 1) % width2) // LANES
    window = range(-H1 // 2, (dims1[0] + H1) // 2)
    spread = []
    for i in window:
        plane = jnp.clip(pos[0] * dims2[0] + i, 0, whole2[0] - 1)

        def wide(row_tile):
            at = pl.ds(pl.multiple_of(plane * y2 + row_tile * TILE, TILE), TILE)
            if width2 == LANES:
                return jnp.take_along_axis(x2s[at, :], lanes, axis=1)
            parts = [x2s[at, pl.ds(pl.multiple_of(t * LANES, LANES), LANES)] for t in (low[1], high[1])]
            parts = [jnp.take_along_axis(v, lanes % LANES, axis=1) for v in parts]
            return jnp.where(lanes // LANES == low[1], *parts)
        if y2 == TILE:
            v = wide(0)
            spread.append([jnp.take_along_axis(v, r, axis=0) for r in rows])
        else:
            v, w = wide(low[0]), wide(high[0])
            spread.append([
                jnp.where(r // TILE == low[0], *(jnp.take_along_axis(u, r % TILE, axis=0) for u in (v, w))) for r in rows])
    for i, halves in zip(window, spread):
        for half, part in enumerate(halves):
            rows = slice(half * TILE, (half + 1) * TILE)
            for p in (2 * i + H1, 2 * i + H1 + 1):
                x1s[p, rows, :] = x1s[p, rows, :] + part
    level1.after(x1s, b1_of, b1, 2)

    settle(X0)

    def put_x0(p, half, value):
        x0[p, half * TILE:(half + 1) * TILE, LANES:2 * LANES] = value
    unpack0(zx0, None, put_x0)

    window = range(-2, dims1[0] + 2)
    for group in range(0, len(window), 4):
        results = []
        for i in window[group:group + 4]:
            first, second = b1[H1 + i, 0:TILE, :], b1[H1 + i, TILE:2 * TILE, :]
            second = jnp.where(sub < 6, first, second)
            for half, part in enumerate((first, second)):
                part = jnp.take_along_axis(part, 4 * half + sub // 2, axis=0)
                for side in range(2):
                    e = jnp.take_along_axis(part, (LANES // 2) * side + lane // 2, axis=1)
                    at = (slice(half * TILE, (half + 1) * TILE), slice(side * LANES, (side + 1) * LANES))
                    for p in (2 * i + H0, 2 * i + H0 + 1):
                        if max(0, H0 - p, p - (H0 + dims0[0] - 1)) + half + side <= H0:
                            results.append(((p,) + at, x0[(p,) + at] + e))
        for at, v in results:
            x0[at] = v
    level0.after(x0, b0, x0, 1)
    for t, p in enumerate(level0.planes(0)):
        p_ref[t] = x0[p, 0:TILE, 0:LANES]
        q_ref[t] = e0[1, p, 0:TILE, 0:LANES] - level0.own_op(x0, p)


def finish(p_ref, q_ref, p_out, q_out):
    p_out[...] = p_ref[...]
    q_out[...] = q_ref[...]


def solution(mesh):
    sizes = tuple(mesh.shape[a] for a in AXES)
    count = sizes[0] * sizes[1] * sizes[2]

    def per_device(b, c):
        dims0 = b.shape
        dims1 = tuple(d // 2 for d in dims0)
        dims2 = tuple(d // 2 for d in dims1)
        assert dims0[1:] == (TILE, LANES) and dims2[0] * dims2[2] == LANES and 8 * dims0[0] == LANES
        whole2 = tuple(d * n for d, n in zip(dims2, sizes))
        assert whole2[1] % TILE == 0
        width2 = -(-whole2[2] // LANES) * LANES
        planes0, planes1 = dims0[0] + 2 * H0, dims1[0] + 2 * H1
        wide = pltpu.VMEM((planes0, 2 * TILE, 2 * LANES), F32)
        slim = pltpu.VMEM((planes1, 2 * TILE, LANES), F32)
        fold = 2 if 2 * whole2[2] == width2 and whole2[0] % 4 == 0 else 1
        flat2 = pltpu.VMEM((whole2[0] // fold * whole2[1], width2), F32)
        flat3 = pltpu.VMEM((whole2[0] // (2 * fold) * whole2[1], width2), F32)
        spot = (TILE, LANES)
        scratch = [
            pltpu.VMEM((2, planes0, 2 * TILE, 2 * LANES), F32), wide,
            pltpu.VMEM((2, 3, 3, 2) + spot, F32), pltpu.VMEM((2, 3, 3) + spot, F32),
            pltpu.VMEM((2,) + spot, F32), pltpu.VMEM(spot, F32),
            slim, slim, slim, pltpu.VMEM((3, 2, 3, 3) + spot, F32), pltpu.VMEM((3,) + spot, F32),
            slim, slim, slim,
            pltpu.VMEM((2, sizes[0], sizes[2], whole2[1], LANES), F32), pltpu.VMEM((2,) + spot, F32),
            pltpu.VMEM((max(4 * dims2[1] * count, 32 * dims0[0] * TILE), LANES), F32), pltpu.VMEM((whole2[0] * whole2[1], width2), F32),
        ] + [wide] * 7 + [slim] * 7 + [flat2] * 5 + [flat3] * 5 + [
            pltpu.SemaphoreType.DMA((2,)), pltpu.SemaphoreType.DMA((5,)), pltpu.SemaphoreType.DMA,
        ]
        shape = jax.ShapeDtypeStruct(dims0, F32)
        p, q = pl.pallas_call(
            functools.partial(kernel, sizes, dims0),
            out_shape=(shape, shape),
            in_specs=[pl.BlockSpec(memory_space=pltpu.HBM)] * 2,
            out_specs=(pl.BlockSpec(memory_space=pltpu.VMEM),) * 2,
            scratch_shapes=scratch,
            compiler_params=pltpu.CompilerParams(
                collective_id=0, has_side_effects=True, vmem_limit_bytes=KERNEL_VMEM),
        )(b, c)
        return pl.pallas_call(
            finish,
            out_shape=(shape, shape),
            in_specs=[pl.BlockSpec(memory_space=pltpu.VMEM)] * 2,
            out_specs=(pl.BlockSpec(memory_space=pltpu.VMEM),) * 2,
            compiler_params=pltpu.CompilerParams(vmem_limit_bytes=2 << 20),
        )(p, q)

    spec = P(*AXES)
    return jax.shard_map(per_device, mesh=mesh, in_specs=(spec, spec), out_specs=(spec, spec), check_vma=False)
```

```python
import functools
import itertools
import math

import jax
import jax.numpy as jnp
from jax import lax
from jax.experimental import pallas as pl
from jax.experimental.pallas import tpu as pltpu
from jax.sharding import PartitionSpec as P

COARSE_DEGREE = 6
AXES = ("gx", "gy", "gz")
LANES = 128
TILE = 8
H0 = 3
H1 = 4
MESH = pl.DeviceIdType.MESH
F32 = jnp.float32
FACES = ((1, 1), (1, -1), (-1, 1), (-1, -1), (1, 0), (-1, 0), (0, 1), (0, -1))
DIRS = tuple((dx, dy, 0) for dx, dy in FACES) + tuple(
    (dx, dy, dz) for dz in (1, -1) for dx, dy in FACES + ((0, 0),)
)
KERNEL_VMEM = 55088 << 10
CB, C1, B1, X0, X1 = range(5)


def iota(shape, dim):
    return lax.broadcasted_iota(jnp.int32, shape, dim)


def invert(v):
    r = pl.reciprocal(v, approx=True)
    return r * (2.0 - v * r)


def factors(lower, upper):
    theta = (upper + lower) / 2.0
    delta = (upper - lower) / 2.0
    sigma = theta / delta
    rho = 1.0 / sigma
    rho_next = 1.0 / (2.0 * sigma - rho)
    return 1.0 / theta, rho_next * rho, 2.0 * rho_next / delta


def chebyshev(start, source, steps, lower, upper, level):
    op_of, inv = level.op, level.inv()
    theta = (upper + lower) / 2.0
    delta = (upper - lower) / 2.0
    sigma = theta / delta
    rho_now = 1.0 / sigma
    if start is None:
        update = source * inv * (1.0 / theta)
        field = update
    else:
        remain = source - op_of(start)
        update = remain * inv * (1.0 / theta)
        field = start + update
    for index in range(steps - 1):
        rho_next = 1.0 / (2.0 * sigma - rho_now)
        remain = source - op_of(field)
        update = rho_next * rho_now * update + (2.0 * rho_next / delta) * (remain * inv)
        field = field + update
        rho_now = rho_next
    return field


class Flat:
    def __init__(self, refs, rows, lanes, step, scale, fold):
        self.refs, self.rows, self.lanes, self.step, self.scale, self.fold = refs, rows, lanes, step, scale, fold

    def ahead(self, v, axis):
        if axis == 2:
            return pltpu.roll(v, v.shape[1] - self.step, 1)
        if axis == 1:
            return pltpu.roll(v, v.shape[0] - self.step, 0)
        end = v[:self.rows]
        if self.fold == 2:
            end = pltpu.roll(end, self.lanes, 1)
        return jnp.concatenate([v[self.rows:], end], 0)

    def behind(self, v, axis):
        if axis == 2:
            return pltpu.roll(v, self.step, 1)
        if axis == 1:
            return pltpu.roll(v, self.step, 0)
        end = v[v.shape[0] - self.rows:]
        if self.fold == 2:
            end = pltpu.roll(end, self.lanes, 1)
        return jnp.concatenate([end, v[:v.shape[0] - self.rows]], 0)

    def coefs(self, c):
        n = c.shape[0] // self.rows
        row, lane = iota(c.shape, 0), iota(c.shape, 1)
        plane = row // self.rows
        if self.fold == 2:
            plane, lane = plane + jnp.where(lane < self.lanes, 0, n), lane % self.lanes
        spots = ((plane, 1, n * self.fold), (row % self.rows, self.step, self.rows), (lane, self.step, self.lanes))
        half = invert(c * (2.0 * self.scale))
        total = None
        for axis, (spot, step, end) in enumerate(spots):
            link = jnp.where(spot >= end - step, 0.0, invert(half + self.ahead(half, axis)))
            self.refs[axis][...] = link
            around = jnp.where(spot < step, 1.0, 0.0) + jnp.where(spot >= end - step, 1.0, 0.0)
            part = link + self.behind(link, axis) + c * (around * self.scale)
            total = part if total is None else total + part
        self.refs[3][...] = total
        self.refs[4][...] = invert(total)

    def inv(self):
        return self.refs[4][...]

    def op(self, v):
        out = self.refs[3][...] * v
        for axis in range(3):
            link = self.refs[axis][...]
            out = out - (link * self.ahead(v, axis) + self.behind(link * v, axis))
        return out


class Level:
    def __init__(self, refs, dims, halo, width, pos, sizes, scale):
        self.lx, self.ly, self.lz, self.diag, self.inv, self.tmp, self.aux = refs
        self.dims, self.halo, self.width, self.scale = dims, halo, width, scale
        shape = (2 * TILE, width)
        row, lane = iota(shape, 0), iota(shape, 1)

        def inner(axis):
            low = jnp.where(pos[axis] > 0, 1.0, 0.0).astype(F32)
            high = jnp.where(pos[axis] < sizes[axis] - 1, 1.0, 0.0).astype(F32)
            return low, high

        self.xlow, self.xhigh = inner(0)
        self.ymask = self.zmask = None
        outer = None
        masks = []
        for index, axis in ((row, 1), (lane, 2)):
            low, high = inner(axis)
            last = dims[axis] - 1
            end = shape[axis - 1] - 1
            masks.append(jnp.where(index == end, low, jnp.where(index == last, high, 1.0)))
            part = jnp.where(index == 0, 1.0 - low, jnp.where(index == last, 1.0 - high, 0.0))
            outer = part if outer is None else outer + part
        self.ymask, self.zmask = masks
        self.outer = outer

    def planes(self, reach):
        return range(self.halo - reach, self.halo + self.dims[0] + reach)

    def put(self, ref, p, v, budget, kind=""):
        own, row_side = slice(0, TILE), slice(TILE, 2 * TILE)
        lanes = slice(0, LANES)
        if self.width == LANES or budget >= 2 or (budget == 1 and kind in ("y", "z")):
            ref[p] = v
        elif kind == "y":
            ref[p, :, lanes] = v[:, lanes]
        elif budget == 1:
            ref[p, own, :] = v[own, :]
            ref[p, row_side, lanes] = v[row_side, lanes]
        elif kind == "z":
            ref[p, own, :] = v[own, :]
        else:
            ref[p, own, lanes] = v[own, lanes]

    def each(self, reach, body):
        first, last = self.halo, self.halo + self.dims[0] - 1
        for p in self.planes(reach):
            for ref, q, v, *kind in body(p):
                near = p + 1 if kind == ["x"] and p < first else p
                self.put(ref, q, v, reach - max(0, first - near, near - last), *kind)

    def back(self, v, dim):
        n = v.shape[dim]
        return pltpu.roll(v, n - 1, dim)

    def coefs(self, c_of):
        first, last = self.halo, self.halo + self.dims[0] - 1
        reach = self.halo - 1
        outer = self.outer * self.scale

        half = {}

        def half_of(p):
            if p not in half:
                half[p] = invert(c_of(p) * (2.0 * self.scale))
            return half[p]

        def face_x(p):
            face = invert(half_of(p) + half_of(p + 1))
            factor = {first - 1: self.xlow, last: self.xhigh}.get(p)
            return face if factor is None else face * factor

        def others(p):
            h = half_of(p)
            ly = invert(h + self.back(h, 0)) * self.ymask
            lz = invert(h + self.back(h, 1)) * self.zmask
            face = face_x(p)
            total = (face + faces.pop()) + (ly + pltpu.roll(ly, 1, 0)) + (lz + pltpu.roll(lz, 1, 1))
            faces.append(face)
            around = outer
            if p in (first, last):
                around = around + (1.0 - (self.xlow if p == first else self.xhigh)) * self.scale
            total = total + c_of(p) * around
            return (self.lx, p, face, "x"), (self.ly, p, ly, "y"), (self.lz, p, lz, "z"), (self.diag, p, total), (self.inv, p, invert(total))

        faces = [face_x(first - reach - 1)]
        self.put(self.lx, first - reach - 1, faces[0], 0)
        self.each(reach, others)

    def op(self, v, p):
        here = v[p]
        ly, lz = self.ly[p], self.lz[p]
        x = self.lx[p] * v[p + 1] + self.lx[p - 1] * v[p - 1]
        y = ly * self.back(here, 0) + pltpu.roll(ly * here, 1, 0)
        z = lz * self.back(here, 1) + pltpu.roll(lz * here, 1, 1)
        return self.diag[p] * here - x - (y + z)

    def own_op(self, v, p):
        own = (slice(0, TILE), slice(0, LANES))
        here = v[p, :, 0:LANES]
        wide = v[p, 0:TILE, :]
        ly, lz = self.ly[p, :, 0:LANES], self.lz[p, 0:TILE, :]
        x = self.lx[p, 0:TILE, 0:LANES] * v[p + 1, 0:TILE, 0:LANES] + self.lx[p - 1, 0:TILE, 0:LANES] * v[p - 1, 0:TILE, 0:LANES]
        y = ly * self.back(here, 0) + pltpu.roll(ly * here, 1, 0)
        z = lz * self.back(wide, 1) + pltpu.roll(lz * wide, 1, 1)
        return self.diag[p, 0:TILE, 0:LANES] * here[own] - x - (y[own] + z[own])

    def before(self, b_of):
        first, mix, gain = factors(0.3, 2.0)

        def one(p):
            return ((self.tmp, p, b_of(p) * self.inv[p] * first),)

        def two(p):
            d = self.tmp[p]
            return ((self.aux, p, d + (mix * d + gain * ((b_of(p) - self.op(self.tmp, p)) * self.inv[p]))),)
        self.each(2, one)
        self.each(1, two)

    def after(self, start, b_of, out, reach):
        first, mix, gain = factors(0.3, 2.0)

        def one(p):
            update = (b_of(p) - self.op(start, p)) * self.inv[p] * first
            return (self.aux, p, update), (self.tmp, p, start[p] + update)

        def two(p):
            update = mix * self.aux[p] + gain * ((b_of(p) - self.op(self.tmp, p)) * self.inv[p])
            return ((out, p, self.tmp[p] + update),)
        self.each(reach + 1, one)
        self.each(reach, two)


def restrict(tiles, lanes, rows):
    out = []
    lane = (2 * iota((TILE, LANES), 1)) % lanes
    row = (2 * iota((TILE, LANES), 0)) % rows
    for a, b in zip(tiles[0::2], tiles[1::2]):
        s = a + b
        s = s + pltpu.roll(s, LANES - 1, 1)
        s = (s + pltpu.roll(s, TILE - 1, 0)) * 0.125
        s = jnp.take_along_axis(s, lane, axis=1)
        out.append(jnp.take_along_axis(s, row, axis=0))
    return out


def kernel(sizes, dims0, b_hbm, c_hbm, p_ref, q_ref, *scratch):
    (e0, x0, zcb, zx0, scb, sx0, c1, b1, x1, z1, s1, c1m, b1m, x1s, slots, tile, pad, x2s) = scratch[:18]
    refs0, refs1, refs2, refs3 = scratch[18:25], scratch[25:32], scratch[32:37], scratch[37:42]
    isem, xsem, gsem = scratch[42:]
    pos = tuple(lax.axis_index(a) for a in AXES)
    dims1 = tuple(d // 2 for d in dims0)
    dims2 = tuple(d // 2 for d in dims1)
    whole2 = tuple(d * n for d, n in zip(dims2, sizes))
    nx, ny, nz = sizes
    count = nx * ny * nz
    me = (pos[0] * ny + pos[1]) * nz + pos[2]
    width2 = x2s.shape[1]
    fold = 2 if 2 * whole2[2] == width2 and whole2[0] % 4 == 0 else 1
    own0 = pl.ds(H0, dims0[0])

    loads = [
        pltpu.make_async_copy(src, e0.at[k, own0, pl.ds(0, TILE), pl.ds(0, LANES)], isem.at[k])
        for k, src in enumerate((c_hbm, b_hbm))
    ]
    for load in loads:
        load.start()

    def coords(index):
        return (index // (ny * nz), (index // nz) % ny, index % nz)

    barrier = pltpu.get_barrier_semaphore()


    def exists(axis, step):
        if step == 0:
            return None
        return pos[axis] < sizes[axis] - 1 if step > 0 else pos[axis] > 0

    def when(conditions, body):
        conditions = [c for c in conditions if c is not None]
        if not conditions:
            body()
            return
        both = conditions[0]
        for c in conditions[1:]:
            both = both & c
        pl.when(both)(body)

    def each(body):
        for dz in (1, -1, 0):
            def group():
                for n, d in enumerate(DIRS):
                    if d[2] == dz:
                        when([exists(0, d[0]), exists(1, d[1])], functools.partial(body, n))
            when([exists(2, dz)], group)

    def greet_near(n):
        pl.semaphore_signal(barrier, inc=1, device_id=tuple(p + d for p, d in zip(pos, DIRS[n])), device_id_type=MESH)

    def greet_all(step, unused):
        pl.semaphore_signal(barrier, inc=1, device_id=coords((me + step) % count), device_id_type=MESH)
        return unused

    if max(sizes) <= 4:
        each(greet_near)
        greeted = 1
        for axis, n in enumerate(sizes):
            greeted = greeted * (1 + jnp.where(pos[axis] > 0, 1, 0) + jnp.where(pos[axis] < n - 1, 1, 0))
        greeted = greeted - 1
    else:
        lax.fori_loop(1, count, greet_all, 0)
        greeted = count - 1

    def cut(step, n, halo, wrap):
        if step == 0:
            return (0, 0, n)
        if step > 0:
            return (n - halo, wrap - halo, halo)
        return (0, n, halo)

    def ends(xid, n):
        dx, dy, dz = DIRS[n]
        if dz:
            packed = {CB: scb, X0: sx0}.get(xid)
            arrived = {CB: zcb, X0: zx0}.get(xid)
            if packed is None:
                at = (C1, B1, X1).index(xid)
                packed, arrived = s1.at[at], z1.at[at]
            return packed, arrived.at[0 if dz > 0 else 1, 1 - dx, 1 - dy]
        low, halo = (xid in (CB, X0)), (H0 if xid in (CB, X0) else H1)
        dims = dims0 if low else dims1
        a, b, planes = cut(dx, dims[0], halo, 0)
        r, s, rows = cut(dy, dims[1], min(halo, dims[1]), 2 * TILE)
        if low:
            ref = e0 if xid == CB else x0
            lead = (slice(None),) if xid == CB else ()
            lanes = (pl.ds(0, LANES),)
        else:
            ref, lead, lanes = {C1: c1, B1: b1, X1: x1}[xid], (), (slice(None),)
        src = ref.at[lead + (pl.ds(halo + a, planes), pl.ds(r, rows)) + lanes]
        dst = ref.at[lead + (pl.ds(halo + b, planes), pl.ds(s, rows)) + lanes]
        return src, dst

    def remote(xid, n):
        src, dst = ends(xid, n)
        return pltpu.make_async_remote_copy(
            src_ref=src, dst_ref=dst, send_sem=xsem.at[xid], recv_sem=xsem.at[xid],
            device_id=tuple(p + d for p, d in zip(pos, DIRS[n])), device_id_type=MESH,
        )

    def launch(xid):
        each(lambda n: remote(xid, n).start())

    def fill(xid):
        def one(n):
            dst = ends(xid, n)[1]
            if xid == CB:
                dst[0] = jnp.ones(dst.shape[1:], F32)
                dst[1] = jnp.zeros(dst.shape[1:], F32)
            else:
                dst[...] = jnp.full(dst.shape, 1.0 if xid == C1 else 0.0, F32)
        for n, d in enumerate(DIRS):
            sources = [exists(axis, -step) for axis, step in enumerate(d) if step]
            present = functools.reduce(jnp.logical_and, sources)
            pl.when(jnp.logical_not(present))(functools.partial(one, n))

    def settle(xid):
        kinds = []
        for axis, n in enumerate(sizes):
            inside = (pos[axis] > 0) & (pos[axis] < n - 1)
            kinds.append([(0, None)] if n == 1 else [(1, None)] if n == 2 else [(1, jnp.logical_not(inside)), (2, inside)])
        for case in itertools.product(*kinds):
            rows = 0
            for n, d in enumerate(DIRS):
                if min(d) >= 0:
                    shape = ends(xid, n)[0].shape
                    rows += math.prod(shape[:-1]) * math.prod(k for (k, unused), step in zip(case, d) if step)
            part = pad.at[pl.ds(0, 2 * rows)]
            when([c for unused, c in case], pltpu.make_async_copy(part, part, xsem.at[xid]).wait)

    lane, sub = iota((TILE, LANES), 1), iota((TILE, LANES), 0)

    def pack0(tiles):
        out = tiles[0]
        for t in range(1, len(tiles)):
            part = pltpu.roll(tiles[t], 8 * t, 1)
            out = jnp.where(((lane - (8 * t - 4)) % LANES) < 8, part, out)
        return out

    def pack1(tiles):
        out = tiles[0]
        for t in range(1, len(tiles)):
            part = pltpu.roll(tiles[t], 8 * t, 1)
            place = (lane - 8 * t) % LANES
            out = jnp.where((place < 4) | ((place >= 60) & (place < 64)), part, out)
        return out

    def both_sides(arrived, dx, dy, k=None):
        at = (dx + 1, dy + 1) + (() if k is None else (k,))
        return jnp.where(lane % 8 < 4, arrived[(1,) + at], arrived[(0,) + at])

    def group_planes(n, halo):
        return ((0, [(t, halo + t) for t in range(n)]),
                (-1, [(t, halo + t - n) for t in range(n - halo, n)]),
                (1, [(t, halo + n + t) for t in range(halo)]))

    def unpack0(arrived, k, store):
        for dx, pairs in group_planes(dims0[0], H0):
            first = both_sides(arrived, dx, 0, k)
            second = jnp.where(sub < 4, both_sides(arrived, dx, 1, k), both_sides(arrived, dx, -1, k))
            for t, p in pairs:
                shift = (-8 * t) % LANES
                beyond = max(0, H0 - p, p - (H0 + dims0[0] - 1))
                if beyond < H0:
                    store(p, 0, pltpu.roll(first, shift, 1) if shift else first)
                if beyond < H0 - 1:
                    store(p, 1, pltpu.roll(second, shift, 1) if shift else second)

    def unpack1(arrived, field, store):
        z = dims1[2]
        for dx, pairs in group_planes(dims1[0], H1):
            first = jnp.where(sub < 4, both_sides(arrived, dx, 0), both_sides(arrived, dx, 1))
            second = both_sides(arrived, dx, -1)
            for t, p in pairs:
                shift = (z - 8 * t) % LANES
                for half, part in enumerate((first, second)):
                    rows = slice(half * TILE, (half + 1) * TILE)
                    part = pltpu.roll(part, shift, 1) if shift else part
                    store(p, rows, jnp.where(lane < z, field[p, rows, :], part))

    def post1(field, packed, tiles):
        for i, v in enumerate(tiles):
            field[H1 + i, 0:dims1[1], :] = v[0:dims1[1]]
        packed[...] = pack1(tiles)

    def message(tiles):
        out = tiles[0]
        for i in range(1, dims2[0]):
            out = jnp.where(lane // dims2[2] == i, tiles[i], out)
        return out

    def gather_start():
        src = tile.at[:, pl.ds(0, dims2[1])]
        dst = slots.at[:, pos[0], pos[2], pl.ds(dims2[1] * pos[1], dims2[1])]

        def go(step, unused):
            pltpu.make_async_remote_copy(
                src_ref=src, dst_ref=dst, send_sem=gsem, recv_sem=gsem,
                device_id=coords((me + step) % count), device_id_type=MESH,
            ).start()
            return unused
        lax.fori_loop(1, count, go, 0)
        pltpu.make_async_copy(src, dst, gsem).start()

    def gather_wait():
        part = pad.at[pl.ds(0, 2 * dims2[1] * (2 * count - 1))]
        pltpu.make_async_copy(part, part, gsem).wait()

    def gathered(kind, outside):
        z = dims2[2]
        per = LANES // z
        spot = iota((whole2[1], LANES), 1)
        planes = []
        for n in range(whole2[0] // fold):
            columns = []
            for first in range(0, width2 // z, per):
                total = None
                for g in range(min(per, fold * nz - first)):
                    plane = n + (first + g) // nz * (whole2[0] // fold)
                    x, i = divmod(plane, dims2[0])
                    shift = (z * (g - i)) % LANES
                    part = slots[kind, x, (first + g) % nz]
                    part = pltpu.roll(part, shift, 1) if shift else part
                    total = part if total is None else jnp.where(spot // z == g, part, total)
                columns.append(total)
            planes.append(columns[0] if len(columns) == 1 else jnp.concatenate(columns, 1))
        v = jnp.concatenate(planes, 0)
        if fold * whole2[2] < width2:
            v = jnp.where(iota(v.shape, 1) < fold * whole2[2], v, outside)
        return v

    for load in loads:
        load.wait()
    for k in range(2):
        scb[k] = pack0([e0[k, H0 + t, 0:TILE, 0:LANES] for t in range(dims0[0])])
    pl.semaphore_wait(barrier, greeted)

    launch(CB)
    for k, value in ((0, 1.0), (1, 0.0)):
        rows = slice(TILE + H0, 2 * TILE - H0)
        e0[k, :, rows, 0:LANES] = jnp.full((e0.shape[1], rows.stop - rows.start, LANES), value, F32)
    fill(CB)
    tiles = restrict([e0[0, H0 + t, 0:TILE, 0:LANES] for t in range(dims0[0])], dims0[2], dims0[1])
    post1(c1, s1.at[0], tiles)
    launch(C1)
    tile[0] = message(restrict(tiles, dims1[2], dims1[1]))
    for ref, value in ((c1, 1.0), (b1, 0.0), (x1, 0.0)):
        ref[:, 2 * dims1[1]:3 * dims1[1], :] = jnp.full((ref.shape[0], dims1[1], LANES), value, F32)
    rows = slice(TILE + H0, 2 * TILE - H0)
    x0[:, rows, 0:LANES] = jnp.zeros((x0.shape[0], rows.stop - rows.start, LANES), F32)
    for xid in (C1, B1, X0, X1):
        fill(xid)

    level0 = Level(refs0, dims0, H0, 2 * LANES, pos, sizes, 1.0)
    level1 = Level(refs1, dims1, H1, LANES, pos, sizes, 0.25)

    settle(CB)
    for k in range(2):
        def put(p, half, value):
            e0[k, p, half * TILE:(half + 1) * TILE, LANES:2 * LANES] = value
        unpack0(zcb, k, put)
    level0.coefs(lambda p: e0[0, p])
    b0 = lambda p: e0[1, p]
    level0.before(b0)
    r0 = [e0[1, p, 0:TILE, 0:LANES] - level0.own_op(level0.aux, p) for p in level0.planes(0)]
    tiles = restrict(r0, dims0[2], dims0[1])
    post1(b1, s1.at[1], tiles)
    launch(B1)

    tiles = [level0.aux[p, 0:TILE, 0:LANES] for p in level0.planes(0)]
    for p, v in zip(level0.planes(0), tiles):
        x0[p, 0:TILE, 0:LANES] = v
    sx0[...] = pack0(tiles)
    settle(C1)

    def put_c1(p, rows, value):
        c1m[p, rows, :] = value
    unpack1(z1.at[0], c1, put_c1)
    level1.coefs(lambda p: c1m[p])

    launch(X0)
    settle(B1)

    def put_b1(p, rows, value):
        b1m[p, rows, :] = value
    unpack1(z1.at[1], b1, put_b1)
    b1_of = lambda p: b1m[p]
    level1.before(b1_of)
    r1 = [b1m[p, 0:TILE, :] - level1.own_op(level1.aux, p) for p in level1.planes(0)]
    tile[1] = message(restrict(r1, dims1[2], dims1[1]))
    gather_start()
    tiles = [level1.aux[p, 0:TILE, :] for p in level1.planes(0)]
    tiles = [jnp.where(lane < dims1[2], v, pltpu.roll(v, dims1[2], 1)) for v in tiles]
    tiles = [jnp.where(sub < dims1[1], v, pltpu.roll(v, dims1[1], 0)) for v in tiles]
    post1(x1, s1.at[2], tiles)
    launch(X1)

    y2, z2 = whole2[1], whole2[2]
    shape3 = (whole2[0] * y2 // (2 * fold), width2)

    def pairs(v):
        return [v[n * y2:(n + 1) * y2] for n in range(v.shape[0] // y2)]

    def restrict2(v):
        planes = pairs(v)
        s = jnp.concatenate([a + b for a, b in zip(planes[0::2], planes[1::2])], 0)
        s = s + pltpu.roll(s, width2 - 1, 1)
        return (s + pltpu.roll(s, s.shape[0] - 1, 0)) * 0.125

    def prolong3(v):
        v = jnp.where((iota(shape3, 0) % 2 == 0) & (iota(shape3, 1) % 2 == 0), v, 0.0)
        v = v + pltpu.roll(v, 1, 1)
        v = v + pltpu.roll(v, 1, 0)
        return jnp.concatenate([part for part in pairs(v) for unused in range(2)], 0)

    gather_wait()
    c2 = gathered(0, 1.0)
    level2 = Flat(refs2, y2, z2, 1, 0.25 ** 2, fold)
    level2.coefs(c2)
    level3 = Flat(refs3, y2, z2, 2, 0.25 ** 3, fold)
    level3.coefs(restrict2(c2))
    b2 = gathered(1, 0.0)
    x2 = chebyshev(None, b2, 2, 0.3, 2.0, level2)
    b3 = restrict2(b2 - level2.op(x2))
    x3 = chebyshev(None, b3, COARSE_DEGREE, 0.05, 2.0, level3)
    x2 = chebyshev(x2 + prolong3(x3), b2, 2, 0.3, 2.0, level2)
    for k in range(fold):
        x2s[pl.ds(k * x2.shape[0], x2.shape[0]), :] = pltpu.roll(x2, z2, 1) if k else x2

    settle(X1)

    def put_x1(p, rows, value):
        x1s[p, rows, :] = value
    unpack1(z1.at[2], x1, put_x1)

    quarter = LANES // 4
    first_lane, first_row = pos[2] * dims2[2], pos[1] * dims2[1]
    lanes = (first_lane + width2 + jnp.where(lane < 3 * quarter, lane // 2, lane // 2 - 2 * quarter)) % width2
    rows = [sub // 2 + 4 * half for half in range(2)]
    rows = [(first_row + y2 + jnp.where(r < 6, r, r - TILE)) % y2 for r in rows]
    low = ((first_row + y2 - 2) % y2) // TILE, ((first_lane + width2 - quarter // 2) % width2) // LANES
    high = ((first_row + 5) % y2) // TILE, ((first_lane + quarter + quarter // 2 - 1) % width2) // LANES
    window = range(-H1 // 2, (dims1[0] + H1) // 2)
    spread = []
    for i in window:
        plane = jnp.clip(pos[0] * dims2[0] + i, 0, whole2[0] - 1)

        def wide(row_tile):
            at = pl.ds(pl.multiple_of(plane * y2 + row_tile * TILE, TILE), TILE)
            if width2 == LANES:
                return jnp.take_along_axis(x2s[at, :], lanes, axis=1)
            parts = [x2s[at, pl.ds(pl.multiple_of(t * LANES, LANES), LANES)] for t in (low[1], high[1])]
            parts = [jnp.take_along_axis(v, lanes % LANES, axis=1) for v in parts]
            return jnp.where(lanes // LANES == low[1], *parts)
        if y2 == TILE:
            v = wide(0)
            spread.append([jnp.take_along_axis(v, r, axis=0) for r in rows])
        else:
            v, w = wide(low[0]), wide(high[0])
            spread.append([
                jnp.where(r // TILE == low[0], *(jnp.take_along_axis(u, r % TILE, axis=0) for u in (v, w))) for r in rows])
    for i, halves in zip(window, spread):
        for half, part in enumerate(halves):
            rows = slice(half * TILE, (half + 1) * TILE)
            for p in (2 * i + H1, 2 * i + H1 + 1):
                x1s[p, rows, :] = x1s[p, rows, :] + part
    level1.after(x1s, b1_of, b1, 2)

    settle(X0)

    def put_x0(p, half, value):
        x0[p, half * TILE:(half + 1) * TILE, LANES:2 * LANES] = value
    unpack0(zx0, None, put_x0)

    window = range(-2, dims1[0] + 2)
    for group in range(0, len(window), 4):
        results = []
        for i in window[group:group + 4]:
            first, second = b1[H1 + i, 0:TILE, :], b1[H1 + i, TILE:2 * TILE, :]
            second = jnp.where(sub < 6, first, second)
            for half, part in enumerate((first, second)):
                part = jnp.take_along_axis(part, 4 * half + sub // 2, axis=0)
                for side in range(2):
                    e = jnp.take_along_axis(part, (LANES // 2) * side + lane // 2, axis=1)
                    at = (slice(half * TILE, (half + 1) * TILE), slice(side * LANES, (side + 1) * LANES))
                    for p in (2 * i + H0, 2 * i + H0 + 1):
                        if max(0, H0 - p, p - (H0 + dims0[0] - 1)) + half + side <= H0:
                            results.append(((p,) + at, x0[(p,) + at] + e))
        for at, v in results:
            x0[at] = v
    level0.after(x0, b0, x0, 1)
    for t, p in enumerate(level0.planes(0)):
        p_ref[t] = x0[p, 0:TILE, 0:LANES]
        q_ref[t] = e0[1, p, 0:TILE, 0:LANES] - level0.own_op(x0, p)


def finish(p_ref, q_ref, p_out, q_out):
    p_out[...] = p_ref[...]
    q_out[...] = q_ref[...]


def solution(mesh):
    sizes = tuple(mesh.shape[a] for a in AXES)
    count = sizes[0] * sizes[1] * sizes[2]

    def per_device(b, c):
        dims0 = b.shape
        dims1 = tuple(d // 2 for d in dims0)
        dims2 = tuple(d // 2 for d in dims1)
        assert dims0[1:] == (TILE, LANES) and dims2[0] * dims2[2] == LANES and 8 * dims0[0] == LANES
        whole2 = tuple(d * n for d, n in zip(dims2, sizes))
        assert whole2[1] % TILE == 0
        width2 = -(-whole2[2] // LANES) * LANES
        planes0, planes1 = dims0[0] + 2 * H0, dims1[0] + 2 * H1
        wide = pltpu.VMEM((planes0, 2 * TILE, 2 * LANES), F32)
        slim = pltpu.VMEM((planes1, 2 * TILE, LANES), F32)
        fold = 2 if 2 * whole2[2] == width2 and whole2[0] % 4 == 0 else 1
        flat2 = pltpu.VMEM((whole2[0] // fold * whole2[1], width2), F32)
        flat3 = pltpu.VMEM((whole2[0] // (2 * fold) * whole2[1], width2), F32)
        spot = (TILE, LANES)
        scratch = [
            pltpu.VMEM((2, planes0, 2 * TILE, 2 * LANES), F32), wide,
            pltpu.VMEM((2, 3, 3, 2) + spot, F32), pltpu.VMEM((2, 3, 3) + spot, F32),
            pltpu.VMEM((2,) + spot, F32), pltpu.VMEM(spot, F32),
            slim, slim, slim, pltpu.VMEM((3, 2, 3, 3) + spot, F32), pltpu.VMEM((3,) + spot, F32),
            slim, slim, slim,
            pltpu.VMEM((2, sizes[0], sizes[2], whole2[1], LANES), F32), pltpu.VMEM((2,) + spot, F32),
            pltpu.VMEM((max(4 * dims2[1] * count, 32 * dims0[0] * TILE), LANES), F32), pltpu.VMEM((whole2[0] * whole2[1], width2), F32),
        ] + [wide] * 7 + [slim] * 7 + [flat2] * 5 + [flat3] * 5 + [
            pltpu.SemaphoreType.DMA((2,)), pltpu.SemaphoreType.DMA((5,)), pltpu.SemaphoreType.DMA,
        ]
        shape = jax.ShapeDtypeStruct(dims0, F32)
        p, q = pl.pallas_call(
            functools.partial(kernel, sizes, dims0),
            out_shape=(shape, shape),
            in_specs=[pl.BlockSpec(memory_space=pltpu.HBM)] * 2,
            out_specs=(pl.BlockSpec(memory_space=pltpu.VMEM),) * 2,
            scratch_shapes=scratch,
            compiler_params=pltpu.CompilerParams(
                collective_id=0, has_side_effects=True, vmem_limit_bytes=KERNEL_VMEM),
        )(b, c)
        return pl.pallas_call(
            finish,
            out_shape=(shape, shape),
            in_specs=[pl.BlockSpec(memory_space=pltpu.VMEM)] * 2,
            out_specs=(pl.BlockSpec(memory_space=pltpu.VMEM),) * 2,
            compiler_params=pltpu.CompilerParams(vmem_limit_bytes=2 << 20),
        )(p, q)

    spec = P(*AXES)
    return jax.shard_map(per_device, mesh=mesh, in_specs=(spec, spec), out_specs=(spec, spec), check_vma=False)
```
